256 devices in a mesh: gx: 32 (over x, y, core), gy: 8 (over z).
Axes of the slice: x: 4, y: 4, z: 8, core: 2. Of those that a mesh axis runs over, the one named last changes fastest.
Arguments:
- probes: float32 [16, 2, 2, 1024, 1024], P(None, None, None, 'gx', 'gy'), may hold values from -12 to 12
- coefficients: float32 [15, 2, 1024, 1024], P(None, None, 'gx', 'gy'), may hold values from 0.03 to 0.9, as said below
Outputs:
- sketch: float32 [16, 2, 2, 1024, 1024], P(None, None, None, 'gx', 'gy')
- factor: float32 [16, 16], replicated
The draws below stay inside these ranges and needn't reach their ends.
Inputs may be any that keep to these rules, and one draw needn't show every extreme that they name: `coefficients`: every coefficient is positive.
All inputs are finite; a program needn't handle non-finite values.
Results may differ from the reference program's by a relative error of at most 0.00016.
Values sent between devices are 32-bit elements; how exact they have to be, the bound alone decides.
No kernel may reach another device: no remote copies, remote signals or barrier semaphores. Data moves between devices by JAX's collectives and lax.ppermute only.
A program may use at most 64 MiB of HBM per device.

```python
import jax
import jax.numpy as jnp
from jax import lax

P_SIZE = 16
NZ = 2
NX = 1024
NY = 1024
ROWS = 4194304


def draw_probes(key, part):
    key_noise = jax.random.fold_in(key, 0)
    full_shape = (P_SIZE, 2, NZ, NX, NY)
    x_ramp = jnp.arange(NX, dtype=jnp.float32) / max(NX - 1, 1)
    y_ramp = jnp.arange(NY, dtype=jnp.float32) / max(NY - 1, 1)
    amplitude = jnp.power(3.0, x_ramp)[:, None] * jnp.power(3.0, y_ramp)[None, :]
    noise_part = jnp.clip(jax.random.normal(key_noise, full_shape, jnp.float32), -4.0, 4.0)
    return noise_part * amplitude / 3.0


def draw_coefficients(key, part):
    lower_end = jnp.array([0.3, 0.3] + [0.03] * 12 + [0.2], jnp.float32)[:, None, None, None]
    upper_end = jnp.array([0.9, 0.9] + [0.15] * 12 + [0.6], jnp.float32)[:, None, None, None]
    uniform_part = jax.random.uniform(key, (15, NZ, NX, NY), jnp.float32)
    return lower_end * jnp.exp(uniform_part * jnp.log(upper_end / lower_end))


def setup_inputs(seed: int = 0) -> dict:
    arg_keys = jax.random.split(jax.random.key(seed), 3)
    probes = draw_probes(jax.random.fold_in(arg_keys[2], 71), 0)
    coefficients = draw_coefficients(jax.random.fold_in(arg_keys[2], 71), 0)
    return dict(probes=probes, coefficients=coefficients)


HORIZONTAL = ((1, 0), (-1, 0), (0, 1), (0, -1))

def window(array, margin, target, step_x, step_y):
    trim = margin - target
    width_x = array.shape[-2] - 2 * trim
    width_y = array.shape[-1] - 2 * trim
    start_x = trim + step_x
    start_y = trim + step_y
    return array[..., start_x:start_x + width_x, start_y:start_y + width_y]

def shift_up(array):
    return jnp.concatenate([array[..., 1:, :, :], jnp.zeros_like(array[..., :1, :, :])], axis=-3)

def shift_down(array):
    return jnp.concatenate([jnp.zeros_like(array[..., :1, :, :]), array[..., :-1, :, :]], axis=-3)

def forward(probe_field, coeffs, margin, coef_margin):
    target = margin - 1
    centre = window(probe_field, margin, target, 0, 0)
    result = window(coeffs[0:2], coef_margin, target, 0, 0) * centre
    for index in range(4):
        step_x, step_y = HORIZONTAL[index]
        result = result + window(coeffs[2 + index:14:6], coef_margin, target, 0, 0) * window(probe_field, margin, target, step_x, step_y)
    result = result + window(coeffs[6:14:6], coef_margin, target, 0, 0) * shift_up(centre)
    result = result + window(coeffs[7:14:6], coef_margin, target, 0, 0) * shift_down(centre)
    coupled = window(coeffs[14], coef_margin, target, 0, 0) * centre[..., 0, :, :, :]
    return jnp.stack([result[..., 0, :, :, :], result[..., 1, :, :, :] + coupled], axis=-4)

def adjoint(probe_field, coeffs, margin, coef_margin):
    target = margin - 1
    centre = window(probe_field, margin, target, 0, 0)
    result = window(coeffs[0:2], coef_margin, target, 0, 0) * centre
    for index in range(4):
        step_x, step_y = HORIZONTAL[index]
        weighted = window(coeffs[2 + index:14:6], coef_margin, margin, 0, 0) * probe_field
        result = result + window(weighted, margin, target, -step_x, -step_y)
    result = result + shift_down(window(coeffs[6:14:6], coef_margin, target, 0, 0) * centre)
    result = result + shift_up(window(coeffs[7:14:6], coef_margin, target, 0, 0) * centre)
    coupled = window(coeffs[14], coef_margin, target, 0, 0) * centre[..., 1, :, :, :]
    return jnp.stack([result[..., 0, :, :, :] + coupled, result[..., 1, :, :, :]], axis=-4)

def pad_plane(array):
    return jnp.pad(array, [(0, 0)] * (array.ndim - 2) + [(1, 1), (1, 1)])

def reference(probes, coefficients):
    coef_pad = pad_plane(coefficients)

    def hessian(probe):
        state_now = forward(pad_plane(probe), coef_pad, 1, 1)
        state_now = forward(pad_plane(state_now), coef_pad, 1, 1)
        state_now = adjoint(pad_plane(state_now), coef_pad, 1, 1)
        return adjoint(pad_plane(state_now), coef_pad, 1, 1)
    sketch = lax.map(hessian, probes)
    flat = sketch.reshape(P_SIZE, -1)
    gram = jnp.dot(flat, flat.T, precision=lax.Precision.HIGHEST) / ROWS
    factor = jnp.linalg.cholesky(gram).T
    return (sketch, factor)
```

```python
import jax
import jax.numpy as jnp
from jax import lax
from jax.experimental import pallas as pl
from jax.experimental.pallas import tpu as pltpu
from jax.sharding import Mesh, PartitionSpec as P

PLANES = 64
COEFS = 30
PAIRS = (PLANES + COEFS) // 2
ROWS = 32
EXT = 48
STARTS = ((5, 13, 21, 29, 35), (6, 14, 22, 30, 34), (7, 15, 23, 31, 33), (8, 16, 24, 32))
F32 = jnp.float32


def iota(shape, dim):
    return lax.broadcasted_iota(jnp.int32, shape, dim)


def lane_roll(array, shift):
    shift = shift % 128
    return array if shift == 0 else pltpu.roll(array, shift, array.ndim - 1)


def half_roll(array):
    return pltpu.roll(array, 4, array.ndim - 2)


def pack_rows_kernel(p_top, p_bottom, c_top, c_bottom, low_ref, high_ref):
    for first, last, offset, half in (
        (p_top, p_bottom, 0, PLANES // 2),
        (c_top, c_bottom, PLANES // 2, COEFS // 2),
    ):
        upper = iota((half, 8, 128), 1) < 4
        low_ref[offset : offset + half] = jnp.where(upper, first[:half], half_roll(first[half:]))
        high_ref[offset : offset + half] = jnp.where(upper, half_roll(last[:half]), last[half:])


def halo_tiles(low_ref, high_ref, index):
    low, high = low_ref[index], high_ref[index]
    upper = iota((8, 128), 0) < 4
    return jnp.where(upper, low, half_roll(high)), jnp.where(upper, half_roll(low), high)


def pack_lanes_kernel(p_ref, c_ref, low_ref, high_ref, left_ref, right_ref):
    lane = iota((8, 128), 1)
    halos = [None] * PLANES
    for k in range(PLANES // 2):
        halos[k], halos[k + PLANES // 2] = halo_tiles(low_ref, high_ref, k)
    first = lane % 8 < 4
    for z in range(2):
        for tile in range(5):
            both = []
            for c in range(2):
                packed = None
                for p in range(16):
                    plane = p * 4 + c * 2 + z
                    value = halos[plane] if tile == 4 else p_ref[plane, tile * 8 : tile * 8 + 8]
                    value = lane_roll(value, 8 * p + 4)
                    packed = value if packed is None else jnp.where(lane // 8 == p, value, packed)
                both.append(packed)
            right_ref[z * 5 + tile] = jnp.where(first, both[0], lane_roll(both[1], 4))
            left_ref[z * 5 + tile] = jnp.where(first, lane_roll(both[0], -4), both[1])
    chalos = [None] * COEFS
    for k in range(COEFS // 2):
        chalos[k], chalos[k + COEFS // 2] = halo_tiles(low_ref, high_ref, PLANES // 2 + k)
    for tile in range(5):
        right = left = None
        for n in range(COEFS):
            value = chalos[n] if tile == 4 else c_ref[n, tile * 8 : tile * 8 + 8]
            to_right, to_left = lane_roll(value, 4 * n + 4), lane_roll(value, 4 * n)
            if right is None:
                right, left = to_right, to_left
            else:
                right = jnp.where(lane // 4 == n, to_right, right)
                left = jnp.where(lane // 4 == n, to_left, left)
        right_ref[10 + tile] = right
        left_ref[10 + tile] = left


def step(source, target, coef, groups, starts, adjoint, shift=0, unroll=4):
    for s in starts:

        def weight(slot, z, move=0):
            return coef[slot * 2 + z, s + move : s + move + 8, :]

        up, down = (-1, 1) if adjoint else (0, 0)
        weights = {}
        for z in range(2):
            weights[14, z] = weight(14, z)
            for c in range(2):
                weights[c, z] = weight(c, z)
                slot = 2 + 6 * c
                weights[slot, z] = weight(slot, z, up)
                weights[slot + 1, z] = weight(slot + 1, z, down)
                weights[slot + 2, z] = weight(slot + 2, z)
                weights[slot + 3, z] = weight(slot + 3, z)
                vertical = slot + (4 if z == 0 else 5)
                weights[vertical, z] = weight(vertical, z)

        def body(group, carry):
            base = group * 4

            def field(c, z, move=0):
                return source[base + (c * 2 + z), s + move : s + move + 8, :]

            centre = {(c, z): field(c, z) for c in range(2) for z in range(2)}
            for c in range(2):
                for z in range(2):
                    value = centre[c, z]
                    slot = 2 + 6 * c
                    total = weights[c, z] * value
                    before, after = field(c, z, -1), field(c, z, 1)
                    if adjoint:
                        total = total + weights[slot, z] * before + weights[slot + 1, z] * after
                        total = total + lane_roll(weights[slot + 2, z] * value, 1)
                        total = total + lane_roll(weights[slot + 3, z] * value, -1)
                        vertical = slot + (5 if z == 0 else 4)
                        total = total + weights[vertical, 1 - z] * centre[c, 1 - z]
                        if c == 0:
                            total = total + weights[14, z] * centre[1, z]
                    else:
                        total = total + weights[slot, z] * after + weights[slot + 1, z] * before
                        total = total + weights[slot + 2, z] * lane_roll(value, -1)
                        total = total + weights[slot + 3, z] * lane_roll(value, 1)
                        vertical = slot + (4 if z == 0 else 5)
                        total = total + weights[vertical, z] * centre[c, 1 - z]
                        if c == 1:
                            total = total + weights[14, z] * centre[0, z]
                    target[base + (c * 2 + z), s + shift : s + shift + 8, :] = total
            return carry

        lax.fori_loop(0, groups, body, 0, unroll=unroll)


def four_steps(first, second, coef, result, groups, shift):
    step(first, second, coef, groups, STARTS[0], False)
    step(second, first, coef, groups, STARTS[1], False)
    step(first, second, coef, groups, STARTS[2], True)
    step(second, result, coef, groups, STARTS[3], True, shift)


def fill(extended, own, low, high, half, offset):
    extended[:, 8:40, :] = own[...]
    for side, row in ((low, 4), (high, 40)):
        extended[:half, row : row + 4, :] = side[offset : offset + half, 0:4, :]
        extended[half:, row : row + 4, :] = side[offset : offset + half, 4:8, :]


def body_kernel(p_ref, c_ref, low_ref, high_ref, main_ref, strip_ref, cstrip_ref, first, second, coef):
    fill(first, p_ref, low_ref, high_ref, PLANES // 2, 0)
    fill(coef, c_ref, low_ref, high_ref, COEFS // 2, PLANES // 2)
    lane = iota((8, 128), 1)
    offset = lane % 32
    for row in range(0, 40, 8):

        def strip(index, carry):
            total = jnp.zeros((8, 128), F32)
            for q in range(4):
                value = first[q * 16 + index, row + 4 : row + 12, :]
                here = lane // 32 == q
                total = jnp.where(here & (offset < 8), lane_roll(value, q * 32 + 8), total)
                total = jnp.where(here & (offset >= 20), lane_roll(value, q * 32 + 20), total)
            strip_ref[index, row : row + 8, :] = total
            return carry

        lax.fori_loop(0, 16, strip, 0, unroll=2)

        def cstrip(index, carry):
            value = coef[index, row + 4 : row + 12, :]
            total = jnp.where(lane < 8, lane_roll(value, 8), jnp.zeros_like(value))
            total = jnp.where((lane >= 20) & (lane < 28), lane_roll(value, 20), total)
            total = total + lane_roll(total, 32)
            cstrip_ref[index, row : row + 8, :] = total + lane_roll(total, 64)
            return carry

        lax.fori_loop(0, COEFS, cstrip, 0, unroll=2)
    four_steps(first, second, coef, main_ref, 16, -8)


def edge_kernel(main_ref, strip_ref, cstrip_ref, left_ref, right_ref, out_ref, gram_ref, first, second, coef, result):
    lane = iota((8, 128), 1)
    offset = lane % 32
    is_right = (offset >= 8) & (offset < 12)
    is_left = (offset >= 16) & (offset < 20)
    first[:, 4:44, :] = strip_ref[...]
    coef[:, 4:44, :] = cstrip_ref[...]

    def put(target, index, tile, merged_left, merged_right):
        if tile < 4:
            rows = slice(8 + tile * 8, 16 + tile * 8)
            value = target[index, rows, :]
            target[index, rows, :] = jnp.where(is_left, merged_left, jnp.where(is_right, merged_right, value))
        else:
            for part, row in ((0, 4), (4, 40)):
                value = target[index, row : row + 4, :]
                target[index, row : row + 4, :] = jnp.where(
                    is_left[:4],
                    merged_left[part : part + 4],
                    jnp.where(is_right[:4], merged_right[part : part + 4], value),
                )

    for z in range(2):
        for tile in range(5):
            left, right = left_ref[z * 5 + tile], right_ref[z * 5 + tile]
            for t in range(4):
                for c in range(2):
                    at = 8 * t + 4 * c
                    put(first, t * 4 + c * 2 + z, tile, lane_roll(left, 16 - at), lane_roll(right, 8 - at))
    for tile in range(5):
        left, right = left_ref[10 + tile], right_ref[10 + tile]
        for n in range(COEFS):
            total = jnp.where(
                (lane >= 16) & (lane < 20),
                lane_roll(left, 16 - 4 * n),
                jnp.where((lane >= 8) & (lane < 12), lane_roll(right, 8 - 4 * n), 0.0),
            )
            total = total + lane_roll(total, 32)
            total = total + lane_roll(total, 64)
            put(coef, n, tile, total, total)
    four_steps(first, second, coef, result, 4, -8)
    for row in range(0, ROWS, 8):

        def merge(index, carry):
            edge = result[index, row : row + 8, :]
            for q in range(4):
                value = main_ref[q * 16 + index, row : row + 8, :]
                value = jnp.where(lane >= 124, lane_roll(edge, 124 - (q * 32 + 4)), value)
                value = jnp.where(lane < 4, lane_roll(edge, -(q * 32 + 20)), value)
                out_ref[q * 16 + index, row : row + 8, :] = value
            return carry

        lax.fori_loop(0, 16, merge, 0, unroll=2)

    gram = jnp.zeros((128, 128), F32)
    view = out_ref.reshape(16, 4, ROWS, 128)
    for part in range(4):
        for row in range(0, ROWS, 8):
            block = view[:, part, row : row + 8, :].reshape(128, 128)
            gram = gram + lax.dot_general(
                block, block, (((1,), (1,)), ((), ())), precision=lax.Precision.HIGHEST, preferred_element_type=F32
            )
    same = iota((128, 128), 0) % 8 == iota((128, 128), 1) % 8
    folded = jnp.where(same, gram, 0.0).reshape(16, 8, 128).sum(axis=1)
    source, target = iota((128, 128), 0) // 8, iota((128, 128), 1)
    tile = jnp.zeros((8, 128), F32)
    for half in range(2):
        select = (target == source + 16 * half).astype(F32)
        tile = tile + jnp.dot(
            folded[8 * half : 8 * half + 8], select, precision=lax.Precision.HIGHEST, preferred_element_type=F32
        )
    gram_ref[...] = jnp.broadcast_to(tile[None], gram_ref.shape)


def sum_kernel(in_ref, out_ref):
    out_ref[...] = jnp.broadcast_to(jnp.sum(in_ref[...], axis=0)[None], out_ref.shape)


def cholesky_kernel(scale, in_ref, out_ref):
    tile = jnp.sum(in_ref[...], axis=0) * scale
    row, col = iota((16, 128), 0), iota((16, 128), 1)
    work = jnp.concatenate([tile, lane_roll(tile, -16)], axis=0)
    work = jnp.where(col < 16, work, 0.0)
    for k in range(15):
        pivot = work[k : k + 1, k : k + 1]
        update = work[:, k : k + 1] * (work[k : k + 1, :] / pivot)
        work = jnp.where(row > k, work - update, work)
    diagonal = jnp.sum(jnp.where(row == col, work, 0.0), axis=1, keepdims=True)
    factor = jnp.where(col >= row, work / jnp.sqrt(diagonal), 0.0)
    out_ref[...] = factor[:, :16]


def shape(*dims):
    return jax.ShapeDtypeStruct(dims, F32)


VMEM = pl.BlockSpec(memory_space=pltpu.VMEM)
PARAMS = pltpu.CompilerParams(vmem_limit_bytes=32 << 20)


def neighbours(array, axes, pairs):
    return lax.ppermute(array, axes, pairs)


def local(probes, coefficients):
    planes = probes.reshape(PLANES, ROWS, 128)
    weights = coefficients.reshape(COEFS, ROWS, 128)
    spec_first = lambda n: pl.BlockSpec((n, 8, 128), lambda i: (0, 0, 0))
    spec_last = lambda n: pl.BlockSpec((n, 8, 128), lambda i: (0, ROWS // 8 - 1, 0))
    whole = pl.BlockSpec((PAIRS, 8, 128), lambda i: (0, 0, 0))
    low, high = pl.pallas_call(
        pack_rows_kernel,
        grid=(1,),
        in_specs=[spec_first(PLANES), spec_last(PLANES), spec_first(COEFS), spec_last(COEFS)],
        out_specs=[whole, whole],
        out_shape=[shape(PAIRS, 8, 128)] * 2,
        name="pack_rows",
    )(planes, planes, weights, weights)
    along_x = ("x", "y", "core")
    count = lax.axis_size(along_x)
    forward = [(i, i + 1) for i in range(count - 1)]
    backward = [(j, i) for i, j in forward]
    from_low = lax.ppermute(high, along_x, forward)
    from_high = lax.ppermute(low, along_x, backward)

    left, right = pl.pallas_call(
        pack_lanes_kernel,
        in_specs=[VMEM] * 4,
        out_specs=[VMEM] * 2,
        out_shape=[shape(15, 8, 128)] * 2,
        compiler_params=PARAMS,
        name="pack_lanes",
    )(planes, weights, from_low, from_high)
    count = lax.axis_size("z")
    forward = [(i, i + 1) for i in range(count - 1)]
    backward = [(j, i) for i, j in forward]
    from_left = lax.ppermute(right, "z", forward)
    from_right = lax.ppermute(left, "z", backward)

    main, strip, cstrip = pl.pallas_call(
        body_kernel,
        in_specs=[VMEM] * 4,
        out_specs=[VMEM] * 3,
        out_shape=[shape(PLANES, ROWS, 128), shape(16, 40, 128), shape(COEFS, 40, 128)],
        scratch_shapes=[
            pltpu.VMEM((PLANES, EXT, 128), F32),
            pltpu.VMEM((PLANES, EXT, 128), F32),
            pltpu.VMEM((COEFS, EXT, 128), F32),
        ],
        compiler_params=PARAMS,
        cost_estimate=pl.CostEstimate(flops=20_000_000, bytes_accessed=4_000_000, transcendentals=0),
        name="body",
    )(planes, weights, from_low, from_high)
    sketch, gram = pl.pallas_call(
        edge_kernel,
        in_specs=[VMEM] * 5,
        out_specs=[VMEM] * 2,
        out_shape=[shape(PLANES, ROWS, 128), shape(16, 8, 128)],
        scratch_shapes=[
            pltpu.VMEM((16, EXT, 128), F32),
            pltpu.VMEM((16, EXT, 128), F32),
            pltpu.VMEM((COEFS, EXT, 128), F32),
            pltpu.VMEM((16, ROWS, 128), F32),
        ],
        compiler_params=PARAMS,
        name="edge",
    )(main, strip, cstrip, from_left, from_right)

    gathered = lax.all_to_all(gram, ("core", "z"), 0, 0, tiled=True)
    gram = pl.pallas_call(
        sum_kernel, in_specs=[VMEM], out_specs=VMEM, out_shape=shape(16, 8, 128), name="partial_sum"
    )(gathered)
    gathered = lax.all_to_all(gram, ("x", "y"), 0, 0, tiled=True)
    total_rows = PLANES // 16 * ROWS * 128 * lax.axis_size(("x", "y", "core", "z"))
    factor = pl.pallas_call(
        lambda *refs: cholesky_kernel(1.0 / total_rows, *refs),
        in_specs=[VMEM],
        out_specs=VMEM,
        out_shape=shape(16, 16),
        name="cholesky",
    )(gathered)
    return sketch.reshape(probes.shape), factor


def solution(mesh):
    fine = Mesh(mesh.devices.reshape(4, 4, 2, 8), ("x", "y", "core", "z"))
    across = ("x", "y", "core")
    placed = (P(None, None, None, across, "z"), P(None, None, across, "z"))
    return jax.shard_map(
        local,
        mesh=fine,
        in_specs=placed,
        out_specs=(P(None, None, None, across, "z"), P()),
        check_vma=False,
    )
```

```python
import jax
import jax.numpy as jnp
from jax import lax
from jax.experimental import pallas as pl
from jax.experimental.pallas import tpu as pltpu
from jax.sharding import Mesh, PartitionSpec as P

PLANES = 64
COEFS = 30
PAIRS = (PLANES + COEFS) // 2
ROWS = 32
EXT = 48
STARTS = ((5, 13, 21, 29, 35), (6, 14, 22, 30, 34), (7, 15, 23, 31, 33), (8, 16, 24, 32))
F32 = jnp.float32


def iota(shape, dim):
    return lax.broadcasted_iota(jnp.int32, shape, dim)


def lane_roll(array, shift):
    shift = shift % 128
    return array if shift == 0 else pltpu.roll(array, shift, array.ndim - 1)


def half_roll(array):
    return pltpu.roll(array, 4, array.ndim - 2)


def pack_rows_kernel(p_top, p_bottom, c_top, c_bottom, low_ref, high_ref):
    for first, last, offset, half in (
        (p_top, p_bottom, 0, PLANES // 2),
        (c_top, c_bottom, PLANES // 2, COEFS // 2),
    ):
        upper = iota((half, 8, 128), 1) < 4
        low_ref[offset : offset + half] = jnp.where(upper, first[:half], half_roll(first[half:]))
        high_ref[offset : offset + half] = jnp.where(upper, half_roll(last[:half]), last[half:])


def halo_tiles(low_ref, high_ref, index):
    low, high = low_ref[index], high_ref[index]
    upper = iota((8, 128), 0) < 4
    return jnp.where(upper, low, half_roll(high)), jnp.where(upper, half_roll(low), high)


def pack_lanes_kernel(p_ref, c_ref, low_ref, high_ref, left_ref, right_ref):
    lane = iota((8, 128), 1)
    halos = [None] * PLANES
    for k in range(PLANES // 2):
        halos[k], halos[k + PLANES // 2] = halo_tiles(low_ref, high_ref, k)
    first = lane % 8 < 4
    for z in range(2):
        for tile in range(5):
            both = []
            for c in range(2):
                packed = None
                for p in range(16):
                    plane = p * 4 + c * 2 + z
                    value = halos[plane] if tile == 4 else p_ref[plane, tile * 8 : tile * 8 + 8]
                    value = lane_roll(value, 8 * p + 4)
                    packed = value if packed is None else jnp.where(lane // 8 == p, value, packed)
                both.append(packed)
            right_ref[z * 5 + tile] = jnp.where(first, both[0], lane_roll(both[1], 4))
            left_ref[z * 5 + tile] = jnp.where(first, lane_roll(both[0], -4), both[1])
    chalos = [None] * COEFS
    for k in range(COEFS // 2):
        chalos[k], chalos[k + COEFS // 2] = halo_tiles(low_ref, high_ref, PLANES // 2 + k)
    for tile in range(5):
        right = left = None
        for n in range(COEFS):
            value = chalos[n] if tile == 4 else c_ref[n, tile * 8 : tile * 8 + 8]
            to_right, to_left = lane_roll(value, 4 * n + 4), lane_roll(value, 4 * n)
            if right is None:
                right, left = to_right, to_left
            else:
                right = jnp.where(lane // 4 == n, to_right, right)
                left = jnp.where(lane // 4 == n, to_left, left)
        right_ref[10 + tile] = right
        left_ref[10 + tile] = left


def step(source, target, coef, groups, starts, adjoint, shift=0, unroll=16):
    for s in starts:

        def weight(slot, z, move=0):
            return coef[slot * 2 + z, s + move : s + move + 8, :]

        up, down = (-1, 1) if adjoint else (0, 0)
        weights = {}
        for z in range(2):
            weights[14, z] = weight(14, z)
            for c in range(2):
                weights[c, z] = weight(c, z)
                slot = 2 + 6 * c
                weights[slot, z] = weight(slot, z, up)
                weights[slot + 1, z] = weight(slot + 1, z, down)
                weights[slot + 2, z] = weight(slot + 2, z)
                weights[slot + 3, z] = weight(slot + 3, z)
                vertical = slot + (4 if z == 0 else 5)
                weights[vertical, z] = weight(vertical, z)

        def body(group, carry):
            base = group * 4

            def field(c, z, move=0):
                return source[base + (c * 2 + z), s + move : s + move + 8, :]

            centre = {(c, z): field(c, z) for c in range(2) for z in range(2)}
            for c in range(2):
                for z in range(2):
                    value = centre[c, z]
                    slot = 2 + 6 * c
                    total = weights[c, z] * value
                    before, after = field(c, z, -1), field(c, z, 1)
                    if adjoint:
                        total = total + weights[slot, z] * before + weights[slot + 1, z] * after
                        total = total + lane_roll(weights[slot + 2, z] * value, 1)
                        total = total + lane_roll(weights[slot + 3, z] * value, -1)
                        vertical = slot + (5 if z == 0 else 4)
                        total = total + weights[vertical, 1 - z] * centre[c, 1 - z]
                        if c == 0:
                            total = total + weights[14, z] * centre[1, z]
                    else:
                        total = total + weights[slot, z] * after + weights[slot + 1, z] * before
                        total = total + weights[slot + 2, z] * lane_roll(value, -1)
                        total = total + weights[slot + 3, z] * lane_roll(value, 1)
                        vertical = slot + (4 if z == 0 else 5)
                        total = total + weights[vertical, z] * centre[c, 1 - z]
                        if c == 1:
                            total = total + weights[14, z] * centre[0, z]
                    target[base + (c * 2 + z), s + shift : s + shift + 8, :] = total
            return carry

        lax.fori_loop(0, groups, body, 0, unroll=min(unroll, groups))


def four_steps(first, second, coef, result, groups, shift):
    step(first, second, coef, groups, STARTS[0], False)
    step(second, first, coef, groups, STARTS[1], False)
    step(first, second, coef, groups, STARTS[2], True)
    step(second, result, coef, groups, STARTS[3], True, shift)


def fill(extended, own, low, high, half, offset):
    extended[:, 8:40, :] = own[...]
    for side, row in ((low, 4), (high, 40)):
        extended[:half, row : row + 4, :] = side[offset : offset + half, 0:4, :]
        extended[half:, row : row + 4, :] = side[offset : offset + half, 4:8, :]


def take_tile(ref, index, tile):
    if tile < 4:
        return ref[index, 8 + 8 * tile : 16 + 8 * tile, :]
    return jnp.where(iota((8, 128), 0) < 4, ref[index, 4:12, :], ref[index, 36:44, :])


def put_tile(ref, index, tile, value):
    if tile < 4:
        ref[index, 8 + 8 * tile : 16 + 8 * tile, :] = value
    else:
        ref[index, 4:8, :] = value[0:4]
        ref[index, 40:44, :] = value[4:8]


def body_kernel(p_ref, c_ref, low_ref, high_ref, main_ref, strip_ref, cstrip_ref, first, second, coef):
    fill(first, p_ref, low_ref, high_ref, PLANES // 2, 0)
    fill(coef, c_ref, low_ref, high_ref, COEFS // 2, PLANES // 2)
    lane = iota((8, 128), 1)
    offset = lane % 32
    near_right = [(lane // 32 == q) & (offset < 8) for q in range(4)]
    near_left = [(lane // 32 == q) & (offset >= 20) for q in range(4)]
    for tile in range(5):
        for index in range(16):
            total = jnp.zeros((8, 128), F32)
            for q in range(4):
                value = take_tile(first, q * 16 + index, tile)
                total = jnp.where(near_right[q], lane_roll(value, q * 32 + 8), total)
                total = jnp.where(near_left[q], lane_roll(value, q * 32 + 20), total)
            strip_ref[index, 8 * tile : 8 * tile + 8, :] = total
        for index in range(COEFS):
            value = take_tile(coef, index, tile)
            total = jnp.where(lane < 8, lane_roll(value, 8), 0.0)
            total = jnp.where((lane >= 20) & (lane < 28), lane_roll(value, 20), total)
            cstrip_ref[index, 8 * tile : 8 * tile + 8, :] = total
    four_steps(first, second, coef, main_ref, 16, -8)


def edge_kernel(
    main_ref, strip_ref, cstrip_ref, left_ref, right_ref, out_hbm, gram_ref, first, second, coef, result, out_ref, sem
):
    lane = iota((8, 128), 1)
    offset = lane % 32
    is_right = (offset >= 8) & (offset < 12)
    is_left = (offset >= 16) & (offset < 20)
    for z in range(2):
        for tile in range(5):
            left, right = left_ref[z * 5 + tile], right_ref[z * 5 + tile]
            for t in range(4):
                for c in range(2):
                    at = 8 * t + 4 * c
                    index = t * 4 + c * 2 + z
                    value = strip_ref[index, 8 * tile : 8 * tile + 8, :]
                    value = jnp.where(is_right, lane_roll(right, 8 - at), value)
                    value = jnp.where(is_left, lane_roll(left, 16 - at), value)
                    put_tile(first, index, tile, value)
    to_right = (lane >= 8) & (lane < 12)
    to_left = (lane >= 16) & (lane < 20)
    for tile in range(5):
        left, right = left_ref[10 + tile], right_ref[10 + tile]
        totals = []
        for n in range(COEFS):
            value = cstrip_ref[n, 8 * tile : 8 * tile + 8, :]
            value = jnp.where(to_right, lane_roll(right, 8 - 4 * n), value)
            totals.append(jnp.where(to_left, lane_roll(left, 16 - 4 * n), value))
        totals = [total + lane_roll(total, 32) for total in totals]
        totals = [total + lane_roll(total, 64) for total in totals]
        for n in range(COEFS):
            put_tile(coef, n, tile, totals[n])
    four_steps(first, second, coef, result, 4, -8)
    for row in range(0, ROWS, 8):
        for index in range(16):
            edge = result[index, row : row + 8, :]
            for q in range(4):
                value = main_ref[q * 16 + index, row : row + 8, :]
                value = jnp.where(lane >= 124, lane_roll(edge, 124 - (q * 32 + 4)), value)
                value = jnp.where(lane < 4, lane_roll(edge, -(q * 32 + 20)), value)
                out_ref[q * 16 + index, row : row + 8, :] = value
    copy = pltpu.make_async_copy(out_ref, out_hbm, sem)
    copy.start()

    view = out_ref.reshape(16, 4, ROWS, 128)
    block = jnp.concatenate(
        [
            view[:, part, row : row + 8, :].reshape(128, 128)
            for part in range(4)
            for row in range(0, ROWS, 8)
        ],
        axis=1,
    )
    gram = lax.dot_general(
        block, block, (((1,), (1,)), ((), ())), precision=lax.Precision.HIGHEST, preferred_element_type=F32
    )
    same = iota((128, 128), 0) % 8 == iota((128, 128), 1) % 8
    folded = jnp.where(same, gram, 0.0).reshape(16, 8, 128).sum(axis=1)
    source, target = iota((128, 128), 0) // 8, iota((128, 128), 1)
    tile = jnp.zeros((8, 128), F32)
    for half in range(2):
        select = (target == source + 16 * half).astype(F32)
        tile = tile + jnp.dot(
            folded[8 * half : 8 * half + 8], select, precision=lax.Precision.HIGHEST, preferred_element_type=F32
        )
    gram_ref[...] = jnp.broadcast_to(tile[None], gram_ref.shape)
    copy.wait()


def sum_kernel(in_ref, out_ref):
    out_ref[...] = jnp.broadcast_to(jnp.sum(in_ref[...], axis=0)[None], out_ref.shape)


def cholesky_kernel(scale, in_ref, out_ref):
    tile = jnp.sum(in_ref[...], axis=0) * scale
    row, col = iota((16, 128), 0), iota((16, 128), 1)
    work = jnp.concatenate([tile, lane_roll(tile, -16)], axis=0)
    work = jnp.where(col < 16, work, 0.0)
    for k in range(15):
        pivot = work[k : k + 1, k : k + 1]
        update = work[:, k : k + 1] * (work[k : k + 1, :] / pivot)
        work = jnp.where(row > k, work - update, work)
    diagonal = jnp.sum(jnp.where(row == col, work, 0.0), axis=1, keepdims=True)
    factor = jnp.where(col >= row, work / jnp.sqrt(diagonal), 0.0)
    out_ref[...] = factor[:, :16]


def shape(*dims):
    return jax.ShapeDtypeStruct(dims, F32)


VMEM = pl.BlockSpec(memory_space=pltpu.VMEM)
PARAMS = pltpu.CompilerParams(vmem_limit_bytes=32 << 20)


def neighbours(array, axes, pairs):
    return lax.ppermute(array, axes, pairs)


def local(probes, coefficients):
    planes = probes.reshape(PLANES, ROWS, 128)
    weights = coefficients.reshape(COEFS, ROWS, 128)
    spec_first = lambda n: pl.BlockSpec((n, 8, 128), lambda i: (0, 0, 0))
    spec_last = lambda n: pl.BlockSpec((n, 8, 128), lambda i: (0, ROWS // 8 - 1, 0))
    whole = pl.BlockSpec((PAIRS, 8, 128), lambda i: (0, 0, 0))
    low, high = pl.pallas_call(
        pack_rows_kernel,
        grid=(1,),
        in_specs=[spec_first(PLANES), spec_last(PLANES), spec_first(COEFS), spec_last(COEFS)],
        out_specs=[whole, whole],
        out_shape=[shape(PAIRS, 8, 128)] * 2,
        name="pack_rows",
    )(planes, planes, weights, weights)
    along_x = ("x", "y", "core")
    count = lax.axis_size(along_x)
    forward = [(i, i + 1) for i in range(count - 1)]
    backward = [(j, i) for i, j in forward]
    from_low = lax.ppermute(high, along_x, forward)
    from_high = lax.ppermute(low, along_x, backward)

    left, right = pl.pallas_call(
        pack_lanes_kernel,
        in_specs=[VMEM] * 4,
        out_specs=[VMEM] * 2,
        out_shape=[shape(15, 8, 128)] * 2,
        compiler_params=PARAMS,
        name="pack_lanes",
    )(planes, weights, from_low, from_high)
    count = lax.axis_size("z")
    forward = [(i, i + 1) for i in range(count - 1)]
    backward = [(j, i) for i, j in forward]
    from_left = lax.ppermute(right, "z", forward)
    from_right = lax.ppermute(left, "z", backward)

    main, strip, cstrip = pl.pallas_call(
        body_kernel,
        in_specs=[VMEM] * 4,
        out_specs=[VMEM] * 3,
        out_shape=[shape(PLANES, ROWS, 128), shape(16, 40, 128), shape(COEFS, 40, 128)],
        scratch_shapes=[
            pltpu.VMEM((PLANES, EXT, 128), F32),
            pltpu.VMEM((PLANES, EXT, 128), F32),
            pltpu.VMEM((COEFS, EXT, 128), F32),
        ],
        compiler_params=PARAMS,
        cost_estimate=pl.CostEstimate(flops=20_000_000, bytes_accessed=4_000_000, transcendentals=0),
        name="body",
    )(planes, weights, from_low, from_high)
    sketch, gram = pl.pallas_call(
        edge_kernel,
        in_specs=[VMEM] * 5,
        out_specs=[pl.BlockSpec(memory_space=pl.ANY), VMEM],
        out_shape=[shape(PLANES, ROWS, 128), shape(16, 8, 128)],
        scratch_shapes=[
            pltpu.VMEM((16, EXT, 128), F32),
            pltpu.VMEM((16, EXT, 128), F32),
            pltpu.VMEM((COEFS, EXT, 128), F32),
            pltpu.VMEM((16, ROWS, 128), F32),
            pltpu.VMEM((PLANES, ROWS, 128), F32),
            pltpu.SemaphoreType.DMA,
        ],
        compiler_params=PARAMS,
        name="edge",
    )(main, strip, cstrip, from_left, from_right)

    gathered = lax.all_to_all(gram, ("core", "z"), 0, 0, tiled=True)
    gram = pl.pallas_call(
        sum_kernel, in_specs=[VMEM], out_specs=VMEM, out_shape=shape(16, 8, 128), name="partial_sum"
    )(gathered)
    gathered = lax.all_to_all(gram, ("x", "y"), 0, 0, tiled=True)
    total_rows = PLANES // 16 * ROWS * 128 * lax.axis_size(("x", "y", "core", "z"))
    factor = pl.pallas_call(
        lambda *refs: cholesky_kernel(1.0 / total_rows, *refs),
        in_specs=[VMEM],
        out_specs=VMEM,
        out_shape=shape(16, 16),
        name="cholesky",
    )(gathered)
    return sketch.reshape(probes.shape), factor


def solution(mesh):
    fine = Mesh(mesh.devices.reshape(4, 4, 2, 8), ("x", "y", "core", "z"))
    across = ("x", "y", "core")
    placed = (P(None, None, None, across, "z"), P(None, None, across, "z"))
    return jax.shard_map(
        local,
        mesh=fine,
        in_specs=placed,
        out_specs=(P(None, None, None, across, "z"), P()),
        check_vma=False,
    )
```

```python
import jax
import jax.numpy as jnp
from jax import lax
from jax.experimental import pallas as pl
from jax.experimental.pallas import tpu as pltpu
from jax.sharding import Mesh, PartitionSpec as P

PLANES = 64
COEFS = 30
PAIRS = (PLANES + COEFS) // 2
ROWS = 32
EXT = 48
STRIP_STARTS = ((5, 13, 21, 29, 35), (6, 14, 22, 30, 34), (7, 15, 23, 31, 33), (8, 16, 24, 32))
INNER_STARTS = ((1, 9, 17, 23), (2, 10, 18, 22), (3, 11, 19, 21), (4, 12, 20))
OUTER_STARTS = ((5, 7, 17, 19), (6, 18), (7, 17), (8, 16))
ACROSS = ("x", "y", "core")
F32 = jnp.float32


def iota(shape, dim):
    return lax.broadcasted_iota(jnp.int32, shape, dim)


def lane_roll(array, shift):
    shift = shift % 128
    return array if shift == 0 else pltpu.roll(array, shift, array.ndim - 1)


def half_roll(array):
    return pltpu.roll(array, 4, array.ndim - 2)


def pack_rows_kernel(p_hbm, c_hbm, low_ref, high_ref, p_top, p_bottom, c_top, c_bottom, sems):
    sources = (p_hbm.at[:, 0:8], p_hbm.at[:, ROWS - 8 : ROWS], c_hbm.at[:, 0:8], c_hbm.at[:, ROWS - 8 : ROWS])
    targets = (p_top, p_bottom, c_top, c_bottom)
    copies = [pltpu.make_async_copy(src, dst, sems.at[i]) for i, (src, dst) in enumerate(zip(sources, targets))]
    for copy in copies:
        copy.start()
    for copy in copies:
        copy.wait()
    for first, last, offset, half in (
        (p_top, p_bottom, 0, PLANES // 2),
        (c_top, c_bottom, PLANES // 2, COEFS // 2),
    ):
        upper = iota((half, 8, 128), 1) < 4
        low_ref[offset : offset + half] = jnp.where(upper, first[:half], half_roll(first[half:]))
        high_ref[offset : offset + half] = jnp.where(upper, half_roll(last[:half]), last[half:])


def inside(axes):
    index = lax.axis_index(axes)
    last = lax.axis_size(axes) - 1
    return jnp.where(index > 0, 1.0, 0.0).astype(F32), jnp.where(index < last, 1.0, 0.0).astype(F32)


def pack_probes(load, lane):
    first = lane % 8 < 4
    both = []
    for c in range(2):
        packed = None
        for p in range(16):
            value = lane_roll(load(p * 4 + c * 2), 8 * p + 4)
            packed = value if packed is None else jnp.where(lane // 8 == p, value, packed)
        both.append(packed)
    right = jnp.where(first, both[0], lane_roll(both[1], 4))
    left = jnp.where(first, lane_roll(both[0], -4), both[1])
    return left, right


def pack_coefs(load, lane):
    right = left = None
    for n in range(COEFS):
        value = load(n)
        to_right, to_left = lane_roll(value, 4 * n + 4), lane_roll(value, 4 * n)
        if right is None:
            right, left = to_right, to_left
        else:
            right = jnp.where(lane // 4 == n, to_right, right)
            left = jnp.where(lane // 4 == n, to_left, left)
    return left, right


def make_strip(load, lane):
    offset = lane % 32
    total = jnp.zeros((8, 128), F32)
    for q in range(4):
        value = load(q * 16)
        here = lane // 32 == q
        total = jnp.where(here & (offset < 8), lane_roll(value, q * 32 + 8), total)
        total = jnp.where(here & (offset >= 20), lane_roll(value, q * 32 + 20), total)
    return total


def make_cstrip(value, lane):
    total = jnp.where(lane < 8, lane_roll(value, 8), 0.0)
    return jnp.where((lane >= 20) & (lane < 28), lane_roll(value, 20), total)


def inner_kernel(p_ref, c_ref, main_ref, left_ref, right_ref, strip_ref, cstrip_ref, first, second):
    lane = iota((8, 128), 1)
    for tile in range(4):
        rows = slice(8 * tile, 8 * tile + 8)
        for z in range(2):
            left_ref[z * 5 + tile], right_ref[z * 5 + tile] = pack_probes(lambda i: p_ref[i + z, rows, :], lane)
        left_ref[10 + tile], right_ref[10 + tile] = pack_coefs(lambda i: c_ref[i, rows, :], lane)
        for index in range(16):
            strip_ref[index, rows, :] = make_strip(lambda i: p_ref[i + index, rows, :], lane)
        for index in range(COEFS):
            cstrip_ref[index, rows, :] = make_cstrip(c_ref[index, rows, :], lane)
    step(p_ref, first, c_ref, 16, INNER_STARTS[0], False)
    step(first, second, c_ref, 16, INNER_STARTS[1], False)
    step(second, first, c_ref, 16, INNER_STARTS[2], True)
    step(first, main_ref, c_ref, 16, INNER_STARTS[3], True)


def halo_kernel(low_ref, high_ref, own_left_ref, own_right_ref, left_ref, right_ref):
    lane = iota((8, 128), 1)
    upper = iota((8, 128), 0) < 4
    has_low, has_high = inside(ACROSS)
    halos = {}
    for offset, half in ((0, PLANES // 2), (PLANES // 2, COEFS // 2)):
        for k in range(half):
            low, high = low_ref[offset + k] * has_low, high_ref[offset + k] * has_high
            halos[offset * 2 + k] = jnp.where(upper, low, half_roll(high))
            halos[offset * 2 + k + half] = jnp.where(upper, half_roll(low), high)
    for part in range(3):
        rows = slice(part * 5, part * 5 + 4)
        left_ref[rows] = own_left_ref[rows]
        right_ref[rows] = own_right_ref[rows]
    for z in range(2):
        left_ref[z * 5 + 4], right_ref[z * 5 + 4] = pack_probes(lambda i: halos[i + z], lane)
    left_ref[14], right_ref[14] = pack_coefs(lambda i: halos[PLANES + i], lane)


def step(source, target, coef, groups, starts, adjoint, shift=0, unroll=16):
    for s in starts:

        def weight(slot, z, move=0):
            return coef[slot * 2 + z, s + move : s + move + 8, :]

        up, down = (-1, 1) if adjoint else (0, 0)
        weights = {}
        for z in range(2):
            weights[14, z] = weight(14, z)
            for c in range(2):
                weights[c, z] = weight(c, z)
                slot = 2 + 6 * c
                weights[slot, z] = weight(slot, z, up)
                weights[slot + 1, z] = weight(slot + 1, z, down)
                weights[slot + 2, z] = weight(slot + 2, z)
                weights[slot + 3, z] = weight(slot + 3, z)
                vertical = slot + (4 if z == 0 else 5)
                weights[vertical, z] = weight(vertical, z)

        def body(group, carry):
            base = group * 4

            def field(c, z, move=0):
                return source[base + (c * 2 + z), s + move : s + move + 8, :]

            centre = {(c, z): field(c, z) for c in range(2) for z in range(2)}
            for c in range(2):
                for z in range(2):
                    value = centre[c, z]
                    slot = 2 + 6 * c
                    total = weights[c, z] * value
                    before, after = field(c, z, -1), field(c, z, 1)
                    if adjoint:
                        total = total + weights[slot, z] * before + weights[slot + 1, z] * after
                        total = total + lane_roll(weights[slot + 2, z] * value, 1)
                        total = total + lane_roll(weights[slot + 3, z] * value, -1)
                        vertical = slot + (5 if z == 0 else 4)
                        total = total + weights[vertical, 1 - z] * centre[c, 1 - z]
                        if c == 0:
                            total = total + weights[14, z] * centre[1, z]
                    else:
                        total = total + weights[slot, z] * after + weights[slot + 1, z] * before
                        total = total + weights[slot + 2, z] * lane_roll(value, -1)
                        total = total + weights[slot + 3, z] * lane_roll(value, 1)
                        vertical = slot + (4 if z == 0 else 5)
                        total = total + weights[vertical, z] * centre[c, 1 - z]
                        if c == 1:
                            total = total + weights[14, z] * centre[0, z]
                    target[base + (c * 2 + z), s + shift : s + shift + 8, :] = total
            return carry

        lax.fori_loop(0, groups, body, 0, unroll=min(unroll, groups))


def fill(outer, own, low, high, half, offset, has_low, has_high):
    outer[:, 8:16, :] = own[:, 0:8, :]
    outer[:, 16:24, :] = own[:, ROWS - 8 : ROWS, :]
    for side, row, has in ((low, 4, has_low), (high, 24, has_high)):
        outer[:half, row : row + 4, :] = side[offset : offset + half, 0:4, :] * has
        outer[half:, row : row + 4, :] = side[offset : offset + half, 4:8, :] * has


def outer_kernel(p_ref, c_ref, low_ref, high_ref, result_ref, strip_ref, cstrip_ref, first, second, coef):
    has_low, has_high = inside(ACROSS)
    fill(first, p_ref, low_ref, high_ref, PLANES // 2, 0, has_low, has_high)
    fill(coef, c_ref, low_ref, high_ref, COEFS // 2, PLANES // 2, has_low, has_high)
    lane = iota((8, 128), 1)
    upper = iota((8, 128), 0) < 4

    def halo(ref, index):
        return jnp.where(upper, ref[index, 4:12, :], ref[index, 20:28, :])

    for index in range(16):
        strip_ref[index] = make_strip(lambda i: halo(first, i + index), lane)
    for index in range(COEFS):
        cstrip_ref[index] = make_cstrip(halo(coef, index), lane)
    step(first, second, coef, 16, OUTER_STARTS[0], False)
    step(second, first, coef, 16, OUTER_STARTS[1], False)
    step(first, second, coef, 16, OUTER_STARTS[2], True)
    step(second, result_ref, coef, 16, OUTER_STARTS[3], True, -8)


def put_tile(ref, index, tile, value):
    if tile < 4:
        ref[index, 8 + 8 * tile : 16 + 8 * tile, :] = value
    else:
        ref[index, 4:8, :] = value[0:4]
        ref[index, 40:44, :] = value[4:8]


def edge_kernel(
    main_ref,
    outer_ref,
    strip_ref,
    halo_strip_ref,
    cstrip_ref,
    halo_cstrip_ref,
    left_ref,
    right_ref,
    out_hbm,
    gram_ref,
    first,
    second,
    coef,
    result,
    out_ref,
    sem,
):
    lane = iota((8, 128), 1)
    upper = iota((8, 128), 0) < 4
    offset = lane % 32
    is_right = (offset >= 8) & (offset < 12)
    is_left = (offset >= 16) & (offset < 20)
    has_left, has_right = inside("z")

    def own(ref, halo_ref, index, tile):
        return ref[index, 8 * tile : 8 * tile + 8, :] if tile < 4 else halo_ref[index]

    for z in range(2):
        for tile in range(5):
            left, right = left_ref[z * 5 + tile] * has_left, right_ref[z * 5 + tile] * has_right
            for t in range(4):
                for c in range(2):
                    at = 8 * t + 4 * c
                    index = t * 4 + c * 2 + z
                    value = own(strip_ref, halo_strip_ref, index, tile)
                    value = jnp.where(is_right, lane_roll(right, 8 - at), value)
                    value = jnp.where(is_left, lane_roll(left, 16 - at), value)
                    put_tile(first, index, tile, value)
    to_right = (lane >= 8) & (lane < 12)
    to_left = (lane >= 16) & (lane < 20)
    for tile in range(5):
        left, right = left_ref[10 + tile] * has_left, right_ref[10 + tile] * has_right
        totals = []
        for n in range(COEFS):
            value = own(cstrip_ref, halo_cstrip_ref, n, tile)
            value = jnp.where(to_right, lane_roll(right, 8 - 4 * n), value)
            totals.append(jnp.where(to_left, lane_roll(left, 16 - 4 * n), value))
        totals = [total + lane_roll(total, 32) for total in totals]
        totals = [total + lane_roll(total, 64) for total in totals]
        for n in range(COEFS):
            put_tile(coef, n, tile, totals[n])
    step(first, second, coef, 4, STRIP_STARTS[0], False)
    step(second, first, coef, 4, STRIP_STARTS[1], False)
    step(first, second, coef, 4, STRIP_STARTS[2], True)
    step(second, result, coef, 4, STRIP_STARTS[3], True, -8)
    for row in range(0, ROWS, 8):
        for index in range(16):
            edge = result[index, row : row + 8, :]
            for q in range(4):
                plane = q * 16 + index
                value = main_ref[plane, row : row + 8, :]
                if row == 0:
                    value = jnp.where(upper, outer_ref[plane, 0:8, :], value)
                elif row == ROWS - 8:
                    value = jnp.where(upper, value, outer_ref[plane, 8:16, :])
                value = jnp.where(lane >= 124, lane_roll(edge, 124 - (q * 32 + 4)), value)
                value = jnp.where(lane < 4, lane_roll(edge, -(q * 32 + 20)), value)
                out_ref[plane, row : row + 8, :] = value
    copy = pltpu.make_async_copy(out_ref, out_hbm, sem)
    copy.start()

    view = out_ref.reshape(16, 4, ROWS, 128)
    block = jnp.concatenate(
        [
            view[:, part, row : row + 8, :].reshape(128, 128)
            for part in range(4)
            for row in range(0, ROWS, 8)
        ],
        axis=1,
    )
    gram = lax.dot_general(
        block, block, (((1,), (1,)), ((), ())), precision=lax.Precision.HIGHEST, preferred_element_type=F32
    )
    same = iota((128, 128), 0) % 8 == iota((128, 128), 1) % 8
    folded = jnp.where(same, gram, 0.0).reshape(16, 8, 128).sum(axis=1)
    select = (iota((128, 128), 0) // 8 == iota((128, 128), 1) % 16).astype(F32)
    spread = jnp.dot(folded, select, precision=lax.Precision.HIGHEST, preferred_element_type=F32)
    mine = iota((16, 128), 1) // 16 == iota((16, 128), 0) % 8
    tile = jnp.where(mine, spread, 0.0).reshape(2, 8, 128).sum(axis=1)
    gram_ref[...] = jnp.broadcast_to(tile[None], gram_ref.shape)
    copy.wait()


def cholesky_kernel(scale, in_ref, out_ref):
    tile = jnp.sum(in_ref[...], axis=0) * scale
    row, col = iota((16, 128), 0), iota((16, 128), 1)
    work = jnp.concatenate([jnp.broadcast_to(tile[i : i + 1], (8, 128)) for i in range(2)], axis=0)
    work = jnp.where(col // 16 == row % 8, work, 0.0)
    for shift in (64, 32, 16):
        work = work + lane_roll(work, shift)
    work = jnp.where(col < 16, work, 0.0)
    for k in range(15):
        pivot = work[k : k + 1, k : k + 1]
        update = work[:, k : k + 1] * (work[k : k + 1, :] / pivot)
        work = jnp.where(row > k, work - update, work)
    diagonal = jnp.sum(jnp.where(row == col, work, 0.0), axis=1, keepdims=True)
    factor = jnp.where(col >= row, work / jnp.sqrt(diagonal), 0.0)
    out_ref[...] = factor[:, :16]


def shape(*dims):
    return jax.ShapeDtypeStruct(dims, F32)


VMEM = pl.BlockSpec(memory_space=pltpu.VMEM)
ANY = pl.BlockSpec(memory_space=pl.ANY)


def call(kernel, name, inputs, outputs, scratch=(), in_specs=None, out_specs=None, flops=1_000_000):
    moved = 4 * sum(a.size for a in inputs) + 4 * sum(a.size for a in outputs)
    return pl.pallas_call(
        kernel,
        in_specs=in_specs or [VMEM] * len(inputs),
        out_specs=out_specs or [VMEM] * len(outputs),
        out_shape=list(outputs),
        scratch_shapes=list(scratch),
        compiler_params=pltpu.CompilerParams(vmem_limit_bytes=32 << 20),
        cost_estimate=pl.CostEstimate(flops=flops, bytes_accessed=moved, transcendentals=0),
        name=name,
    )(*inputs)


def exchange(to_low, to_high, axes):
    count = lax.axis_size(axes)
    forward = [(i, (i + 1) % count) for i in range(count)]
    backward = [(j, i) for i, j in forward]
    return lax.ppermute(to_high, axes, forward), lax.ppermute(to_low, axes, backward)


def local(probes, coefficients):
    planes = probes.reshape(PLANES, ROWS, 128)
    weights = coefficients.reshape(COEFS, ROWS, 128)
    scratch = lambda *dims: pltpu.VMEM(dims, F32)
    low, high = call(
        pack_rows_kernel,
        "pack_rows",
        (planes, weights),
        [shape(PAIRS, 8, 128)] * 2,
        [scratch(PLANES, 8, 128)] * 2 + [scratch(COEFS, 8, 128)] * 2 + [pltpu.SemaphoreType.DMA((4,))],
        in_specs=[pl.BlockSpec(memory_space=pltpu.HBM)] * 2,
    )
    from_low, from_high = exchange(low, high, ACROSS)

    main, own_left, own_right, strip, cstrip = call(
        inner_kernel,
        "inner",
        (planes, weights),
        [
            shape(PLANES, ROWS, 128),
            shape(15, 8, 128),
            shape(15, 8, 128),
            shape(16, ROWS, 128),
            shape(COEFS, ROWS, 128),
        ],
        [scratch(PLANES, ROWS, 128)] * 2,
        flops=15_000_000,
    )
    left, right = call(
        halo_kernel, "halo", (from_low, from_high, own_left, own_right), [shape(15, 8, 128)] * 2
    )
    from_left, from_right = exchange(left, right, "z")

    outer, halo_strip, halo_cstrip = call(
        outer_kernel,
        "outer",
        (planes, weights, from_low, from_high),
        [shape(PLANES, 16, 128), shape(16, 8, 128), shape(COEFS, 8, 128)],
        [scratch(PLANES, 32, 128)] * 2 + [scratch(COEFS, 32, 128)],
        flops=10_000_000,
    )
    sketch, gram = call(
        edge_kernel,
        "edge",
        (main, outer, strip, halo_strip, cstrip, halo_cstrip, from_left, from_right),
        [shape(PLANES, ROWS, 128), shape(16, 2, 128)],
        [
            scratch(16, EXT, 128),
            scratch(16, EXT, 128),
            scratch(COEFS, EXT, 128),
            scratch(16, ROWS, 128),
            scratch(PLANES, ROWS, 128),
            pltpu.SemaphoreType.DMA,
        ],
        out_specs=[ANY, VMEM],
    )

    gathered = lax.all_to_all(gram, ("core", "z"), 0, 0, tiled=True)
    gram = jnp.broadcast_to(gathered.sum(axis=0)[None], (16, 2, 128))
    gathered = lax.all_to_all(gram, ("x", "y"), 0, 0, tiled=True)
    total_rows = PLANES // 16 * ROWS * 128 * lax.axis_size(ACROSS + ("z",))
    (factor,) = call(
        lambda *refs: cholesky_kernel(1.0 / total_rows, *refs), "cholesky", (gathered,), [shape(16, 16)]
    )
    return sketch.reshape(probes.shape), factor


def solution(mesh):
    fine = Mesh(mesh.devices.reshape(4, 4, 2, 8), ("x", "y", "core", "z"))
    placed = (P(None, None, None, ACROSS, "z"), P(None, None, ACROSS, "z"))
    return jax.shard_map(
        local,
        mesh=fine,
        in_specs=placed,
        out_specs=(P(None, None, None, ACROSS, "z"), P()),
        check_vma=False,
    )
```

```python
import jax
import jax.numpy as jnp
from jax import lax
from jax.experimental import pallas as pl
from jax.experimental.pallas import tpu as pltpu
from jax.sharding import Mesh, PartitionSpec as P

PLANES = 64
COEFS = 30
PAIRS = (PLANES + COEFS) // 2
ROWS = 32
EXT = 48
STRIP_STARTS = ((5, 13, 21, 29, 35), (6, 14, 22, 30, 34), (7, 15, 23, 31, 33), (8, 16, 24, 32))
INNER_STARTS = ((1, 9, 17, 23), (2, 10, 18, 22), (3, 11, 19, 21), (4, 12, 20))
OUTER_STARTS = ((5, 7, 17, 19), (6, 18), (7, 17), (8, 16))
ACROSS = ("x", "y", "core")
F32 = jnp.float32


def iota(shape, dim):
    return lax.broadcasted_iota(jnp.int32, shape, dim)


def lane_roll(array, shift):
    shift = shift % 128
    return array if shift == 0 else pltpu.roll(array, shift, array.ndim - 1)


def half_roll(array):
    return pltpu.roll(array, 4, array.ndim - 2)


def pack_rows_kernel(p_hbm, c_hbm, low_ref, high_ref, p_top, p_bottom, c_top, c_bottom, sems):
    sources = (p_hbm.at[:, 0:8], p_hbm.at[:, ROWS - 8 : ROWS], c_hbm.at[:, 0:8], c_hbm.at[:, ROWS - 8 : ROWS])
    targets = (p_top, p_bottom, c_top, c_bottom)
    copies = [pltpu.make_async_copy(src, dst, sems.at[i]) for i, (src, dst) in enumerate(zip(sources, targets))]
    for copy in copies:
        copy.start()
    for copy in copies:
        copy.wait()
    for first, last, offset, half in (
        (p_top, p_bottom, 0, PLANES // 2),
        (c_top, c_bottom, PLANES // 2, COEFS // 2),
    ):
        upper = iota((half, 8, 128), 1) < 4
        low_ref[offset : offset + half] = jnp.where(upper, first[:half], half_roll(first[half:]))
        high_ref[offset : offset + half] = jnp.where(upper, half_roll(last[:half]), last[half:])


def inside(axes):
    index = lax.axis_index(axes)
    last = lax.axis_size(axes) - 1
    return jnp.where(index > 0, 1.0, 0.0).astype(F32), jnp.where(index < last, 1.0, 0.0).astype(F32)


def pack_columns(values, lane):
    first = lane % 8 < 4
    both = []
    for planes in (values[:16], values[16:]):
        packed = None
        for k, value in enumerate(planes):
            value = lane_roll(value, 8 * k + 4)
            packed = value if packed is None else jnp.where(lane // 8 == k, value, packed)
        both.append(packed)
    right = jnp.where(first, both[0], lane_roll(both[1], 4))
    left = jnp.where(first, lane_roll(both[0], -4), both[1])
    return left, right


def halo_columns(left, right, lane):
    first = lane % 8 < 4
    return jnp.where(first, right, lane_roll(left, 4)), jnp.where(first, lane_roll(right, -4), left)


def make_strips(load, count, lane):
    group, offset = lane // 32, lane % 32
    strips = []
    for index in range(count):
        total = lane_roll(load(index), 8)
        for q in range(1, 4):
            total = jnp.where(group == q, lane_roll(load(index + q * 16), q * 32 + 8), total)
        strips.append(total)
    return [jnp.where(offset < 8, total, lane_roll(total, 8)) for total in strips]


def make_cstrips(load, lane):
    strips = [load(index) for index in range(COEFS)]
    strips = [jnp.where(lane < 8, lane_roll(v, 8), jnp.where((lane >= 16) & (lane < 24), lane_roll(v, 16), 0.0)) for v in strips]
    strips = [v + lane_roll(v, 32) for v in strips]
    return [v + lane_roll(v, 64) for v in strips]


def inner_kernel(p_ref, c_ref, main_ref, left_ref, right_ref, strip_ref, cstrip_ref, first, second):
    lane = iota((8, 128), 1)
    for tile in range(4):
        rows = slice(8 * tile, 8 * tile + 8)
        for z in range(2):
            planes = [p_ref[p * 4 + c * 2 + z, rows, :] for c in range(2) for p in range(16)]
            left_ref[z * 5 + tile], right_ref[z * 5 + tile] = pack_columns(planes, lane)
        planes = [c_ref[index, rows, :] for index in range(COEFS)]
        left_ref[10 + tile], right_ref[10 + tile] = pack_columns(planes, lane)
        for index, strip in enumerate(make_strips(lambda i: p_ref[i, rows, :], 16, lane)):
            strip_ref[index, rows, :] = strip
        for index, strip in enumerate(make_cstrips(lambda i: c_ref[i, rows, :], lane)):
            cstrip_ref[index, rows, :] = strip
    step(p_ref, first, c_ref, 16, INNER_STARTS[0], False)
    step(first, second, c_ref, 16, INNER_STARTS[1], False)
    step(second, first, c_ref, 16, INNER_STARTS[2], True)
    step(first, main_ref, c_ref, 16, INNER_STARTS[3], True)


def halo_kernel(low_ref, high_ref, own_left_ref, own_right_ref, left_ref, right_ref):
    lane = iota((8, 128), 1)
    upper = iota((8, 128), 0) < 4
    has_low, has_high = inside(ACROSS)
    halos = {}
    for offset, half in ((0, PLANES // 2), (PLANES // 2, COEFS // 2)):
        for k in range(half):
            low, high = low_ref[offset + k] * has_low, high_ref[offset + k] * has_high
            halos[offset * 2 + k] = jnp.where(upper, low, half_roll(high))
            halos[offset * 2 + k + half] = jnp.where(upper, half_roll(low), high)
    for part in range(3):
        rows = slice(part * 5, part * 5 + 4)
        left_ref[rows] = own_left_ref[rows]
        right_ref[rows] = own_right_ref[rows]
    for z in range(2):
        planes = [halos[p * 4 + c * 2 + z] for c in range(2) for p in range(16)]
        left_ref[z * 5 + 4], right_ref[z * 5 + 4] = pack_columns(planes, lane)
    left_ref[14], right_ref[14] = pack_columns([halos[PLANES + i] for i in range(COEFS)], lane)


def step(source, target, coef, groups, starts, adjoint, shift=0, unroll=16):
    for s in starts:

        def weight(slot, z, move=0):
            return coef[slot * 2 + z, s + move : s + move + 8, :]

        up, down = (-1, 1) if adjoint else (0, 0)
        weights = {}
        for z in range(2):
            weights[14, z] = weight(14, z)
            for c in range(2):
                weights[c, z] = weight(c, z)
                slot = 2 + 6 * c
                weights[slot, z] = weight(slot, z, up)
                weights[slot + 1, z] = weight(slot + 1, z, down)
                weights[slot + 2, z] = weight(slot + 2, z)
                weights[slot + 3, z] = weight(slot + 3, z)
                vertical = slot + (4 if z == 0 else 5)
                weights[vertical, z] = weight(vertical, z)

        def body(group, carry):
            base = group * 4

            def field(c, z, move=0):
                return source[base + (c * 2 + z), s + move : s + move + 8, :]

            centre = {(c, z): field(c, z) for c in range(2) for z in range(2)}
            for c in range(2):
                for z in range(2):
                    value = centre[c, z]
                    slot = 2 + 6 * c
                    total = weights[c, z] * value
                    before, after = field(c, z, -1), field(c, z, 1)
                    if adjoint:
                        total = total + weights[slot, z] * before + weights[slot + 1, z] * after
                        total = total + lane_roll(weights[slot + 2, z] * value, 1)
                        total = total + lane_roll(weights[slot + 3, z] * value, -1)
                        vertical = slot + (5 if z == 0 else 4)
                        total = total + weights[vertical, 1 - z] * centre[c, 1 - z]
                        if c == 0:
                            total = total + weights[14, z] * centre[1, z]
                    else:
                        total = total + weights[slot, z] * after + weights[slot + 1, z] * before
                        total = total + weights[slot + 2, z] * lane_roll(value, -1)
                        total = total + weights[slot + 3, z] * lane_roll(value, 1)
                        vertical = slot + (4 if z == 0 else 5)
                        total = total + weights[vertical, z] * centre[c, 1 - z]
                        if c == 1:
                            total = total + weights[14, z] * centre[0, z]
                    target[base + (c * 2 + z), s + shift : s + shift + 8, :] = total
            return carry

        lax.fori_loop(0, groups, body, 0, unroll=min(unroll, groups))


def fill(outer, own, low, high, half, offset, has_low, has_high):
    outer[:, 8:16, :] = own[:, 0:8, :]
    outer[:, 16:24, :] = own[:, ROWS - 8 : ROWS, :]
    for side, row, has in ((low, 4, has_low), (high, 24, has_high)):
        outer[:half, row : row + 4, :] = side[offset : offset + half, 0:4, :] * has
        outer[half:, row : row + 4, :] = side[offset : offset + half, 4:8, :] * has


def put_tile(ref, index, tile, value):
    if tile < 4:
        ref[index, 8 + 8 * tile : 16 + 8 * tile, :] = value
    else:
        ref[index, 4:8, :] = value[0:4]
        ref[index, 40:44, :] = value[4:8]


def gram_of(block, contract):
    return lax.dot_general(
        block,
        block,
        (((contract,), (contract,)), ((), ())),
        precision=lax.Precision.HIGHEST,
        preferred_element_type=F32,
    )


def outer_kernel(
    p_ref, c_ref, low_ref, high_ref, inner_ref, main_ref, gram_ref, strip_ref, cstrip_ref, first, second, coef, result
):
    has_low, has_high = inside(ACROSS)
    fill(first, p_ref, low_ref, high_ref, PLANES // 2, 0, has_low, has_high)
    fill(coef, c_ref, low_ref, high_ref, COEFS // 2, PLANES // 2, has_low, has_high)
    lane = iota((8, 128), 1)
    upper = iota((8, 128), 0) < 4

    def halo(ref, index):
        return jnp.where(upper, ref[index, 4:12, :], ref[index, 20:28, :])

    for index, strip in enumerate(make_strips(lambda i: halo(first, i), 16, lane)):
        strip_ref[index] = strip
    for index, strip in enumerate(make_cstrips(lambda i: halo(coef, i), lane)):
        cstrip_ref[index] = strip
    step(first, second, coef, 16, OUTER_STARTS[0], False)
    step(second, first, coef, 16, OUTER_STARTS[1], False)
    step(first, second, coef, 16, OUTER_STARTS[2], True)
    step(second, result, coef, 16, OUTER_STARTS[3], True, -8)
    known = (lane >= 4) & (lane < 124)
    blocks = []
    for part in range(4):
        for row in range(0, ROWS, 8):
            block = []
            for p in range(16):
                plane = p * 4 + part
                value = inner_ref[plane, row : row + 8, :]
                if row == 0:
                    value = jnp.where(upper, result[plane, 0:8, :], value)
                elif row == ROWS - 8:
                    value = jnp.where(upper, value, result[plane, 8:16, :])
                main_ref[plane, row : row + 8, :] = value
                block.append(jnp.where(known, value, 0.0))
            blocks.append(jnp.concatenate(block, axis=0))
    gram_ref[...] = gram_of(jnp.concatenate(blocks, axis=1), 1)


def edge_kernel(
    main_ref,
    partial_ref,
    strip_ref,
    halo_strip_ref,
    cstrip_ref,
    halo_cstrip_ref,
    left_ref,
    right_ref,
    out_hbm,
    gram_ref,
    first,
    second,
    coef,
    result,
    out_ref,
    sem,
):
    lane = iota((8, 128), 1)
    group, offset = lane // 32, lane % 32
    is_halo = (offset >= 8) & (offset < 16)
    has_left, has_right = inside("z")

    def own(ref, halo_ref, index, tile):
        return ref[index, 8 * tile : 8 * tile + 8, :] if tile < 4 else halo_ref[index]

    def columns(part, tile):
        index = part * 5 + tile
        return halo_columns(left_ref[index] * has_left, right_ref[index] * has_right, lane)

    for z in range(2):
        for tile in range(5):
            halos = columns(z, tile)
            for t in range(4):
                for c in range(2):
                    index = t * 4 + c * 2 + z
                    value = own(strip_ref, halo_strip_ref, index, tile)
                    put_tile(first, index, tile, jnp.where(is_halo, lane_roll(halos[c], 8 - 8 * t), value))
    for tile in range(5):
        halos = columns(2, tile)
        for half in range(2):
            rolled = [lane_roll(halos[half], 8 * k) for k in range(16)]
            for k in range(16 if half == 0 else COEFS - 16):
                index = half * 16 + k
                spread = rolled[(1 - k) % 16]
                for q in range(1, 4):
                    spread = jnp.where(group == q, rolled[(4 * q + 1 - k) % 16], spread)
                value = own(cstrip_ref, halo_cstrip_ref, index, tile)
                put_tile(coef, index, tile, jnp.where(is_halo, spread, value))
    step(first, second, coef, 4, STRIP_STARTS[0], False)
    step(second, first, coef, 4, STRIP_STARTS[1], False)
    step(first, second, coef, 4, STRIP_STARTS[2], True)
    step(second, result, coef, 4, STRIP_STARTS[3], True, -8)

    blocks = []
    for part in range(4):
        for row in range(0, ROWS, 8):
            packed = None
            for t in range(4):
                value = result[t * 4 + part, row : row + 8, :]
                value = jnp.where(lane % 8 < 4, lane_roll(value, 8 * t - 4), lane_roll(value, 8 * t - 12))
                packed = value if packed is None else jnp.where(offset // 8 == t, value, packed)
            blocks.append(packed)
    is_edge = (lane < 4) | (lane >= 124)
    for i, packed in enumerate(blocks):
        part, row = i // 4, i % 4 * 8
        for p in range(16):
            plane = p * 4 + part
            value = main_ref[plane, row : row + 8, :]
            out_ref[plane, row : row + 8, :] = jnp.where(is_edge, lane_roll(packed, 124 - 8 * p), value)
    copy = pltpu.make_async_copy(out_ref, out_hbm, sem)
    copy.start()

    gram = partial_ref[...] + gram_of(jnp.concatenate(blocks, axis=0), 0)
    same = iota((128, 128), 0) % 8 == iota((128, 128), 1) % 8
    folded = jnp.where(same, gram, 0.0).reshape(16, 8, 128).sum(axis=1)
    select = (iota((128, 128), 0) // 8 == iota((128, 128), 1) % 16).astype(F32)
    spread = jnp.dot(folded, select, precision=lax.Precision.HIGHEST, preferred_element_type=F32)
    mine = iota((16, 128), 1) // 16 == iota((16, 128), 0) % 8
    tile = jnp.where(mine, spread, 0.0).reshape(2, 8, 128).sum(axis=1)
    gram_ref[...] = jnp.broadcast_to(tile[None], gram_ref.shape)
    copy.wait()


def cholesky_kernel(scale, in_ref, out_ref):
    tile = jnp.sum(in_ref[...], axis=0) * scale
    row, col = iota((16, 128), 0), iota((16, 128), 1)
    work = jnp.concatenate([jnp.broadcast_to(tile[i : i + 1], (8, 128)) for i in range(2)], axis=0)
    work = jnp.where(col // 16 == row % 8, work, 0.0)
    for shift in (64, 32, 16):
        work = work + lane_roll(work, shift)
    work = jnp.where(col < 16, work, 0.0)
    for k in range(15):
        pivot = work[k : k + 1, k : k + 1]
        update = work[:, k : k + 1] * (work[k : k + 1, :] / pivot)
        work = jnp.where(row > k, work - update, work)
    diagonal = jnp.sum(jnp.where(row == col, work, 0.0), axis=1, keepdims=True)
    factor = jnp.where(col >= row, work / jnp.sqrt(diagonal), 0.0)
    out_ref[...] = factor[:, :16]


def shape(*dims):
    return jax.ShapeDtypeStruct(dims, F32)


VMEM = pl.BlockSpec(memory_space=pltpu.VMEM)
ANY = pl.BlockSpec(memory_space=pl.ANY)


def call(kernel, name, inputs, outputs, scratch=(), in_specs=None, out_specs=None, flops=1_000_000, vmem=32):
    moved = 4 * sum(a.size for a in inputs) + 4 * sum(a.size for a in outputs)
    return pl.pallas_call(
        kernel,
        in_specs=in_specs or [VMEM] * len(inputs),
        out_specs=out_specs or [VMEM] * len(outputs),
        out_shape=list(outputs),
        scratch_shapes=list(scratch),
        compiler_params=pltpu.CompilerParams(vmem_limit_bytes=vmem << 20),
        cost_estimate=pl.CostEstimate(flops=flops, bytes_accessed=moved, transcendentals=0),
        name=name,
    )(*inputs)


def exchange(to_low, to_high, axes):
    count = lax.axis_size(axes)
    forward = [(i, (i + 1) % count) for i in range(count)]
    backward = [(j, i) for i, j in forward]
    return lax.ppermute(to_high, axes, forward), lax.ppermute(to_low, axes, backward)


def local(probes, coefficients):
    planes = probes.reshape(PLANES, ROWS, 128)
    weights = coefficients.reshape(COEFS, ROWS, 128)
    scratch = lambda *dims: pltpu.VMEM(dims, F32)
    low, high = call(
        pack_rows_kernel,
        "pack_rows",
        (planes, weights),
        [shape(PAIRS, 8, 128)] * 2,
        [scratch(PLANES, 8, 128)] * 2 + [scratch(COEFS, 8, 128)] * 2 + [pltpu.SemaphoreType.DMA((4,))],
        in_specs=[ANY, ANY],
        vmem=60,
    )
    from_low, from_high = exchange(low, high, ACROSS)

    inner, own_left, own_right, strip, cstrip = call(
        inner_kernel,
        "inner",
        (planes, weights),
        [
            shape(PLANES, ROWS, 128),
            shape(15, 8, 128),
            shape(15, 8, 128),
            shape(16, ROWS, 128),
            shape(COEFS, ROWS, 128),
        ],
        [scratch(PLANES, ROWS, 128)] * 2,
        flops=15_000_000,
    )
    left, right = call(
        halo_kernel, "halo", (from_low, from_high, own_left, own_right), [shape(15, 8, 128)] * 2
    )
    from_left, from_right = exchange(left, right, "z")

    main, partial, halo_strip, halo_cstrip = call(
        outer_kernel,
        "outer",
        (planes, weights, from_low, from_high, inner),
        [shape(PLANES, ROWS, 128), shape(128, 128), shape(16, 8, 128), shape(COEFS, 8, 128)],
        [scratch(PLANES, 32, 128)] * 2 + [scratch(COEFS, 32, 128), scratch(PLANES, 16, 128)],
        flops=10_000_000,
    )
    sketch, gram = call(
        edge_kernel,
        "edge",
        (main, partial, strip, halo_strip, cstrip, halo_cstrip, from_left, from_right),
        [shape(PLANES, ROWS, 128), shape(16, 2, 128)],
        [
            scratch(16, EXT, 128),
            scratch(16, EXT, 128),
            scratch(COEFS, EXT, 128),
            scratch(16, ROWS, 128),
            scratch(PLANES, ROWS, 128),
            pltpu.SemaphoreType.DMA,
        ],
        out_specs=[ANY, VMEM],
    )

    gathered = lax.all_to_all(gram, ("core", "z"), 0, 0, tiled=True)
    gram = jnp.broadcast_to(gathered.sum(axis=0)[None], (16, 2, 128))
    gathered = lax.all_to_all(gram, ("x", "y"), 0, 0, tiled=True)
    total_rows = PLANES // 16 * ROWS * 128 * lax.axis_size(ACROSS + ("z",))
    (factor,) = call(
        lambda *refs: cholesky_kernel(1.0 / total_rows, *refs), "cholesky", (gathered,), [shape(16, 16)]
    )
    return sketch.reshape(probes.shape), factor


def solution(mesh):
    fine = Mesh(mesh.devices.reshape(4, 4, 2, 8), ("x", "y", "core", "z"))
    placed = (P(None, None, None, ACROSS, "z"), P(None, None, ACROSS, "z"))
    return jax.shard_map(
        local,
        mesh=fine,
        in_specs=placed,
        out_specs=(P(None, None, None, ACROSS, "z"), P()),
        check_vma=False,
    )
```

```python
import math

import jax
import jax.numpy as jnp
from jax import lax
from jax.experimental import pallas as pl
from jax.experimental.pallas import tpu as pltpu
from jax.sharding import Mesh, PartitionSpec as P

PLANES = 64
COEFS = 30
PAIRS = (PLANES + COEFS) // 2
ROWS = 32
EXT = 48
STRIP_STARTS = ((5, 13, 21, 29, 35), (6, 14, 22, 30, 34), (7, 15, 23, 31, 33), (8, 16, 24, 32))
INNER_STARTS = ((1, 9, 17, 23), (2, 10, 18, 22), (3, 11, 19, 21), (4, 12, 20))
OUTER_STARTS = ((5, 13, 19), (6, 18), (7, 17), (8, 16))
ACROSS = ("x", "y", "core")
F32 = jnp.float32


def iota(shape, dim):
    return lax.broadcasted_iota(jnp.int32, shape, dim)


def lane_roll(array, shift):
    shift = shift % 128
    return array if shift == 0 else pltpu.roll(array, shift, array.ndim - 1)


def half_roll(array):
    return pltpu.roll(array, 4, array.ndim - 2)


def is_even(axes):
    return lax.rem(lax.axis_index(axes), 2) == 0


def pack_rows_kernel(p_hbm, c_hbm, first_ref, second_ref, p_top, p_bottom, c_top, c_bottom, sems):
    sources = (p_hbm.at[:, 0:8], p_hbm.at[:, ROWS - 8 : ROWS], c_hbm.at[:, 0:8], c_hbm.at[:, ROWS - 8 : ROWS])
    targets = (p_top, p_bottom, c_top, c_bottom)
    copies = [pltpu.make_async_copy(src, dst, sems.at[i]) for i, (src, dst) in enumerate(zip(sources, targets))]
    for copy in copies:
        copy.start()
    even = is_even(ACROSS)
    for copy in copies:
        copy.wait()
    for first, last, offset, half in (
        (p_top, p_bottom, 0, PLANES // 2),
        (c_top, c_bottom, PLANES // 2, COEFS // 2),
    ):
        upper = iota((half, 8, 128), 1) < 4
        low = jnp.where(upper, first[:half], half_roll(first[half:]))
        high = jnp.where(upper, half_roll(last[:half]), last[half:])
        first_ref[offset : offset + half] = jnp.where(even, high, low)
        second_ref[offset : offset + half] = jnp.where(even, low, high)


def inside(axes):
    index = lax.axis_index(axes)
    last = lax.axis_size(axes) - 1
    return jnp.where(index > 0, 1.0, 0.0).astype(F32), jnp.where(index < last, 1.0, 0.0).astype(F32)


def pack_columns(values, lane):
    both = []
    for planes in (values[:16], values[16:]):
        packed = None
        for k, value in enumerate(planes):
            value = lane_roll(value, 8 * k + 4)
            packed = value if packed is None else jnp.where(lane // 8 == k, value, packed)
        both.append(packed)
    return split_columns(both, lane)


def halo_columns(left, right, lane):
    first = lane % 8 < 4
    return jnp.where(first, right, lane_roll(left, 4)), jnp.where(first, lane_roll(right, -4), left)


def gather_columns(load, count, lane):
    group = lane // 32
    gathered = []
    for index in range(count):
        total = lane_roll(load(index), 8)
        for q in range(1, 4):
            total = jnp.where(group == q, lane_roll(load(index + q * 16), q * 32 + 8), total)
        gathered.append(total)
    return gathered


def own_strips(gathered, lane):
    return [jnp.where(lane % 32 < 8, total, lane_roll(total, 8)) for total in gathered]


def split_columns(both, lane):
    first = lane % 8 < 4
    return jnp.where(first, lane_roll(both[0], -4), both[1]), jnp.where(first, both[0], lane_roll(both[1], 4))


def pack_gathered(gathered, z, lane):
    block = lane % 32 // 8
    both = []
    for c in range(2):
        packed = None
        for t in range(4):
            value = lane_roll(gathered[t * 4 + c * 2 + z], 8 * t - 4)
            packed = value if packed is None else jnp.where(block == t, value, packed)
        both.append(packed)
    return split_columns(both, lane)


def make_cstrips(values):
    source, target = iota((128, 128), 0), iota((128, 128), 1) % 32
    wanted = jnp.where(target < 8, target + 120, jnp.where((target >= 16) & (target < 24), target - 16, -1))
    select = (source == wanted).astype(jnp.bfloat16)
    total = None
    for _ in range(3):
        part = values.astype(jnp.bfloat16)
        values = values - part.astype(F32)
        moved = jnp.dot(part, select, preferred_element_type=F32)
        total = moved if total is None else total + moved
    return total


def inner_kernel(p_ref, c_ref, main_ref, left_ref, right_ref, strip_ref, cstrip_ref, first, second):
    lane = iota((8, 128), 1)
    for tile in range(4):
        rows = slice(8 * tile, 8 * tile + 8)
        gathered = gather_columns(lambda i: p_ref[i, rows, :], 16, lane)
        for z in range(2):
            left_ref[z * 5 + tile], right_ref[z * 5 + tile] = pack_gathered(gathered, z, lane)
        for index, strip in enumerate(own_strips(gathered, lane)):
            strip_ref[index, rows, :] = strip
        planes = [c_ref[index, rows, :] for index in range(COEFS)]
        left_ref[10 + tile], right_ref[10 + tile] = pack_columns(planes, lane)
    cstrip_ref[...] = make_cstrips(c_ref[...].reshape(COEFS * ROWS, 128)).reshape(COEFS, ROWS, 128)
    step(p_ref, first, c_ref, 16, INNER_STARTS[0], False)
    step(first, second, c_ref, 16, INNER_STARTS[1], False)
    step(second, first, c_ref, 16, INNER_STARTS[2], True)
    step(first, main_ref, c_ref, 16, INNER_STARTS[3], True)


def halo_kernel(x_first_ref, x_second_ref, own_left_ref, own_right_ref, first_ref, second_ref):
    lane = iota((8, 128), 1)
    upper = iota((8, 128), 0) < 4
    has_low, has_high = inside(ACROSS)
    even, even_z = is_even(ACROSS), is_even("z")

    def put(index, left, right):
        first_ref[index] = jnp.where(even_z, right, left)
        second_ref[index] = jnp.where(even_z, left, right)

    halos = {}
    for offset, half in ((0, PLANES // 2), (PLANES // 2, COEFS // 2)):
        for k in range(half):
            x_first, x_second = x_first_ref[offset + k], x_second_ref[offset + k]
            low = jnp.where(even, x_second, x_first) * has_low
            high = jnp.where(even, x_first, x_second) * has_high
            halos[offset * 2 + k] = jnp.where(upper, low, half_roll(high))
            halos[offset * 2 + k + half] = jnp.where(upper, half_roll(low), high)
    for part in range(3):
        rows = slice(part * 5, part * 5 + 4)
        put(rows, own_left_ref[rows], own_right_ref[rows])
    for z in range(2):
        planes = [halos[p * 4 + c * 2 + z] for c in range(2) for p in range(16)]
        put(z * 5 + 4, *pack_columns(planes, lane))
    put(14, *pack_columns([halos[PLANES + i] for i in range(COEFS)], lane))


def step(source, target, coef, groups, starts, adjoint, shift=0, unroll=16):
    for s in starts:

        def weight(slot, z, move=0):
            return coef[slot * 2 + z, s + move : s + move + 8, :]

        up, down = (-1, 1) if adjoint else (0, 0)
        weights = {}
        for z in range(2):
            weights[14, z] = weight(14, z)
            for c in range(2):
                weights[c, z] = weight(c, z)
                slot = 2 + 6 * c
                weights[slot, z] = weight(slot, z, up)
                weights[slot + 1, z] = weight(slot + 1, z, down)
                weights[slot + 2, z] = weight(slot + 2, z)
                weights[slot + 3, z] = weight(slot + 3, z)
                vertical = slot + (4 if z == 0 else 5)
                weights[vertical, z] = weight(vertical, z)

        def body(group, carry):
            base = group * 4

            def field(c, z, move=0):
                return source[base + (c * 2 + z), s + move : s + move + 8, :]

            centre = {(c, z): field(c, z) for c in range(2) for z in range(2)}
            for c in range(2):
                for z in range(2):
                    value = centre[c, z]
                    slot = 2 + 6 * c
                    total = weights[c, z] * value
                    before, after = field(c, z, -1), field(c, z, 1)
                    if adjoint:
                        total = total + weights[slot, z] * before + weights[slot + 1, z] * after
                        total = total + lane_roll(weights[slot + 2, z] * value, 1)
                        total = total + lane_roll(weights[slot + 3, z] * value, -1)
                        vertical = slot + (5 if z == 0 else 4)
                        total = total + weights[vertical, 1 - z] * centre[c, 1 - z]
                        if c == 0:
                            total = total + weights[14, z] * centre[1, z]
                    else:
                        total = total + weights[slot, z] * after + weights[slot + 1, z] * before
                        total = total + weights[slot + 2, z] * lane_roll(value, -1)
                        total = total + weights[slot + 3, z] * lane_roll(value, 1)
                        vertical = slot + (4 if z == 0 else 5)
                        total = total + weights[vertical, z] * centre[c, 1 - z]
                        if c == 1:
                            total = total + weights[14, z] * centre[0, z]
                    target[base + (c * 2 + z), s + shift : s + shift + 8, :] = total
            return carry

        lax.fori_loop(0, groups, body, 0, unroll=min(unroll, groups))


def fill(outer, own, x_first, x_second, half, offset, has_low, has_high, even):
    outer[:, 8:16, :] = own[:, 0:8, :]
    outer[:, 16:24, :] = own[:, ROWS - 8 : ROWS, :]
    for here, there, row, has in ((x_second, x_first, 4, has_low), (x_first, x_second, 24, has_high)):
        side = jnp.where(even, here[offset : offset + half], there[offset : offset + half]) * has
        outer[:half, row : row + 4, :] = side[:, 0:4, :]
        outer[half:, row : row + 4, :] = side[:, 4:8, :]


def put_tile(ref, index, tile, value):
    if tile < 4:
        ref[index, 8 + 8 * tile : 16 + 8 * tile, :] = value
    else:
        ref[index, 4:8, :] = value[0:4]
        ref[index, 40:44, :] = value[4:8]


def gram_of(block, contract):
    return lax.dot_general(
        block,
        block,
        (((contract,), (contract,)), ((), ())),
        precision=lax.Precision.HIGHEST,
        preferred_element_type=F32,
    )


def outer_kernel(
    p_ref, c_ref, x_first_ref, x_second_ref, inner_ref, main_ref, gram_ref, strip_ref, cstrip_ref, first, second, coef, result
):
    has_low, has_high = inside(ACROSS)
    even = is_even(ACROSS)
    fill(first, p_ref, x_first_ref, x_second_ref, PLANES // 2, 0, has_low, has_high, even)
    fill(coef, c_ref, x_first_ref, x_second_ref, COEFS // 2, PLANES // 2, has_low, has_high, even)
    lane = iota((8, 128), 1)
    upper = iota((8, 128), 0) < 4

    def halo(ref, index):
        return jnp.where(upper, ref[index, 4:12, :], ref[index, 20:28, :])

    gathered = gather_columns(lambda i: halo(first, i), 16, lane)
    for index, strip in enumerate(own_strips(gathered, lane)):
        strip_ref[index] = strip
    halos = jnp.concatenate([halo(coef, index) for index in range(COEFS)], axis=0)
    cstrip_ref[...] = make_cstrips(halos).reshape(COEFS, 8, 128)
    step(first, second, coef, 16, OUTER_STARTS[0], False)
    step(second, first, coef, 16, OUTER_STARTS[1], False)
    step(first, second, coef, 16, OUTER_STARTS[2], True)
    step(second, result, coef, 16, OUTER_STARTS[3], True, -8)
    known = (lane >= 4) & (lane < 124)
    blocks = []
    for part in range(4):
        for row in range(0, ROWS, 8):
            block = []
            for p in range(16):
                plane = p * 4 + part
                value = inner_ref[plane, row : row + 8, :]
                if row == 0:
                    value = jnp.where(upper, result[plane, 0:8, :], value)
                elif row == ROWS - 8:
                    value = jnp.where(upper, value, result[plane, 8:16, :])
                main_ref[plane, row : row + 8, :] = value
                block.append(jnp.where(known, value, 0.0))
            blocks.append(jnp.concatenate(block, axis=0))
    high = [block.astype(jnp.bfloat16) for block in blocks]
    low = [(block - part.astype(F32)).astype(jnp.bfloat16) for block, part in zip(blocks, high)]
    high, low = jnp.concatenate(high, axis=1), jnp.concatenate(low, axis=1)
    product = lambda a, b: lax.dot_general(a, b, (((1,), (1,)), ((), ())), preferred_element_type=F32)
    mixed = product(high, low)
    gram_ref[...] = product(high, high) + product(low, low) + (mixed + mixed.T)


def edge_kernel(
    main_ref,
    partial_ref,
    strip_ref,
    halo_strip_ref,
    cstrip_ref,
    halo_cstrip_ref,
    y_first_ref,
    y_second_ref,
    out_hbm,
    gram_ref,
    first,
    second,
    coef,
    result,
    out_ref,
    sem,
):
    lane = iota((8, 128), 1)
    group, offset = lane // 32, lane % 32
    is_halo = (offset >= 8) & (offset < 16)
    has_left, has_right = inside("z")
    even = is_even("z")

    def own(ref, halo_ref, index, tile):
        return ref[index, 8 * tile : 8 * tile + 8, :] if tile < 4 else halo_ref[index]

    def columns(part, tile):
        index = part * 5 + tile
        y_first, y_second = y_first_ref[index], y_second_ref[index]
        left, right = jnp.where(even, y_second, y_first), jnp.where(even, y_first, y_second)
        return halo_columns(left * has_left, right * has_right, lane)

    for z in range(2):
        for tile in range(5):
            halos = columns(z, tile)
            for t in range(4):
                for c in range(2):
                    index = t * 4 + c * 2 + z
                    value = own(strip_ref, halo_strip_ref, index, tile)
                    put_tile(first, index, tile, jnp.where(is_halo, lane_roll(halos[c], 8 - 8 * t), value))
    for tile in range(5):
        halos = columns(2, tile)
        for half in range(2):
            rolled = [lane_roll(halos[half], 8 * k) for k in range(16)]
            for k in range(16 if half == 0 else COEFS - 16):
                index = half * 16 + k
                spread = rolled[(1 - k) % 16]
                for q in range(1, 4):
                    spread = jnp.where(group == q, rolled[(4 * q + 1 - k) % 16], spread)
                value = own(cstrip_ref, halo_cstrip_ref, index, tile)
                put_tile(coef, index, tile, jnp.where(is_halo, spread, value))
    step(first, second, coef, 4, STRIP_STARTS[0], False)
    step(second, first, coef, 4, STRIP_STARTS[1], False)
    step(first, second, coef, 4, STRIP_STARTS[2], True)
    step(second, result, coef, 4, STRIP_STARTS[3], True, -8)

    blocks = []
    for part in range(4):
        for row in range(0, ROWS, 8):
            packed = None
            for t in range(4):
                value = result[t * 4 + part, row : row + 8, :]
                value = jnp.where(lane % 8 < 4, lane_roll(value, 8 * t - 4), lane_roll(value, 8 * t - 12))
                packed = value if packed is None else jnp.where(offset // 8 == t, value, packed)
            blocks.append(packed)
    is_edge = (lane < 4) | (lane >= 124)
    for i, packed in enumerate(blocks):
        part, row = i // 4, i % 4 * 8
        for p in range(16):
            plane = p * 4 + part
            value = main_ref[plane, row : row + 8, :]
            out_ref[plane, row : row + 8, :] = jnp.where(is_edge, lane_roll(packed, 124 - 8 * p), value)
    copy = pltpu.make_async_copy(out_ref, out_hbm, sem)
    copy.start()

    gram = partial_ref[...] + gram_of(jnp.concatenate(blocks, axis=0), 0)
    same = iota((128, 128), 0) % 8 == iota((128, 128), 1) % 8
    folded = jnp.where(same, gram, 0.0).reshape(16, 8, 128).sum(axis=1)
    select = (iota((128, 128), 0) // 8 == iota((128, 128), 1) % 16).astype(F32)
    spread = jnp.dot(folded, select, precision=lax.Precision.HIGHEST, preferred_element_type=F32)
    mine = iota((16, 128), 1) // 16 == iota((16, 128), 0) % 8
    tile = jnp.where(mine, spread, 0.0).reshape(2, 8, 128).sum(axis=1)
    gram_ref[...] = jnp.broadcast_to(tile[None], gram_ref.shape)
    copy.wait()


def cholesky_kernel(scale, in_ref, out_ref):
    tile = jnp.sum(in_ref[...], axis=0) * scale
    row, col = iota((16, 128), 0), iota((16, 128), 1)
    work = jnp.concatenate([jnp.broadcast_to(tile[i : i + 1], (8, 128)) for i in range(2)], axis=0)
    work = jnp.where(col // 16 == row % 8, work, 0.0)
    for shift in (64, 32, 16):
        work = work + lane_roll(work, shift)
    work = jnp.where(col < 16, work, 0.0)
    for k in range(15):
        pivot = work[k : k + 1, k : k + 1]
        update = work[:, k : k + 1] * (work[k : k + 1, :] / pivot)
        work = jnp.where(row > k, work - update, work)
    diagonal = jnp.sum(jnp.where(row == col, work, 0.0), axis=1, keepdims=True)
    factor = jnp.where(col >= row, work / jnp.sqrt(diagonal), 0.0)
    out_ref[...] = factor[:, :16]


def shape(*dims):
    return jax.ShapeDtypeStruct(dims, F32)


VMEM = pl.BlockSpec(memory_space=pltpu.VMEM)
ANY = pl.BlockSpec(memory_space=pl.ANY)


def call(kernel, name, inputs, outputs, scratch=(), in_specs=None, out_specs=None, flops=1_000_000, vmem=32):
    moved = 4 * sum(math.prod(a.shape) for a in (*inputs, *outputs))
    return pl.pallas_call(
        kernel,
        in_specs=in_specs or [VMEM] * len(inputs),
        out_specs=out_specs or [VMEM] * len(outputs),
        out_shape=list(outputs),
        scratch_shapes=list(scratch),
        compiler_params=pltpu.CompilerParams(vmem_limit_bytes=vmem << 20),
        cost_estimate=pl.CostEstimate(flops=flops, bytes_accessed=moved, transcendentals=0),
        name=name,
    )(*inputs)


def exchange(first, second, axes):
    count = lax.axis_size(axes)
    inner = [(i, i ^ 1) for i in range(count)]
    outer = [(i, (((i + 1) ^ 1) - 1) % count) for i in range(count)]
    return lax.ppermute(first, axes, inner), lax.ppermute(second, axes, outer)


def local(probes, coefficients):
    planes = probes.reshape(PLANES, ROWS, 128)
    weights = coefficients.reshape(COEFS, ROWS, 128)
    scratch = lambda *dims: pltpu.VMEM(dims, F32)
    x_first, x_second = call(
        pack_rows_kernel,
        "pack_rows",
        [pltpu.with_memory_space_constraint(array, pltpu.HBM) for array in (planes, weights)],
        [pltpu.VMEM((PAIRS, 8, 128), F32)] * 2,
        [scratch(PLANES, 8, 128)] * 2 + [scratch(COEFS, 8, 128)] * 2 + [pltpu.SemaphoreType.DMA((4,))],
        in_specs=[pl.BlockSpec(memory_space=pltpu.HBM)] * 2,
    )
    x_first, x_second = exchange(x_first, x_second, ACROSS)

    inner, own_left, own_right, strip, cstrip = call(
        inner_kernel,
        "inner",
        (planes, weights),
        [
            shape(PLANES, ROWS, 128),
            shape(15, 8, 128),
            shape(15, 8, 128),
            shape(16, ROWS, 128),
            shape(COEFS, ROWS, 128),
        ],
        [scratch(PLANES, ROWS, 128)] * 2,
        flops=15_000_000,
    )
    y_first, y_second = call(
        halo_kernel, "halo", (x_first, x_second, own_left, own_right), [shape(15, 8, 128)] * 2
    )
    y_first, y_second = exchange(y_first, y_second, "z")

    main, partial, halo_strip, halo_cstrip = call(
        outer_kernel,
        "outer",
        (planes, weights, x_first, x_second, inner),
        [shape(PLANES, ROWS, 128), shape(128, 128), shape(16, 8, 128), shape(COEFS, 8, 128)],
        [scratch(PLANES, 32, 128)] * 2 + [scratch(COEFS, 32, 128), scratch(PLANES, 16, 128)],
        flops=10_000_000,
    )
    sketch, gram = call(
        edge_kernel,
        "edge",
        (main, partial, strip, halo_strip, cstrip, halo_cstrip, y_first, y_second),
        [shape(PLANES, ROWS, 128), shape(16, 2, 128)],
        [
            scratch(16, EXT, 128),
            scratch(16, EXT, 128),
            scratch(COEFS, EXT, 128),
            scratch(16, ROWS, 128),
            scratch(PLANES, ROWS, 128),
            pltpu.SemaphoreType.DMA,
        ],
        out_specs=[ANY, VMEM],
    )

    gathered = lax.all_to_all(gram, ("core", "z"), 0, 0, tiled=True)
    gram = jnp.broadcast_to(gathered.sum(axis=0)[None], (16, 2, 128))
    gathered = lax.all_to_all(gram, ("x", "y"), 0, 0, tiled=True)
    total_rows = PLANES // 16 * ROWS * 128 * lax.axis_size(ACROSS + ("z",))
    (factor,) = call(
        lambda *refs: cholesky_kernel(1.0 / total_rows, *refs), "cholesky", (gathered,), [shape(16, 16)]
    )
    return sketch.reshape(probes.shape), factor


def solution(mesh):
    fine = Mesh(mesh.devices.reshape(4, 4, 2, 8), ("x", "y", "core", "z"))
    placed = (P(None, None, None, ACROSS, "z"), P(None, None, ACROSS, "z"))
    return jax.shard_map(
        local,
        mesh=fine,
        in_specs=placed,
        out_specs=(P(None, None, None, ACROSS, "z"), P()),
        check_vma=False,
    )
```

```python
import math

import jax
import jax.numpy as jnp
from jax import lax
from jax.experimental import pallas as pl
from jax.experimental.pallas import tpu as pltpu
from jax.sharding import Mesh, PartitionSpec as P

PLANES = 64
COEFS = 30
PAIRS = (PLANES + COEFS) // 2
ROWS = 32
EXT = 48
STRIP_STARTS = ((5, 13, 21, 29, 35), (6, 14, 22, 30, 34), (7, 15, 23, 31, 33), (8, 16, 24, 32))
INNER_STARTS = ((1, 9, 17, 23), (2, 10, 18, 22), (3, 11, 19, 21), (4, 12, 20))
OUTER_STARTS = ((5, 13, 19), (6, 18), (7, 17), (8, 16))
ACROSS = ("x", "y", "core")
F32 = jnp.float32


def iota(shape, dim):
    return lax.broadcasted_iota(jnp.int32, shape, dim)


def lane_roll(array, shift):
    shift = shift % 128
    return array if shift == 0 else pltpu.roll(array, shift, array.ndim - 1)


def half_roll(array):
    return pltpu.roll(array, 4, array.ndim - 2)


def is_even(axes):
    return lax.rem(lax.axis_index(axes), 2) == 0


def pack_rows_kernel(p_hbm, c_hbm, first_ref, second_ref, p_top, p_bottom, c_top, c_bottom, sems):
    sources = (p_hbm.at[:, 0:8], p_hbm.at[:, ROWS - 8 : ROWS], c_hbm.at[:, 0:8], c_hbm.at[:, ROWS - 8 : ROWS])
    targets = (p_top, p_bottom, c_top, c_bottom)
    copies = [pltpu.make_async_copy(src, dst, sems.at[i]) for i, (src, dst) in enumerate(zip(sources, targets))]
    for copy in copies:
        copy.start()
    even = is_even(ACROSS)
    for copy in copies:
        copy.wait()
    for first, last, offset, half in (
        (p_top, p_bottom, 0, PLANES // 2),
        (c_top, c_bottom, PLANES // 2, COEFS // 2),
    ):
        upper = iota((half, 8, 128), 1) < 4
        low = jnp.where(upper, first[:half], half_roll(first[half:]))
        high = jnp.where(upper, half_roll(last[:half]), last[half:])
        first_ref[offset : offset + half] = jnp.where(even, high, low)
        second_ref[offset : offset + half] = jnp.where(even, low, high)


def inside(axes):
    index = lax.axis_index(axes)
    last = lax.axis_size(axes) - 1
    return jnp.where(index > 0, 1.0, 0.0).astype(F32), jnp.where(index < last, 1.0, 0.0).astype(F32)


def pack_columns(values, lane):
    both = []
    for planes in (values[:16], values[16:]):
        packed = None
        for k, value in enumerate(planes):
            value = lane_roll(value, 8 * k + 4)
            packed = value if packed is None else jnp.where(lane // 8 == k, value, packed)
        both.append(packed)
    return split_columns(both, lane)


def halo_columns(left, right, lane):
    first = lane % 8 < 4
    return jnp.where(first, right, lane_roll(left, 4)), jnp.where(first, lane_roll(right, -4), left)


def gather_columns(load, count, lane):
    group = lane // 32
    gathered = []
    for index in range(count):
        total = lane_roll(load(index), 8)
        for q in range(1, 4):
            total = jnp.where(group == q, lane_roll(load(index + q * 16), q * 32 + 8), total)
        gathered.append(total)
    return gathered


def own_strips(gathered, lane):
    return [jnp.where(lane % 32 < 8, total, lane_roll(total, 8)) for total in gathered]


def split_columns(both, lane):
    first = lane % 8 < 4
    return jnp.where(first, lane_roll(both[0], -4), both[1]), jnp.where(first, both[0], lane_roll(both[1], 4))


def make_cstrips(values):
    source, target = iota((128, 128), 0), iota((128, 128), 1) % 32
    wanted = jnp.where(target < 8, target + 120, jnp.where((target >= 16) & (target < 24), target - 16, -1))
    select = (source == wanted).astype(jnp.bfloat16)
    total = None
    for _ in range(3):
        part = values.astype(jnp.bfloat16)
        values = values - part.astype(F32)
        moved = jnp.dot(part, select, preferred_element_type=F32)
        total = moved if total is None else total + moved
    return total


def inner_kernel(p_ref, c_ref, main_ref, left_ref, right_ref, first, second):
    lane = iota((8, 128), 1)
    for tile in range(4):
        rows = slice(8 * tile, 8 * tile + 8)
        for z in range(2):
            planes = [p_ref[p * 4 + c * 2 + z, rows, :] for c in range(2) for p in range(16)]
            left_ref[z * 5 + tile], right_ref[z * 5 + tile] = pack_columns(planes, lane)
        planes = [c_ref[index, rows, :] for index in range(COEFS)]
        left_ref[10 + tile], right_ref[10 + tile] = pack_columns(planes, lane)
    step(p_ref, first, c_ref, 16, INNER_STARTS[0], False)
    step(first, second, c_ref, 16, INNER_STARTS[1], False)
    step(second, first, c_ref, 16, INNER_STARTS[2], True)
    step(first, main_ref, c_ref, 16, INNER_STARTS[3], True)


def halo_kernel(x_first_ref, x_second_ref, own_left_ref, own_right_ref, first_ref, second_ref):
    lane = iota((8, 128), 1)
    upper = iota((8, 128), 0) < 4
    has_low, has_high = inside(ACROSS)
    even, even_z = is_even(ACROSS), is_even("z")

    def put(index, left, right):
        first_ref[index] = jnp.where(even_z, right, left)
        second_ref[index] = jnp.where(even_z, left, right)

    halos = {}
    for offset, half in ((0, PLANES // 2), (PLANES // 2, COEFS // 2)):
        for k in range(half):
            x_first, x_second = x_first_ref[offset + k], x_second_ref[offset + k]
            low = jnp.where(even, x_second, x_first) * has_low
            high = jnp.where(even, x_first, x_second) * has_high
            halos[offset * 2 + k] = jnp.where(upper, low, half_roll(high))
            halos[offset * 2 + k + half] = jnp.where(upper, half_roll(low), high)
    for part in range(3):
        rows = slice(part * 5, part * 5 + 4)
        put(rows, own_left_ref[rows], own_right_ref[rows])
    for z in range(2):
        planes = [halos[p * 4 + c * 2 + z] for c in range(2) for p in range(16)]
        put(z * 5 + 4, *pack_columns(planes, lane))
    put(14, *pack_columns([halos[PLANES + i] for i in range(COEFS)], lane))


def step(source, target, coef, groups, starts, adjoint, shift=0, unroll=16):
    for s in starts:

        def weight(slot, z, move=0):
            return coef[slot * 2 + z, s + move : s + move + 8, :]

        up, down = (-1, 1) if adjoint else (0, 0)
        weights = {}
        for z in range(2):
            weights[14, z] = weight(14, z)
            for c in range(2):
                weights[c, z] = weight(c, z)
                slot = 2 + 6 * c
                weights[slot, z] = weight(slot, z, up)
                weights[slot + 1, z] = weight(slot + 1, z, down)
                weights[slot + 2, z] = weight(slot + 2, z)
                weights[slot + 3, z] = weight(slot + 3, z)
                vertical = slot + (4 if z == 0 else 5)
                weights[vertical, z] = weight(vertical, z)

        def body(group, carry):
            base = group * 4

            def field(c, z, move=0):
                return source[base + (c * 2 + z), s + move : s + move + 8, :]

            centre = {(c, z): field(c, z) for c in range(2) for z in range(2)}
            for c in range(2):
                for z in range(2):
                    value = centre[c, z]
                    slot = 2 + 6 * c
                    total = weights[c, z] * value
                    before, after = field(c, z, -1), field(c, z, 1)
                    if adjoint:
                        total = total + weights[slot, z] * before + weights[slot + 1, z] * after
                        total = total + lane_roll(weights[slot + 2, z] * value, 1)
                        total = total + lane_roll(weights[slot + 3, z] * value, -1)
                        vertical = slot + (5 if z == 0 else 4)
                        total = total + weights[vertical, 1 - z] * centre[c, 1 - z]
                        if c == 0:
                            total = total + weights[14, z] * centre[1, z]
                    else:
                        total = total + weights[slot, z] * after + weights[slot + 1, z] * before
                        total = total + weights[slot + 2, z] * lane_roll(value, -1)
                        total = total + weights[slot + 3, z] * lane_roll(value, 1)
                        vertical = slot + (4 if z == 0 else 5)
                        total = total + weights[vertical, z] * centre[c, 1 - z]
                        if c == 1:
                            total = total + weights[14, z] * centre[0, z]
                    target[base + (c * 2 + z), s + shift : s + shift + 8, :] = total
            return carry

        lax.fori_loop(0, groups, body, 0, unroll=min(unroll, groups))


def fill(outer, own, x_first, x_second, half, offset, has_low, has_high, even):
    outer[:, 8:16, :] = own[:, 0:8, :]
    outer[:, 16:24, :] = own[:, ROWS - 8 : ROWS, :]
    for here, there, row, has in ((x_second, x_first, 4, has_low), (x_first, x_second, 24, has_high)):
        side = jnp.where(even, here[offset : offset + half], there[offset : offset + half]) * has
        outer[:half, row : row + 4, :] = side[:, 0:4, :]
        outer[half:, row : row + 4, :] = side[:, 4:8, :]


def put_tile(ref, index, tile, value):
    if tile < 4:
        ref[index, 8 + 8 * tile : 16 + 8 * tile, :] = value
    else:
        ref[index, 4:8, :] = value[0:4]
        ref[index, 40:44, :] = value[4:8]


def gram_of(block, contract):
    return lax.dot_general(
        block,
        block,
        (((contract,), (contract,)), ((), ())),
        precision=lax.Precision.HIGHEST,
        preferred_element_type=F32,
    )


def outer_kernel(
    p_ref, c_ref, x_first_ref, x_second_ref, inner_ref, main_ref, gram_ref, strip_ref, cstrip_ref, first, second, coef, result
):
    has_low, has_high = inside(ACROSS)
    even = is_even(ACROSS)
    fill(first, p_ref, x_first_ref, x_second_ref, PLANES // 2, 0, has_low, has_high, even)
    fill(coef, c_ref, x_first_ref, x_second_ref, COEFS // 2, PLANES // 2, has_low, has_high, even)
    lane = iota((8, 128), 1)
    upper = iota((8, 128), 0) < 4

    def halo(ref, index):
        return jnp.where(upper, ref[index, 4:12, :], ref[index, 20:28, :])

    for tile in range(5):
        rows = slice(8 * tile, 8 * tile + 8)
        load = (lambda i: p_ref[i, rows, :]) if tile < 4 else (lambda i: halo(first, i))
        for index, strip in enumerate(own_strips(gather_columns(load, 16, lane), lane)):
            strip_ref[index, rows, :] = strip
    halos = jnp.concatenate([halo(coef, index) for index in range(COEFS)], axis=0)
    cstrip_ref[:, 32:40, :] = make_cstrips(halos).reshape(COEFS, 8, 128)
    cstrip_ref[:, 0:32, :] = make_cstrips(c_ref[...].reshape(COEFS * ROWS, 128)).reshape(COEFS, ROWS, 128)
    step(first, second, coef, 16, OUTER_STARTS[0], False)
    step(second, first, coef, 16, OUTER_STARTS[1], False)
    step(first, second, coef, 16, OUTER_STARTS[2], True)
    step(second, result, coef, 16, OUTER_STARTS[3], True, -8)
    known = (lane >= 4) & (lane < 124)
    blocks = []
    for part in range(4):
        for row in range(0, ROWS, 8):
            block = []
            for p in range(16):
                plane = p * 4 + part
                value = inner_ref[plane, row : row + 8, :]
                if row == 0:
                    value = jnp.where(upper, result[plane, 0:8, :], value)
                elif row == ROWS - 8:
                    value = jnp.where(upper, value, result[plane, 8:16, :])
                main_ref[plane, row : row + 8, :] = value
                block.append(jnp.where(known, value, 0.0))
            blocks.append(jnp.concatenate(block, axis=0))
    high = [block.astype(jnp.bfloat16) for block in blocks]
    low = [(block - part.astype(F32)).astype(jnp.bfloat16) for block, part in zip(blocks, high)]
    high, low = jnp.concatenate(high, axis=1), jnp.concatenate(low, axis=1)
    product = lambda a, b: lax.dot_general(a, b, (((1,), (1,)), ((), ())), preferred_element_type=F32)
    mixed = product(high, low)
    gram_ref[...] = product(high, high) + product(low, low) + (mixed + mixed.T)


def edge_kernel(
    main_ref,
    partial_ref,
    strip_ref,
    cstrip_ref,
    y_first_ref,
    y_second_ref,
    out_hbm,
    gram_ref,
    first,
    second,
    coef,
    result,
    out_ref,
    sem,
):
    lane = iota((8, 128), 1)
    group, offset = lane // 32, lane % 32
    is_halo = (offset >= 8) & (offset < 16)
    has_left, has_right = inside("z")
    even = is_even("z")

    def own(ref, index, tile):
        return ref[index, 8 * tile : 8 * tile + 8, :]

    def columns(part, tile):
        index = part * 5 + tile
        y_first, y_second = y_first_ref[index], y_second_ref[index]
        left, right = jnp.where(even, y_second, y_first), jnp.where(even, y_first, y_second)
        return halo_columns(left * has_left, right * has_right, lane)

    for z in range(2):
        for tile in range(5):
            halos = columns(z, tile)
            for t in range(4):
                for c in range(2):
                    index = t * 4 + c * 2 + z
                    value = own(strip_ref, index, tile)
                    put_tile(first, index, tile, jnp.where(is_halo, lane_roll(halos[c], 8 - 8 * t), value))
    for tile in range(5):
        halos = columns(2, tile)
        for half in range(2):
            rolled = [lane_roll(halos[half], 8 * k) for k in range(16)]
            for k in range(16 if half == 0 else COEFS - 16):
                index = half * 16 + k
                spread = rolled[(1 - k) % 16]
                for q in range(1, 4):
                    spread = jnp.where(group == q, rolled[(4 * q + 1 - k) % 16], spread)
                value = own(cstrip_ref, index, tile)
                put_tile(coef, index, tile, jnp.where(is_halo, spread, value))
    step(first, second, coef, 4, STRIP_STARTS[0], False)
    step(second, first, coef, 4, STRIP_STARTS[1], False)
    step(first, second, coef, 4, STRIP_STARTS[2], True)
    step(second, result, coef, 4, STRIP_STARTS[3], True, -8)

    blocks = []
    for part in range(4):
        for row in range(0, ROWS, 8):
            packed = None
            for t in range(4):
                value = result[t * 4 + part, row : row + 8, :]
                value = jnp.where(lane % 8 < 4, lane_roll(value, 8 * t - 4), lane_roll(value, 8 * t - 12))
                packed = value if packed is None else jnp.where(offset // 8 == t, value, packed)
            blocks.append(packed)
    is_edge = (lane < 4) | (lane >= 124)
    for i, packed in enumerate(blocks):
        part, row = i // 4, i % 4 * 8
        for p in range(16):
            plane = p * 4 + part
            value = main_ref[plane, row : row + 8, :]
            out_ref[plane, row : row + 8, :] = jnp.where(is_edge, lane_roll(packed, 124 - 8 * p), value)
    copy = pltpu.make_async_copy(out_ref, out_hbm, sem)
    copy.start()

    gram = partial_ref[...] + gram_of(jnp.concatenate(blocks, axis=0), 0)
    same = iota((128, 128), 0) % 8 == iota((128, 128), 1) % 8
    folded = jnp.where(same, gram, 0.0).reshape(16, 8, 128).sum(axis=1)
    select = (iota((128, 128), 0) // 8 == iota((128, 128), 1) % 16).astype(F32)
    spread = jnp.dot(folded, select, precision=lax.Precision.HIGHEST, preferred_element_type=F32)
    mine = iota((16, 128), 1) // 16 == iota((16, 128), 0) % 8
    tile = jnp.where(mine, spread, 0.0).reshape(2, 8, 128).sum(axis=1)
    gram_ref[...] = jnp.broadcast_to(tile[None], gram_ref.shape)
    copy.wait()


def cholesky_kernel(scale, in_ref, out_ref):
    tile = jnp.sum(in_ref[...], axis=0) * scale
    row, col = iota((16, 128), 0), iota((16, 128), 1)
    work = jnp.concatenate([jnp.broadcast_to(tile[i : i + 1], (8, 128)) for i in range(2)], axis=0)
    work = jnp.where(col // 16 == row % 8, work, 0.0)
    for shift in (64, 32, 16):
        work = work + lane_roll(work, shift)
    work = jnp.where(col < 16, work, 0.0)
    columns = [jnp.broadcast_to(work[:, j : j + 1], (16, 128)) for j in range(16)]
    for k in range(16):
        pivot = columns[k][k : k + 1, :]
        if k < 15:
            scaled = jnp.where(row > k, columns[k] / pivot, 0.0)
            for j in range(k + 1, 16):
                columns[j] = columns[j] - scaled * columns[j][k : k + 1, :]
    factor = jnp.zeros((16, 128), F32)
    for k in range(16):
        factor = jnp.where(col == k, columns[k], factor)
    diagonal = jnp.sum(jnp.where(row == col, factor, 0.0), axis=1, keepdims=True)
    factor = jnp.where(col >= row, factor / jnp.sqrt(diagonal), 0.0)
    out_ref[...] = factor[:, :16]


def shape(*dims):
    return jax.ShapeDtypeStruct(dims, F32)


VMEM = pl.BlockSpec(memory_space=pltpu.VMEM)
ANY = pl.BlockSpec(memory_space=pl.ANY)


def call(kernel, name, inputs, outputs, scratch=(), in_specs=None, out_specs=None, flops=1_000_000, vmem=32):
    moved = 4 * sum(math.prod(a.shape) for a in (*inputs, *outputs))
    return pl.pallas_call(
        kernel,
        in_specs=in_specs or [VMEM] * len(inputs),
        out_specs=out_specs or [VMEM] * len(outputs),
        out_shape=list(outputs),
        scratch_shapes=list(scratch),
        compiler_params=pltpu.CompilerParams(vmem_limit_bytes=vmem << 20),
        cost_estimate=pl.CostEstimate(flops=flops, bytes_accessed=moved, transcendentals=0),
        name=name,
    )(*inputs)


def exchange(first, second, axes):
    count = lax.axis_size(axes)
    inner = [(i, i ^ 1) for i in range(count)]
    outer = [(i, (((i + 1) ^ 1) - 1) % count) for i in range(count)]
    return lax.ppermute(first, axes, inner), lax.ppermute(second, axes, outer)


def local(probes, coefficients):
    planes = probes.reshape(PLANES, ROWS, 128)
    weights = coefficients.reshape(COEFS, ROWS, 128)
    scratch = lambda *dims: pltpu.VMEM(dims, F32)
    x_first, x_second = call(
        pack_rows_kernel,
        "pack_rows",
        [pltpu.with_memory_space_constraint(array, pltpu.HBM) for array in (planes, weights)],
        [pltpu.VMEM((PAIRS, 8, 128), F32)] * 2,
        [scratch(PLANES, 8, 128)] * 2 + [scratch(COEFS, 8, 128)] * 2 + [pltpu.SemaphoreType.DMA((4,))],
        in_specs=[pl.BlockSpec(memory_space=pltpu.HBM)] * 2,
    )
    x_first, x_second = exchange(x_first, x_second, ACROSS)

    inner, own_left, own_right = call(
        inner_kernel,
        "inner",
        (planes, weights),
        [
            shape(PLANES, ROWS, 128),
            shape(15, 8, 128),
            shape(15, 8, 128),
        ],
        [scratch(PLANES, ROWS, 128)] * 2,
        flops=15_000_000,
    )
    y_first, y_second = call(
        halo_kernel, "halo", (x_first, x_second, own_left, own_right), [shape(15, 8, 128)] * 2
    )
    y_first, y_second = exchange(y_first, y_second, "z")

    main, partial, strip, cstrip = call(
        outer_kernel,
        "outer",
        (planes, weights, x_first, x_second, inner),
        [shape(PLANES, ROWS, 128), shape(128, 128), shape(16, 40, 128), shape(COEFS, 40, 128)],
        [scratch(PLANES, 32, 128)] * 2 + [scratch(COEFS, 32, 128), scratch(PLANES, 16, 128)],
        flops=10_000_000,
    )
    sketch, gram = call(
        edge_kernel,
        "edge",
        (main, partial, strip, cstrip, y_first, y_second),
        [shape(PLANES, ROWS, 128), shape(16, 2, 128)],
        [
            scratch(16, EXT, 128),
            scratch(16, EXT, 128),
            scratch(COEFS, EXT, 128),
            scratch(16, ROWS, 128),
            scratch(PLANES, ROWS, 128),
            pltpu.SemaphoreType.DMA,
        ],
        out_specs=[ANY, VMEM],
    )

    gathered = lax.all_to_all(gram, ("core", "z"), 0, 0, tiled=True)
    gram = jnp.broadcast_to(gathered.sum(axis=0)[None], (16, 2, 128))
    gathered = lax.all_to_all(gram, ("x", "y"), 0, 0, tiled=True)
    total_rows = PLANES // 16 * ROWS * 128 * lax.axis_size(ACROSS + ("z",))
    (factor,) = call(
        lambda *refs: cholesky_kernel(1.0 / total_rows, *refs), "cholesky", (gathered,), [shape(16, 16)]
    )
    return sketch.reshape(probes.shape), factor


def solution(mesh):
    fine = Mesh(mesh.devices.reshape(4, 4, 2, 8), ("x", "y", "core", "z"))
    placed = (P(None, None, None, ACROSS, "z"), P(None, None, ACROSS, "z"))
    return jax.shard_map(
        local,
        mesh=fine,
        in_specs=placed,
        out_specs=(P(None, None, None, ACROSS, "z"), P()),
        check_vma=False,
    )
```

```python
import math

import jax
import jax.numpy as jnp
from jax import lax
from jax.experimental import pallas as pl
from jax.experimental.pallas import tpu as pltpu
from jax.sharding import Mesh, PartitionSpec as P

PLANES = 64
COEFS = 30
PAIRS = (PLANES + COEFS) // 2
ROWS = 32
EXT = 48
STRIP_STARTS = ((5, 13, 21, 29, 35), (6, 14, 22, 30, 34), (7, 15, 23, 31, 33), (8, 16, 24, 32))
INNER_STARTS = ((1, 9, 17, 23), (2, 10, 18, 22), (3, 11, 19, 21), (4, 12, 20))
OUTER_STARTS = ((5, 13, 19), (6, 18), (7, 17), (8, 16))
ACROSS = ("x", "y", "core")
F32 = jnp.float32


def iota(shape, dim):
    return lax.broadcasted_iota(jnp.int32, shape, dim)


def lane_roll(array, shift):
    shift = shift % 128
    return array if shift == 0 else pltpu.roll(array, shift, array.ndim - 1)


def half_roll(array):
    return pltpu.roll(array, 4, array.ndim - 2)


def is_even(axes):
    return lax.rem(lax.axis_index(axes), 2) == 0


def pack_rows_kernel(p_hbm, c_hbm, first_ref, second_ref, p_top, p_bottom, c_top, c_bottom, sems):
    sources = (p_hbm.at[:, 0:8], p_hbm.at[:, ROWS - 8 : ROWS], c_hbm.at[:, 0:8], c_hbm.at[:, ROWS - 8 : ROWS])
    targets = (p_top, p_bottom, c_top, c_bottom)
    copies = [pltpu.make_async_copy(src, dst, sems.at[i]) for i, (src, dst) in enumerate(zip(sources, targets))]
    for copy in copies:
        copy.start()
    even = is_even(ACROSS)
    for copy in copies:
        copy.wait()
    for first, last, offset, half in (
        (p_top, p_bottom, 0, PLANES // 2),
        (c_top, c_bottom, PLANES // 2, COEFS // 2),
    ):
        upper = iota((half, 8, 128), 1) < 4
        low = jnp.where(upper, first[:half], half_roll(first[half:]))
        high = jnp.where(upper, half_roll(last[:half]), last[half:])
        first_ref[offset : offset + half] = jnp.where(even, high, low)
        second_ref[offset : offset + half] = jnp.where(even, low, high)


def inside(axes):
    index = lax.axis_index(axes)
    last = lax.axis_size(axes) - 1
    return jnp.where(index > 0, 1.0, 0.0).astype(F32), jnp.where(index < last, 1.0, 0.0).astype(F32)


def pack_columns(values, lane):
    both = []
    for planes in (values[:16], values[16:]):
        packed = None
        for k, value in enumerate(planes):
            value = lane_roll(value, 8 * k + 4)
            packed = value if packed is None else jnp.where(lane // 8 == k, value, packed)
        both.append(packed)
    return split_columns(both, lane)


def halo_columns(left, right, lane):
    first = lane % 8 < 4
    return jnp.where(first, right, lane_roll(left, 4)), jnp.where(first, lane_roll(right, -4), left)


def gather_columns(load, count, lane):
    group = lane // 32
    gathered = []
    for index in range(count):
        total = lane_roll(load(index), 8)
        for q in range(1, 4):
            total = jnp.where(group == q, lane_roll(load(index + q * 16), q * 32 + 8), total)
        gathered.append(total)
    return gathered


def own_strips(gathered, lane):
    return [jnp.where(lane % 32 < 8, total, lane_roll(total, 8)) for total in gathered]


def split_columns(both, lane):
    first = lane % 8 < 4
    return jnp.where(first, lane_roll(both[0], -4), both[1]), jnp.where(first, both[0], lane_roll(both[1], 4))


def make_cstrips(values):
    source, target = iota((128, 128), 0), iota((128, 128), 1) % 32
    wanted = jnp.where(target < 8, target + 120, jnp.where((target >= 16) & (target < 24), target - 16, -1))
    select = (source == wanted).astype(jnp.bfloat16)
    total = None
    for _ in range(3):
        part = values.astype(jnp.bfloat16)
        values = values - part.astype(F32)
        moved = jnp.dot(part, select, preferred_element_type=F32)
        total = moved if total is None else total + moved
    return total


def inner_kernel(p_ref, c_ref, main_ref, left_ref, right_ref, first, second):
    lane = iota((8, 128), 1)
    for tile in range(4):
        rows = slice(8 * tile, 8 * tile + 8)
        for z in range(2):
            planes = [p_ref[p * 4 + c * 2 + z, rows, :] for c in range(2) for p in range(16)]
            left_ref[z * 5 + tile], right_ref[z * 5 + tile] = pack_columns(planes, lane)
        planes = [c_ref[index, rows, :] for index in range(COEFS)]
        left_ref[10 + tile], right_ref[10 + tile] = pack_columns(planes, lane)
    step(p_ref, first, c_ref, 16, INNER_STARTS[0], False)
    step(first, second, c_ref, 16, INNER_STARTS[1], False)
    step(second, first, c_ref, 16, INNER_STARTS[2], True)
    step(first, main_ref, c_ref, 16, INNER_STARTS[3], True)


def halo_kernel(x_first_ref, x_second_ref, own_left_ref, own_right_ref, first_ref, second_ref):
    lane = iota((8, 128), 1)
    upper = iota((8, 128), 0) < 4
    has_low, has_high = inside(ACROSS)
    even, even_z = is_even(ACROSS), is_even("z")

    def put(index, left, right):
        first_ref[index] = jnp.where(even_z, right, left)
        second_ref[index] = jnp.where(even_z, left, right)

    halos = {}
    for offset, half in ((0, PLANES // 2), (PLANES // 2, COEFS // 2)):
        for k in range(half):
            x_first, x_second = x_first_ref[offset + k], x_second_ref[offset + k]
            low = jnp.where(even, x_second, x_first) * has_low
            high = jnp.where(even, x_first, x_second) * has_high
            halos[offset * 2 + k] = jnp.where(upper, low, half_roll(high))
            halos[offset * 2 + k + half] = jnp.where(upper, half_roll(low), high)
    for part in range(3):
        rows = slice(part * 5, part * 5 + 4)
        put(rows, own_left_ref[rows], own_right_ref[rows])
    for z in range(2):
        planes = [halos[p * 4 + c * 2 + z] for c in range(2) for p in range(16)]
        put(z * 5 + 4, *pack_columns(planes, lane))
    put(14, *pack_columns([halos[PLANES + i] for i in range(COEFS)], lane))


def step(source, target, coef, groups, starts, adjoint, shift=0, unroll=16):
    for s in starts:

        def weight(slot, z, move=0):
            return coef[slot * 2 + z, s + move : s + move + 8, :]

        up, down = (-1, 1) if adjoint else (0, 0)
        weights = {}
        for z in range(2):
            weights[14, z] = weight(14, z)
            for c in range(2):
                weights[c, z] = weight(c, z)
                slot = 2 + 6 * c
                weights[slot, z] = weight(slot, z, up)
                weights[slot + 1, z] = weight(slot + 1, z, down)
                weights[slot + 2, z] = weight(slot + 2, z)
                weights[slot + 3, z] = weight(slot + 3, z)
                vertical = slot + (4 if z == 0 else 5)
                weights[vertical, z] = weight(vertical, z)

        def body(group, carry):
            base = group * 4

            def field(c, z, move=0):
                return source[base + (c * 2 + z), s + move : s + move + 8, :]

            centre = {(c, z): field(c, z) for c in range(2) for z in range(2)}
            for c in range(2):
                for z in range(2):
                    value = centre[c, z]
                    slot = 2 + 6 * c
                    total = weights[c, z] * value
                    before, after = field(c, z, -1), field(c, z, 1)
                    if adjoint:
                        total = total + weights[slot, z] * before + weights[slot + 1, z] * after
                        total = total + lane_roll(weights[slot + 2, z] * value, 1)
                        total = total + lane_roll(weights[slot + 3, z] * value, -1)
                        vertical = slot + (5 if z == 0 else 4)
                        total = total + weights[vertical, 1 - z] * centre[c, 1 - z]
                        if c == 0:
                            total = total + weights[14, z] * centre[1, z]
                    else:
                        total = total + weights[slot, z] * after + weights[slot + 1, z] * before
                        total = total + weights[slot + 2, z] * lane_roll(value, -1)
                        total = total + weights[slot + 3, z] * lane_roll(value, 1)
                        vertical = slot + (4 if z == 0 else 5)
                        total = total + weights[vertical, z] * centre[c, 1 - z]
                        if c == 1:
                            total = total + weights[14, z] * centre[0, z]
                    target[base + (c * 2 + z), s + shift : s + shift + 8, :] = total
            return carry

        lax.fori_loop(0, groups, body, 0, unroll=min(unroll, groups))


def fill(outer, own, x_first, x_second, half, offset, has_low, has_high, even):
    outer[:, 8:16, :] = own[:, 0:8, :]
    outer[:, 16:24, :] = own[:, ROWS - 8 : ROWS, :]
    for here, there, row, has in ((x_second, x_first, 4, has_low), (x_first, x_second, 24, has_high)):
        side = jnp.where(even, here[offset : offset + half], there[offset : offset + half]) * has
        outer[:half, row : row + 4, :] = side[:, 0:4, :]
        outer[half:, row : row + 4, :] = side[:, 4:8, :]


def put_tile(ref, index, tile, value):
    if tile < 4:
        ref[index, 8 + 8 * tile : 16 + 8 * tile, :] = value
    else:
        ref[index, 4:8, :] = value[0:4]
        ref[index, 40:44, :] = value[4:8]


def gram_of(block, contract):
    return lax.dot_general(
        block,
        block,
        (((contract,), (contract,)), ((), ())),
        precision=lax.Precision.HIGHEST,
        preferred_element_type=F32,
    )


def outer_kernel(
    p_ref, c_ref, x_first_ref, x_second_ref, inner_ref, main_ref, gram_ref, strip_ref, cstrip_ref, first, second, coef, result
):
    has_low, has_high = inside(ACROSS)
    even = is_even(ACROSS)
    fill(first, p_ref, x_first_ref, x_second_ref, PLANES // 2, 0, has_low, has_high, even)
    fill(coef, c_ref, x_first_ref, x_second_ref, COEFS // 2, PLANES // 2, has_low, has_high, even)
    lane = iota((8, 128), 1)
    upper = iota((8, 128), 0) < 4

    def halo(ref, index):
        return jnp.where(upper, ref[index, 4:12, :], ref[index, 20:28, :])

    for tile in range(5):
        rows = slice(8 * tile, 8 * tile + 8)
        load = (lambda i: p_ref[i, rows, :]) if tile < 4 else (lambda i: halo(first, i))
        for index, strip in enumerate(own_strips(gather_columns(load, 16, lane), lane)):
            strip_ref[index, rows, :] = strip
    halos = jnp.concatenate([halo(coef, index) for index in range(COEFS)], axis=0)
    cstrip_ref[:, 32:40, :] = make_cstrips(halos).reshape(COEFS, 8, 128)
    cstrip_ref[:, 0:32, :] = make_cstrips(c_ref[...].reshape(COEFS * ROWS, 128)).reshape(COEFS, ROWS, 128)
    step(first, second, coef, 16, OUTER_STARTS[0], False)
    step(second, first, coef, 16, OUTER_STARTS[1], False)
    step(first, second, coef, 16, OUTER_STARTS[2], True)
    step(second, result, coef, 16, OUTER_STARTS[3], True, -8)
    known = (lane >= 4) & (lane < 124)
    blocks = []
    for part in range(4):
        for row in range(0, ROWS, 8):
            block = []
            for p in range(16):
                plane = p * 4 + part
                value = inner_ref[plane, row : row + 8, :]
                if row == 0:
                    value = jnp.where(upper, result[plane, 0:8, :], value)
                elif row == ROWS - 8:
                    value = jnp.where(upper, value, result[plane, 8:16, :])
                main_ref[plane, row : row + 8, :] = value
                block.append(jnp.where(known, value, 0.0))
            blocks.append(jnp.concatenate(block, axis=0))
    high = [block.astype(jnp.bfloat16) for block in blocks]
    low = [(block - part.astype(F32)).astype(jnp.bfloat16) for block, part in zip(blocks, high)]
    high, low = jnp.concatenate(high, axis=1), jnp.concatenate(low, axis=1)
    product = lambda a, b: lax.dot_general(a, b, (((1,), (1,)), ((), ())), preferred_element_type=F32)
    mixed = product(high, low)
    gram_ref[...] = product(high, high) + product(low, low) + (mixed + mixed.T)


def edge_kernel(
    main_ref,
    partial_ref,
    strip_ref,
    cstrip_ref,
    y_first_ref,
    y_second_ref,
    out_ref,
    gram_ref,
    first,
    second,
    coef,
    result,
):
    lane = iota((8, 128), 1)
    group, offset = lane // 32, lane % 32
    is_halo = (offset >= 8) & (offset < 16)
    has_left, has_right = inside("z")
    even = is_even("z")

    def own(ref, index, tile):
        return ref[index, 8 * tile : 8 * tile + 8, :]

    def columns(part, tile):
        index = part * 5 + tile
        y_first, y_second = y_first_ref[index], y_second_ref[index]
        left, right = jnp.where(even, y_second, y_first), jnp.where(even, y_first, y_second)
        return halo_columns(left * has_left, right * has_right, lane)

    for z in range(2):
        for tile in range(5):
            halos = columns(z, tile)
            for t in range(4):
                for c in range(2):
                    index = t * 4 + c * 2 + z
                    value = own(strip_ref, index, tile)
                    put_tile(first, index, tile, jnp.where(is_halo, lane_roll(halos[c], 8 - 8 * t), value))
    for tile in range(5):
        halos = columns(2, tile)
        for half in range(2):
            rolled = [lane_roll(halos[half], 8 * k) for k in range(16)]
            for k in range(16 if half == 0 else COEFS - 16):
                index = half * 16 + k
                spread = rolled[(1 - k) % 16]
                for q in range(1, 4):
                    spread = jnp.where(group == q, rolled[(4 * q + 1 - k) % 16], spread)
                value = own(cstrip_ref, index, tile)
                put_tile(coef, index, tile, jnp.where(is_halo, spread, value))
    step(first, second, coef, 4, STRIP_STARTS[0], False)
    step(second, first, coef, 4, STRIP_STARTS[1], False)
    step(first, second, coef, 4, STRIP_STARTS[2], True)
    step(second, result, coef, 4, STRIP_STARTS[3], True, -8)

    blocks = []
    for part in range(4):
        for row in range(0, ROWS, 8):
            packed = None
            for t in range(4):
                value = result[t * 4 + part, row : row + 8, :]
                value = jnp.where(lane % 8 < 4, lane_roll(value, 8 * t - 4), lane_roll(value, 8 * t - 12))
                packed = value if packed is None else jnp.where(offset // 8 == t, value, packed)
            blocks.append(packed)
    is_edge = (lane < 4) | (lane >= 124)
    for i, packed in enumerate(blocks):
        part, row = i // 4, i % 4 * 8
        for p in range(16):
            plane = p * 4 + part
            value = main_ref[plane, row : row + 8, :]
            out_ref[plane, row : row + 8, :] = jnp.where(is_edge, lane_roll(packed, 124 - 8 * p), value)

    gram = partial_ref[...] + gram_of(jnp.concatenate(blocks, axis=0), 0)
    same = iota((128, 128), 0) % 8 == iota((128, 128), 1) % 8
    folded = jnp.where(same, gram, 0.0).reshape(16, 8, 128).sum(axis=1)
    select = (iota((128, 128), 0) // 8 == iota((128, 128), 1) % 16).astype(F32)
    spread = jnp.dot(folded, select, precision=lax.Precision.HIGHEST, preferred_element_type=F32)
    mine = iota((16, 128), 1) // 16 == iota((16, 128), 0) % 8
    tile = jnp.where(mine, spread, 0.0).reshape(2, 8, 128).sum(axis=1)
    gram_ref[...] = jnp.broadcast_to(tile[None], gram_ref.shape)


def cholesky_kernel(scale, in_ref, out_ref):
    tile = jnp.sum(in_ref[...], axis=0) * scale
    row, col = iota((16, 128), 0), iota((16, 128), 1)
    work = jnp.concatenate([jnp.broadcast_to(tile[i : i + 1], (8, 128)) for i in range(2)], axis=0)
    work = jnp.where(col // 16 == row % 8, work, 0.0)
    for shift in (64, 32, 16):
        work = work + lane_roll(work, shift)
    work = jnp.where(col < 16, work, 0.0)
    columns = [jnp.broadcast_to(work[:, j : j + 1], (16, 128)) for j in range(16)]
    for k in range(16):
        pivot = columns[k][k : k + 1, :]
        if k < 15:
            scaled = jnp.where(row > k, columns[k] / pivot, 0.0)
            for j in range(k + 1, 16):
                columns[j] = columns[j] - scaled * columns[j][k : k + 1, :]
    factor = jnp.zeros((16, 128), F32)
    for k in range(16):
        factor = jnp.where(col == k, columns[k], factor)
    diagonal = jnp.sum(jnp.where(row == col, factor, 0.0), axis=1, keepdims=True)
    factor = jnp.where(col >= row, factor / jnp.sqrt(diagonal), 0.0)
    out_ref[...] = factor[:, :16]


def shape(*dims):
    return jax.ShapeDtypeStruct(dims, F32)


VMEM = pl.BlockSpec(memory_space=pltpu.VMEM)
ANY = pl.BlockSpec(memory_space=pl.ANY)


def call(kernel, name, inputs, outputs, scratch=(), in_specs=None, out_specs=None, flops=1_000_000, vmem=32):
    moved = 4 * sum(math.prod(a.shape) for a in (*inputs, *outputs))
    return pl.pallas_call(
        kernel,
        in_specs=in_specs or [VMEM] * len(inputs),
        out_specs=out_specs or [VMEM] * len(outputs),
        out_shape=list(outputs),
        scratch_shapes=list(scratch),
        compiler_params=pltpu.CompilerParams(vmem_limit_bytes=vmem << 20),
        cost_estimate=pl.CostEstimate(flops=flops, bytes_accessed=moved, transcendentals=0),
        name=name,
    )(*inputs)


def exchange(first, second, axes):
    count = lax.axis_size(axes)
    inner = [(i, i ^ 1) for i in range(count)]
    outer = [(i, (((i + 1) ^ 1) - 1) % count) for i in range(count)]
    return lax.ppermute(first, axes, inner), lax.ppermute(second, axes, outer)


def local(probes, coefficients):
    planes = probes.reshape(PLANES, ROWS, 128)
    weights = coefficients.reshape(COEFS, ROWS, 128)
    scratch = lambda *dims: pltpu.VMEM(dims, F32)
    x_first, x_second = call(
        pack_rows_kernel,
        "pack_rows",
        [pltpu.with_memory_space_constraint(array, pltpu.HBM) for array in (planes, weights)],
        [pltpu.VMEM((PAIRS, 8, 128), F32)] * 2,
        [scratch(PLANES, 8, 128)] * 2 + [scratch(COEFS, 8, 128)] * 2 + [pltpu.SemaphoreType.DMA((4,))],
        in_specs=[pl.BlockSpec(memory_space=pltpu.HBM)] * 2,
    )
    x_first, x_second = exchange(x_first, x_second, ACROSS)

    inner, own_left, own_right = call(
        inner_kernel,
        "inner",
        (planes, weights),
        [
            shape(PLANES, ROWS, 128),
            shape(15, 8, 128),
            shape(15, 8, 128),
        ],
        [scratch(PLANES, ROWS, 128)] * 2,
        flops=15_000_000,
    )
    y_first, y_second = call(
        halo_kernel, "halo", (x_first, x_second, own_left, own_right), [shape(15, 8, 128)] * 2
    )
    y_first, y_second = exchange(y_first, y_second, "z")

    main, partial, strip, cstrip = call(
        outer_kernel,
        "outer",
        (planes, weights, x_first, x_second, inner),
        [shape(PLANES, ROWS, 128), shape(128, 128), shape(16, 40, 128), shape(COEFS, 40, 128)],
        [scratch(PLANES, 32, 128)] * 2 + [scratch(COEFS, 32, 128), scratch(PLANES, 16, 128)],
        flops=10_000_000,
    )
    sketch, gram = call(
        edge_kernel,
        "edge",
        (main, partial, strip, cstrip, y_first, y_second),
        [pltpu.VMEM((PLANES, ROWS, 128), F32), shape(16, 2, 128)],
        [
            scratch(16, EXT, 128),
            scratch(16, EXT, 128),
            scratch(COEFS, EXT, 128),
            scratch(16, ROWS, 128),
        ],
    )

    gathered = lax.all_to_all(gram, ("core", "z"), 0, 0, tiled=True)
    gram = jnp.broadcast_to(gathered.sum(axis=0)[None], (16, 2, 128))
    gathered = lax.all_to_all(gram, ("x", "y"), 0, 0, tiled=True)
    total_rows = PLANES // 16 * ROWS * 128 * lax.axis_size(ACROSS + ("z",))
    (factor,) = call(
        lambda *refs: cholesky_kernel(1.0 / total_rows, *refs), "cholesky", (gathered,), [shape(16, 16)]
    )
    return sketch.reshape(probes.shape), factor


def solution(mesh):
    fine = Mesh(mesh.devices.reshape(4, 4, 2, 8), ("x", "y", "core", "z"))
    placed = (P(None, None, None, ACROSS, "z"), P(None, None, ACROSS, "z"))
    return jax.shard_map(
        local,
        mesh=fine,
        in_specs=placed,
        out_specs=(P(None, None, None, ACROSS, "z"), P()),
        check_vma=False,
    )
```

```python
import math

import jax
import jax.numpy as jnp
from jax import lax
from jax.experimental import pallas as pl
from jax.experimental.pallas import tpu as pltpu
from jax.sharding import Mesh, PartitionSpec as P

PLANES = 64
COEFS = 30
PAIRS = (PLANES + COEFS) // 2
ROWS = 32
EXT = 48
STRIP_STARTS = ((5, 13, 21, 29, 35), (6, 14, 22, 30, 34), (7, 15, 23, 31, 33), (8, 16, 24, 32))
INNER_STARTS = ((1, 9, 17, 23), (2, 10, 18, 22), (3, 11, 19, 21), (4, 12, 20))
OUTER_STARTS = ((5, 13, 19), (6, 18), (7, 17), (8, 16))
ACROSS = ("x", "y", "core")
F32 = jnp.float32


def iota(shape, dim):
    return lax.broadcasted_iota(jnp.int32, shape, dim)


def lane_roll(array, shift):
    shift = shift % 128
    return array if shift == 0 else pltpu.roll(array, shift, array.ndim - 1)


def half_roll(array):
    return pltpu.roll(array, 4, array.ndim - 2)


def is_even(axes):
    return lax.rem(lax.axis_index(axes), 2) == 0


def pack_rows_kernel(p_hbm, c_hbm, first_ref, second_ref, p_top, p_bottom, c_top, c_bottom, sems):
    sources = (p_hbm.at[:, 0:8], p_hbm.at[:, ROWS - 8 : ROWS], c_hbm.at[:, 0:8], c_hbm.at[:, ROWS - 8 : ROWS])
    targets = (p_top, p_bottom, c_top, c_bottom)
    copies = [pltpu.make_async_copy(src, dst, sems.at[i]) for i, (src, dst) in enumerate(zip(sources, targets))]
    for copy in copies:
        copy.start()
    even = is_even(ACROSS)
    for copy in copies:
        copy.wait()
    for first, last, offset, half in (
        (p_top, p_bottom, 0, PLANES // 2),
        (c_top, c_bottom, PLANES // 2, COEFS // 2),
    ):
        upper = iota((half, 8, 128), 1) < 4
        low = jnp.where(upper, first[:half], half_roll(first[half:]))
        high = jnp.where(upper, half_roll(last[:half]), last[half:])
        first_ref[offset : offset + half] = jnp.where(even, high, low)
        second_ref[offset : offset + half] = jnp.where(even, low, high)


def inside(axes):
    index = lax.axis_index(axes)
    last = lax.axis_size(axes) - 1
    return jnp.where(index > 0, 1.0, 0.0).astype(F32), jnp.where(index < last, 1.0, 0.0).astype(F32)


def pack_columns(values, lane):
    both = []
    for planes in (values[:16], values[16:]):
        packed = None
        for k, value in enumerate(planes):
            value = lane_roll(value, 8 * k + 4)
            packed = value if packed is None else jnp.where(lane // 8 == k, value, packed)
        both.append(packed)
    return split_columns(both, lane)


def halo_columns(left, right, lane):
    first = lane % 8 < 4
    return jnp.where(first, right, lane_roll(left, 4)), jnp.where(first, lane_roll(right, -4), left)


def gather_columns(load, count, lane):
    group = lane // 32
    gathered = []
    for index in range(count):
        total = lane_roll(load(index), 8)
        for q in range(1, 4):
            total = jnp.where(group == q, lane_roll(load(index + q * 16), q * 32 + 8), total)
        gathered.append(total)
    return gathered


def own_strips(gathered, lane):
    return [jnp.where(lane % 32 < 8, total, lane_roll(total, 8)) for total in gathered]


def split_columns(both, lane):
    first = lane % 8 < 4
    return jnp.where(first, lane_roll(both[0], -4), both[1]), jnp.where(first, both[0], lane_roll(both[1], 4))


def make_cstrips(values):
    source, target = iota((128, 128), 0), iota((128, 128), 1) % 32
    wanted = jnp.where(target < 8, target + 120, jnp.where((target >= 16) & (target < 24), target - 16, -1))
    select = (source == wanted).astype(jnp.bfloat16)
    total = None
    for _ in range(3):
        part = values.astype(jnp.bfloat16)
        values = values - part.astype(F32)
        moved = jnp.dot(part, select, preferred_element_type=F32)
        total = moved if total is None else total + moved
    return total


def inner_kernel(p_ref, c_ref, main_ref, left_ref, right_ref, first, second):
    lane = iota((8, 128), 1)
    for tile in range(4):
        rows = slice(8 * tile, 8 * tile + 8)
        for z in range(2):
            planes = [p_ref[p * 4 + c * 2 + z, rows, :] for c in range(2) for p in range(16)]
            left_ref[z * 5 + tile], right_ref[z * 5 + tile] = pack_columns(planes, lane)
        planes = [c_ref[index, rows, :] for index in range(COEFS)]
        left_ref[10 + tile], right_ref[10 + tile] = pack_columns(planes, lane)
    step(p_ref, first, c_ref, 16, INNER_STARTS[0], False)
    step(first, second, c_ref, 16, INNER_STARTS[1], False)
    step(second, first, c_ref, 16, INNER_STARTS[2], True)
    step(first, main_ref, c_ref, 16, INNER_STARTS[3], True)


def halo_kernel(x_first_ref, x_second_ref, own_left_ref, own_right_ref, first_ref, second_ref):
    lane = iota((8, 128), 1)
    upper = iota((8, 128), 0) < 4
    has_low, has_high = inside(ACROSS)
    even, even_z = is_even(ACROSS), is_even("z")

    def put(index, left, right):
        first_ref[index] = jnp.where(even_z, right, left)
        second_ref[index] = jnp.where(even_z, left, right)

    halos = {}
    for offset, half in ((0, PLANES // 2), (PLANES // 2, COEFS // 2)):
        for k in range(half):
            x_first, x_second = x_first_ref[offset + k], x_second_ref[offset + k]
            low = jnp.where(even, x_second, x_first) * has_low
            high = jnp.where(even, x_first, x_second) * has_high
            halos[offset * 2 + k] = jnp.where(upper, low, half_roll(high))
            halos[offset * 2 + k + half] = jnp.where(upper, half_roll(low), high)
    for part in range(3):
        rows = slice(part * 5, part * 5 + 4)
        put(rows, own_left_ref[rows], own_right_ref[rows])
    for z in range(2):
        planes = [halos[p * 4 + c * 2 + z] for c in range(2) for p in range(16)]
        put(z * 5 + 4, *pack_columns(planes, lane))
    put(14, *pack_columns([halos[PLANES + i] for i in range(COEFS)], lane))


def step(source, target, coef, groups, starts, adjoint, shift=0, unroll=16):
    for s in starts:

        def weight(slot, z, move=0):
            return coef[slot * 2 + z, s + move : s + move + 8, :]

        up, down = (-1, 1) if adjoint else (0, 0)
        weights = {}
        for z in range(2):
            weights[14, z] = weight(14, z)
            for c in range(2):
                weights[c, z] = weight(c, z)
                slot = 2 + 6 * c
                weights[slot, z] = weight(slot, z, up)
                weights[slot + 1, z] = weight(slot + 1, z, down)
                weights[slot + 2, z] = weight(slot + 2, z)
                weights[slot + 3, z] = weight(slot + 3, z)
                vertical = slot + (4 if z == 0 else 5)
                weights[vertical, z] = weight(vertical, z)

        def body(group, carry):
            base = group * 4

            def field(c, z, move=0):
                return source[base + (c * 2 + z), s + move : s + move + 8, :]

            centre = {(c, z): field(c, z) for c in range(2) for z in range(2)}
            for c in range(2):
                for z in range(2):
                    value = centre[c, z]
                    slot = 2 + 6 * c
                    total = weights[c, z] * value
                    before, after = field(c, z, -1), field(c, z, 1)
                    if adjoint:
                        total = total + weights[slot, z] * before + weights[slot + 1, z] * after
                        total = total + lane_roll(weights[slot + 2, z] * value, 1)
                        total = total + lane_roll(weights[slot + 3, z] * value, -1)
                        vertical = slot + (5 if z == 0 else 4)
                        total = total + weights[vertical, 1 - z] * centre[c, 1 - z]
                        if c == 0:
                            total = total + weights[14, z] * centre[1, z]
                    else:
                        total = total + weights[slot, z] * after + weights[slot + 1, z] * before
                        total = total + weights[slot + 2, z] * lane_roll(value, -1)
                        total = total + weights[slot + 3, z] * lane_roll(value, 1)
                        vertical = slot + (4 if z == 0 else 5)
                        total = total + weights[vertical, z] * centre[c, 1 - z]
                        if c == 1:
                            total = total + weights[14, z] * centre[0, z]
                    target[base + (c * 2 + z), s + shift : s + shift + 8, :] = total
            return carry

        lax.fori_loop(0, groups, body, 0, unroll=min(unroll, groups))


def fill(outer, own, x_first, x_second, half, offset, has_low, has_high, even):
    outer[:, 8:16, :] = own[:, 0:8, :]
    outer[:, 16:24, :] = own[:, ROWS - 8 : ROWS, :]
    for here, there, row, has in ((x_second, x_first, 4, has_low), (x_first, x_second, 24, has_high)):
        side = jnp.where(even, here[offset : offset + half], there[offset : offset + half]) * has
        outer[:half, row : row + 4, :] = side[:, 0:4, :]
        outer[half:, row : row + 4, :] = side[:, 4:8, :]


def put_tile(ref, index, tile, value):
    if tile < 4:
        ref[index, 8 + 8 * tile : 16 + 8 * tile, :] = value
    else:
        ref[index, 4:8, :] = value[0:4]
        ref[index, 40:44, :] = value[4:8]


def gram_of(block, contract):
    return lax.dot_general(
        block,
        block,
        (((contract,), (contract,)), ((), ())),
        precision=lax.Precision.HIGHEST,
        preferred_element_type=F32,
    )


def outer_kernel(
    p_ref, c_ref, x_first_ref, x_second_ref, inner_ref, main_ref, gram_ref, strip_ref, cstrip_ref, first, second, coef, result
):
    has_low, has_high = inside(ACROSS)
    even = is_even(ACROSS)
    fill(first, p_ref, x_first_ref, x_second_ref, PLANES // 2, 0, has_low, has_high, even)
    fill(coef, c_ref, x_first_ref, x_second_ref, COEFS // 2, PLANES // 2, has_low, has_high, even)
    lane = iota((8, 128), 1)
    upper = iota((8, 128), 0) < 4

    def halo(ref, index):
        return jnp.where(upper, ref[index, 4:12, :], ref[index, 20:28, :])

    for tile in range(5):
        rows = slice(8 * tile, 8 * tile + 8)
        load = (lambda i: p_ref[i, rows, :]) if tile < 4 else (lambda i: halo(first, i))
        for index, strip in enumerate(own_strips(gather_columns(load, 16, lane), lane)):
            strip_ref[index, rows, :] = strip
    halos = jnp.concatenate([halo(coef, index) for index in range(COEFS)], axis=0)
    cstrip_ref[:, 32:40, :] = make_cstrips(halos).reshape(COEFS, 8, 128)
    cstrip_ref[:, 0:32, :] = make_cstrips(c_ref[...].reshape(COEFS * ROWS, 128)).reshape(COEFS, ROWS, 128)
    step(first, second, coef, 16, OUTER_STARTS[0], False)
    step(second, first, coef, 16, OUTER_STARTS[1], False)
    step(first, second, coef, 16, OUTER_STARTS[2], True)
    step(second, result, coef, 16, OUTER_STARTS[3], True, -8)
    known = (lane >= 4) & (lane < 124)
    blocks = []
    for part in range(4):
        for row in range(0, ROWS, 8):
            block = []
            for p in range(16):
                plane = p * 4 + part
                value = inner_ref[plane, row : row + 8, :]
                if row == 0:
                    value = jnp.where(upper, result[plane, 0:8, :], value)
                elif row == ROWS - 8:
                    value = jnp.where(upper, value, result[plane, 8:16, :])
                main_ref[plane, row : row + 8, :] = value
                block.append(jnp.where(known, value, 0.0))
            blocks.append(jnp.concatenate(block, axis=0))
    high = [block.astype(jnp.bfloat16) for block in blocks]
    low = [(block - part.astype(F32)).astype(jnp.bfloat16) for block, part in zip(blocks, high)]
    high, low = jnp.concatenate(high, axis=1), jnp.concatenate(low, axis=1)
    product = lambda a, b: lax.dot_general(a, b, (((1,), (1,)), ((), ())), preferred_element_type=F32)
    mixed = product(high, low)
    gram_ref[...] = product(high, high) + product(low, low) + (mixed + mixed.T)


def edge_kernel(
    main_ref,
    partial_ref,
    strip_ref,
    cstrip_ref,
    y_first_ref,
    y_second_ref,
    out_ref,
    gram_ref,
    first,
    second,
    coef,
    result,
):
    lane = iota((8, 128), 1)
    group, offset = lane // 32, lane % 32
    is_halo = (offset >= 8) & (offset < 16)
    has_left, has_right = inside("z")
    even = is_even("z")

    def own(ref, index, tile):
        return ref[index, 8 * tile : 8 * tile + 8, :]

    def columns(part, tile):
        index = part * 5 + tile
        y_first, y_second = y_first_ref[index], y_second_ref[index]
        left, right = jnp.where(even, y_second, y_first), jnp.where(even, y_first, y_second)
        return halo_columns(left * has_left, right * has_right, lane)

    for z in range(2):
        for tile in range(5):
            halos = columns(z, tile)
            for t in range(4):
                for c in range(2):
                    index = t * 4 + c * 2 + z
                    value = own(strip_ref, index, tile)
                    put_tile(first, index, tile, jnp.where(is_halo, lane_roll(halos[c], 8 - 8 * t), value))
    for tile in range(5):
        halos = columns(2, tile)
        for half in range(2):
            rolled = [lane_roll(halos[half], 8 * k) for k in range(16)]
            for k in range(16 if half == 0 else COEFS - 16):
                index = half * 16 + k
                spread = rolled[(1 - k) % 16]
                for q in range(1, 4):
                    spread = jnp.where(group == q, rolled[(4 * q + 1 - k) % 16], spread)
                value = own(cstrip_ref, index, tile)
                put_tile(coef, index, tile, jnp.where(is_halo, spread, value))
    step(first, second, coef, 4, STRIP_STARTS[0], False)
    step(second, first, coef, 4, STRIP_STARTS[1], False)
    step(first, second, coef, 4, STRIP_STARTS[2], True)
    step(second, result, coef, 4, STRIP_STARTS[3], True, -8)

    blocks = []
    for part in range(4):
        for row in range(0, ROWS, 8):
            packed = None
            for t in range(4):
                value = result[t * 4 + part, row : row + 8, :]
                value = jnp.where(lane % 8 < 4, lane_roll(value, 8 * t - 4), lane_roll(value, 8 * t - 12))
                packed = value if packed is None else jnp.where(offset // 8 == t, value, packed)
            blocks.append(packed)
    is_edge = (lane < 4) | (lane >= 124)
    for i, packed in enumerate(blocks):
        part, row = i // 4, i % 4 * 8
        for p in range(16):
            plane = p * 4 + part
            value = main_ref[plane, row : row + 8, :]
            out_ref[plane, row : row + 8, :] = jnp.where(is_edge, lane_roll(packed, 124 - 8 * p), value)

    gram = partial_ref[...] + gram_of(jnp.concatenate(blocks, axis=0), 0)
    same = iota((128, 128), 0) % 8 == iota((128, 128), 1) % 8
    folded = jnp.where(same, gram, 0.0).reshape(16, 8, 128).sum(axis=1)
    select = (iota((128, 128), 0) // 8 == iota((128, 128), 1) % 16).astype(F32)
    spread = jnp.dot(folded, select, precision=lax.Precision.HIGHEST, preferred_element_type=F32)
    mine = iota((16, 128), 1) // 16 == iota((16, 128), 0) % 8
    tile = jnp.where(mine, spread, 0.0).reshape(2, 8, 128).sum(axis=1)
    gram_ref[...] = jnp.broadcast_to(tile[None], gram_ref.shape)


def finish_kernel(scale, in_ref, sketch_ref, out_ref, sketch_hbm, sem):
    copy = pltpu.make_async_copy(sketch_ref, sketch_hbm, sem)
    copy.start()
    tile = jnp.sum(in_ref[...], axis=0) * scale
    row, col = iota((16, 128), 0), iota((16, 128), 1)
    work = jnp.concatenate([jnp.broadcast_to(tile[i : i + 1], (8, 128)) for i in range(2)], axis=0)
    work = jnp.where(col // 16 == row % 8, work, 0.0)
    for shift in (64, 32, 16):
        work = work + lane_roll(work, shift)
    work = jnp.where(col < 16, work, 0.0)
    columns = [jnp.broadcast_to(work[:, j : j + 1], (16, 128)) for j in range(16)]
    for k in range(16):
        pivot = columns[k][k : k + 1, :]
        if k < 15:
            scaled = jnp.where(row > k, columns[k] / pivot, 0.0)
            for j in range(k + 1, 16):
                columns[j] = columns[j] - scaled * columns[j][k : k + 1, :]
    factor = jnp.zeros((16, 128), F32)
    for k in range(16):
        factor = jnp.where(col == k, columns[k], factor)
    diagonal = jnp.sum(jnp.where(row == col, factor, 0.0), axis=1, keepdims=True)
    factor = jnp.where(col >= row, factor / jnp.sqrt(diagonal), 0.0)
    out_ref[...] = factor[:, :16]
    copy.wait()


def shape(*dims):
    return jax.ShapeDtypeStruct(dims, F32)


VMEM = pl.BlockSpec(memory_space=pltpu.VMEM)
ANY = pl.BlockSpec(memory_space=pl.ANY)


def call(kernel, name, inputs, outputs, scratch=(), in_specs=None, out_specs=None, flops=1_000_000, vmem=32):
    moved = 4 * sum(math.prod(a.shape) for a in (*inputs, *outputs))
    return pl.pallas_call(
        kernel,
        in_specs=in_specs or [VMEM] * len(inputs),
        out_specs=out_specs or [VMEM] * len(outputs),
        out_shape=list(outputs),
        scratch_shapes=list(scratch),
        compiler_params=pltpu.CompilerParams(vmem_limit_bytes=vmem << 20),
        cost_estimate=pl.CostEstimate(flops=flops, bytes_accessed=moved, transcendentals=0),
        name=name,
    )(*inputs)


def exchange(first, second, axes):
    count = lax.axis_size(axes)
    inner = [(i, i ^ 1) for i in range(count)]
    outer = [(i, (((i + 1) ^ 1) - 1) % count) for i in range(count)]
    return lax.ppermute(first, axes, inner), lax.ppermute(second, axes, outer)


def local(probes, coefficients):
    planes = probes.reshape(PLANES, ROWS, 128)
    weights = coefficients.reshape(COEFS, ROWS, 128)
    scratch = lambda *dims: pltpu.VMEM(dims, F32)
    x_first, x_second = call(
        pack_rows_kernel,
        "pack_rows",
        [pltpu.with_memory_space_constraint(array, pltpu.HBM) for array in (planes, weights)],
        [pltpu.VMEM((PAIRS, 8, 128), F32)] * 2,
        [scratch(PLANES, 8, 128)] * 2 + [scratch(COEFS, 8, 128)] * 2 + [pltpu.SemaphoreType.DMA((4,))],
        in_specs=[pl.BlockSpec(memory_space=pltpu.HBM)] * 2,
    )
    x_first, x_second = exchange(x_first, x_second, ACROSS)

    inner, own_left, own_right = call(
        inner_kernel,
        "inner",
        (planes, weights),
        [
            shape(PLANES, ROWS, 128),
            shape(15, 8, 128),
            shape(15, 8, 128),
        ],
        [scratch(PLANES, ROWS, 128)] * 2,
        flops=15_000_000,
    )
    y_first, y_second = call(
        halo_kernel, "halo", (x_first, x_second, own_left, own_right), [shape(15, 8, 128)] * 2
    )
    y_first, y_second = exchange(y_first, y_second, "z")

    main, partial, strip, cstrip = call(
        outer_kernel,
        "outer",
        (planes, weights, x_first, x_second, inner),
        [shape(PLANES, ROWS, 128), shape(128, 128), shape(16, 40, 128), shape(COEFS, 40, 128)],
        [scratch(PLANES, 32, 128)] * 2 + [scratch(COEFS, 32, 128), scratch(PLANES, 16, 128)],
        flops=10_000_000,
    )
    sketch, gram = call(
        edge_kernel,
        "edge",
        (main, partial, strip, cstrip, y_first, y_second),
        [pltpu.VMEM((PLANES, ROWS, 128), F32), shape(16, 2, 128)],
        [
            scratch(16, EXT, 128),
            scratch(16, EXT, 128),
            scratch(COEFS, EXT, 128),
            scratch(16, ROWS, 128),
        ],
    )

    gathered = lax.all_to_all(gram, ("core", "z"), 0, 0, tiled=True)
    gram = jnp.broadcast_to(gathered.sum(axis=0)[None], (16, 2, 128))
    gathered = lax.all_to_all(gram, ("x", "y"), 0, 0, tiled=True)
    total_rows = PLANES // 16 * ROWS * 128 * lax.axis_size(ACROSS + ("z",))
    factor, sketch = call(
        lambda *refs: finish_kernel(1.0 / total_rows, *refs),
        "finish",
        (gathered, sketch),
        [shape(16, 16), shape(PLANES, ROWS, 128)],
        [pltpu.SemaphoreType.DMA],
        out_specs=[VMEM, ANY],
    )
    return sketch.reshape(probes.shape), factor


def solution(mesh):
    fine = Mesh(mesh.devices.reshape(4, 4, 2, 8), ("x", "y", "core", "z"))
    placed = (P(None, None, None, ACROSS, "z"), P(None, None, ACROSS, "z"))
    return jax.shard_map(
        local,
        mesh=fine,
        in_specs=placed,
        out_specs=(P(None, None, None, ACROSS, "z"), P()),
        check_vma=False,
    )
```

```python
import math

import jax
import jax.numpy as jnp
from jax import lax
from jax.experimental import pallas as pl
from jax.experimental.pallas import tpu as pltpu
from jax.sharding import Mesh, PartitionSpec as P

PLANES = 64
COEFS = 30
PAIRS = (PLANES + COEFS) // 2
ROWS = 32
EXT = 48
STRIP_STARTS = ((5, 13, 21, 29, 35), (6, 14, 22, 30, 34), (7, 15, 23, 31, 33), (8, 16, 24, 32))
INNER_STARTS = ((1, 9, 17, 23), (2, 10, 18, 22), (3, 11, 19, 21), (4, 12, 20))
OUTER_STARTS = ((5, 13, 19), (6, 18), (7, 17), (8, 16))
ACROSS = ("x", "y", "core")
F32 = jnp.float32


def iota(shape, dim):
    return lax.broadcasted_iota(jnp.int32, shape, dim)


def lane_roll(array, shift):
    shift = shift % 128
    return array if shift == 0 else pltpu.roll(array, shift, array.ndim - 1)


def half_roll(array):
    return pltpu.roll(array, 4, array.ndim - 2)


def is_even(axes):
    return lax.rem(lax.axis_index(axes), 2) == 0


def pack_rows_kernel(p_hbm, c_hbm, first_ref, second_ref, p_top, p_bottom, c_top, c_bottom, sems):
    sources = (p_hbm.at[:, 0:8], p_hbm.at[:, ROWS - 8 : ROWS], c_hbm.at[:, 0:8], c_hbm.at[:, ROWS - 8 : ROWS])
    targets = (p_top, p_bottom, c_top, c_bottom)
    copies = [pltpu.make_async_copy(src, dst, sems.at[i]) for i, (src, dst) in enumerate(zip(sources, targets))]
    for copy in copies:
        copy.start()
    even = is_even(ACROSS)
    for copy in copies:
        copy.wait()
    for first, last, offset, half in (
        (p_top, p_bottom, 0, PLANES // 2),
        (c_top, c_bottom, PLANES // 2, COEFS // 2),
    ):
        upper = iota((half, 8, 128), 1) < 4
        low = jnp.where(upper, first[:half], half_roll(first[half:]))
        high = jnp.where(upper, half_roll(last[:half]), last[half:])
        first_ref[offset : offset + half] = jnp.where(even, high, low)
        second_ref[offset : offset + half] = jnp.where(even, low, high)


def inside(axes):
    index = lax.axis_index(axes)
    last = lax.axis_size(axes) - 1
    return jnp.where(index > 0, 1.0, 0.0).astype(F32), jnp.where(index < last, 1.0, 0.0).astype(F32)


def pack_columns(values, lane):
    both = []
    for planes in (values[:16], values[16:]):
        packed = None
        for k, value in enumerate(planes):
            value = lane_roll(value, 8 * k + 4)
            packed = value if packed is None else jnp.where(lane // 8 == k, value, packed)
        both.append(packed)
    return split_columns(both, lane)


def halo_columns(left, right, lane):
    first = lane % 8 < 4
    return jnp.where(first, right, lane_roll(left, 4)), jnp.where(first, lane_roll(right, -4), left)


def gather_columns(load, count, lane):
    group = lane // 32
    gathered = []
    for index in range(count):
        total = lane_roll(load(index), 8)
        for q in range(1, 4):
            total = jnp.where(group == q, lane_roll(load(index + q * 16), q * 32 + 8), total)
        gathered.append(total)
    return gathered


def own_strips(gathered, lane):
    return [jnp.where(lane % 32 < 8, total, lane_roll(total, 8)) for total in gathered]


def split_columns(both, lane):
    first = lane % 8 < 4
    return jnp.where(first, lane_roll(both[0], -4), both[1]), jnp.where(first, both[0], lane_roll(both[1], 4))


def make_cstrips(values):
    source, target = iota((128, 128), 0), iota((128, 128), 1) % 32
    wanted = jnp.where(target < 8, target + 120, jnp.where((target >= 16) & (target < 24), target - 16, -1))
    select = (source == wanted).astype(jnp.bfloat16)
    total = None
    for _ in range(3):
        part = values.astype(jnp.bfloat16)
        values = values - part.astype(F32)
        moved = jnp.dot(part, select, preferred_element_type=F32)
        total = moved if total is None else total + moved
    return total


def inner_kernel(p_ref, c_ref, main_ref, left_ref, right_ref, first, second):
    lane = iota((8, 128), 1)
    for tile in range(4):
        rows = slice(8 * tile, 8 * tile + 8)
        for z in range(2):
            planes = [p_ref[p * 4 + c * 2 + z, rows, :] for c in range(2) for p in range(16)]
            left_ref[z * 5 + tile], right_ref[z * 5 + tile] = pack_columns(planes, lane)
        planes = [c_ref[index, rows, :] for index in range(COEFS)]
        left_ref[10 + tile], right_ref[10 + tile] = pack_columns(planes, lane)
    step(p_ref, first, c_ref, 16, INNER_STARTS[0], False)
    step(first, second, c_ref, 16, INNER_STARTS[1], False)
    step(second, first, c_ref, 16, INNER_STARTS[2], True)
    step(first, main_ref, c_ref, 16, INNER_STARTS[3], True)


def halo_kernel(x_first_ref, x_second_ref, own_left_ref, own_right_ref, first_ref, second_ref):
    lane = iota((8, 128), 1)
    upper = iota((8, 128), 0) < 4
    has_low, has_high = inside(ACROSS)
    even, even_z = is_even(ACROSS), is_even("z")

    def put(index, left, right):
        first_ref[index] = jnp.where(even_z, right, left)
        second_ref[index] = jnp.where(even_z, left, right)

    halos = {}
    for offset, half in ((0, PLANES // 2), (PLANES // 2, COEFS // 2)):
        for k in range(half):
            x_first, x_second = x_first_ref[offset + k], x_second_ref[offset + k]
            low = jnp.where(even, x_second, x_first) * has_low
            high = jnp.where(even, x_first, x_second) * has_high
            halos[offset * 2 + k] = jnp.where(upper, low, half_roll(high))
            halos[offset * 2 + k + half] = jnp.where(upper, half_roll(low), high)
    for part in range(3):
        rows = slice(part * 5, part * 5 + 4)
        put(rows, own_left_ref[rows], own_right_ref[rows])
    for z in range(2):
        planes = [halos[p * 4 + c * 2 + z] for c in range(2) for p in range(16)]
        put(z * 5 + 4, *pack_columns(planes, lane))
    put(14, *pack_columns([halos[PLANES + i] for i in range(COEFS)], lane))


def step(source, target, coef, groups, starts, adjoint, shift=0, unroll=16):
    for s in starts:

        def weight(slot, z, move=0):
            return coef[slot * 2 + z, s + move : s + move + 8, :]

        up, down = (-1, 1) if adjoint else (0, 0)
        weights = {}
        for z in range(2):
            weights[14, z] = weight(14, z)
            for c in range(2):
                weights[c, z] = weight(c, z)
                slot = 2 + 6 * c
                weights[slot, z] = weight(slot, z, up)
                weights[slot + 1, z] = weight(slot + 1, z, down)
                weights[slot + 2, z] = weight(slot + 2, z)
                weights[slot + 3, z] = weight(slot + 3, z)
                vertical = slot + (4 if z == 0 else 5)
                weights[vertical, z] = weight(vertical, z)

        def body(group, carry):
            base = group * 4

            def field(c, z, move=0):
                return source[base + (c * 2 + z), s + move : s + move + 8, :]

            centre = {(c, z): field(c, z) for c in range(2) for z in range(2)}
            for c in range(2):
                for z in range(2):
                    value = centre[c, z]
                    slot = 2 + 6 * c
                    total = weights[c, z] * value
                    before, after = field(c, z, -1), field(c, z, 1)
                    if adjoint:
                        total = total + weights[slot, z] * before + weights[slot + 1, z] * after
                        total = total + lane_roll(weights[slot + 2, z] * value, 1)
                        total = total + lane_roll(weights[slot + 3, z] * value, -1)
                        vertical = slot + (5 if z == 0 else 4)
                        total = total + weights[vertical, 1 - z] * centre[c, 1 - z]
                        if c == 0:
                            total = total + weights[14, z] * centre[1, z]
                    else:
                        total = total + weights[slot, z] * after + weights[slot + 1, z] * before
                        total = total + weights[slot + 2, z] * lane_roll(value, -1)
                        total = total + weights[slot + 3, z] * lane_roll(value, 1)
                        vertical = slot + (4 if z == 0 else 5)
                        total = total + weights[vertical, z] * centre[c, 1 - z]
                        if c == 1:
                            total = total + weights[14, z] * centre[0, z]
                    target[base + (c * 2 + z), s + shift : s + shift + 8, :] = total
            return carry

        lax.fori_loop(0, groups, body, 0, unroll=min(unroll, groups))


def fill(outer, own, x_first, x_second, half, offset, has_low, has_high, even):
    outer[:, 8:16, :] = own[:, 0:8, :]
    outer[:, 16:24, :] = own[:, ROWS - 8 : ROWS, :]
    for here, there, row, has in ((x_second, x_first, 4, has_low), (x_first, x_second, 24, has_high)):
        side = jnp.where(even, here[offset : offset + half], there[offset : offset + half]) * has
        outer[:half, row : row + 4, :] = side[:, 0:4, :]
        outer[half:, row : row + 4, :] = side[:, 4:8, :]


def put_tile(ref, index, tile, value):
    if tile < 4:
        ref[index, 8 + 8 * tile : 16 + 8 * tile, :] = value
    else:
        ref[index, 4:8, :] = value[0:4]
        ref[index, 40:44, :] = value[4:8]


def gram_of(block, contract):
    return lax.dot_general(
        block,
        block,
        (((contract,), (contract,)), ((), ())),
        precision=lax.Precision.HIGHEST,
        preferred_element_type=F32,
    )


def outer_kernel(
    p_ref, c_ref, x_first_ref, x_second_ref, inner_ref, main_ref, gram_ref, strip_ref, cstrip_ref, first, second, coef, result
):
    has_low, has_high = inside(ACROSS)
    even = is_even(ACROSS)
    fill(first, p_ref, x_first_ref, x_second_ref, PLANES // 2, 0, has_low, has_high, even)
    fill(coef, c_ref, x_first_ref, x_second_ref, COEFS // 2, PLANES // 2, has_low, has_high, even)
    lane = iota((8, 128), 1)
    upper = iota((8, 128), 0) < 4

    def halo(ref, index):
        return jnp.where(upper, ref[index, 4:12, :], ref[index, 20:28, :])

    for tile in range(5):
        rows = slice(8 * tile, 8 * tile + 8)
        load = (lambda i: p_ref[i, rows, :]) if tile < 4 else (lambda i: halo(first, i))
        for index, strip in enumerate(own_strips(gather_columns(load, 16, lane), lane)):
            strip_ref[index, rows, :] = strip
    halos = jnp.concatenate([halo(coef, index) for index in range(COEFS)], axis=0)
    cstrip_ref[:, 32:40, :] = make_cstrips(halos).reshape(COEFS, 8, 128)
    cstrip_ref[:, 0:32, :] = make_cstrips(c_ref[...].reshape(COEFS * ROWS, 128)).reshape(COEFS, ROWS, 128)
    step(first, second, coef, 16, OUTER_STARTS[0], False)
    step(second, first, coef, 16, OUTER_STARTS[1], False)
    step(first, second, coef, 16, OUTER_STARTS[2], True)
    step(second, result, coef, 16, OUTER_STARTS[3], True, -8)
    known = (lane >= 4) & (lane < 124)
    blocks = []
    for part in range(4):
        for row in range(0, ROWS, 8):
            block = []
            for p in range(16):
                plane = p * 4 + part
                value = inner_ref[plane, row : row + 8, :]
                if row == 0:
                    value = jnp.where(upper, result[plane, 0:8, :], value)
                elif row == ROWS - 8:
                    value = jnp.where(upper, value, result[plane, 8:16, :])
                main_ref[plane, row : row + 8, :] = value
                block.append(jnp.where(known, value, 0.0))
            blocks.append(jnp.concatenate(block, axis=0))
    high = [block.astype(jnp.bfloat16) for block in blocks]
    low = [(block - part.astype(F32)).astype(jnp.bfloat16) for block, part in zip(blocks, high)]
    high, low = jnp.concatenate(high, axis=1), jnp.concatenate(low, axis=1)
    product = lambda a, b: lax.dot_general(a, b, (((1,), (1,)), ((), ())), preferred_element_type=F32)
    mixed = product(high, low)
    gram_ref[...] = product(high, high) + product(low, low) + (mixed + mixed.T)


def edge_kernel(
    main_ref,
    partial_ref,
    strip_ref,
    cstrip_ref,
    y_first_ref,
    y_second_ref,
    out_hbm,
    late_ref,
    gram_ref,
    first,
    second,
    coef,
    result,
    early_ref,
    sems,
):
    lane = iota((8, 128), 1)
    group, offset = lane // 32, lane % 32
    is_halo = (offset >= 8) & (offset < 16)
    has_left, has_right = inside("z")
    even = is_even("z")

    def own(ref, index, tile):
        return ref[index, 8 * tile : 8 * tile + 8, :]

    def columns(part, tile):
        index = part * 5 + tile
        y_first, y_second = y_first_ref[index], y_second_ref[index]
        left, right = jnp.where(even, y_second, y_first), jnp.where(even, y_first, y_second)
        return halo_columns(left * has_left, right * has_right, lane)

    for z in range(2):
        for tile in range(5):
            halos = columns(z, tile)
            for t in range(4):
                for c in range(2):
                    index = t * 4 + c * 2 + z
                    value = own(strip_ref, index, tile)
                    put_tile(first, index, tile, jnp.where(is_halo, lane_roll(halos[c], 8 - 8 * t), value))
    for tile in range(5):
        halos = columns(2, tile)
        for half in range(2):
            rolled = [lane_roll(halos[half], 8 * k) for k in range(16)]
            for k in range(16 if half == 0 else COEFS - 16):
                index = half * 16 + k
                spread = rolled[(1 - k) % 16]
                for q in range(1, 4):
                    spread = jnp.where(group == q, rolled[(4 * q + 1 - k) % 16], spread)
                value = own(cstrip_ref, index, tile)
                put_tile(coef, index, tile, jnp.where(is_halo, spread, value))
    step(first, second, coef, 4, STRIP_STARTS[0], False)
    step(second, first, coef, 4, STRIP_STARTS[1], False)
    step(first, second, coef, 4, STRIP_STARTS[2], True)
    step(second, result, coef, 4, STRIP_STARTS[3], True, -8)

    is_edge = (lane < 4) | (lane >= 124)
    blocks, copies = [], []
    for part in range(4):
        for row in range(0, ROWS, 8):
            packed = None
            for t in range(4):
                value = result[t * 4 + part, row : row + 8, :]
                value = jnp.where(lane % 8 < 4, lane_roll(value, 8 * t - 4), lane_roll(value, 8 * t - 12))
                packed = value if packed is None else jnp.where(offset // 8 == t, value, packed)
            blocks.append(packed)
        merged = early_ref if part < 2 else late_ref
        for packed, row in zip(blocks[-4:], range(0, ROWS, 8)):
            for p in range(16):
                value = main_ref[p * 4 + part, row : row + 8, :]
                merged[p, part % 2, row : row + 8, :] = jnp.where(is_edge, lane_roll(packed, 124 - 8 * p), value)
        if part < 2:
            copies.append(pltpu.make_async_copy(early_ref.at[:, part], out_hbm.at[:, part], sems.at[part]))
            copies[-1].start()

    gram = partial_ref[...] + gram_of(jnp.concatenate(blocks, axis=0), 0)
    same = iota((128, 128), 0) % 8 == iota((128, 128), 1) % 8
    folded = jnp.where(same, gram, 0.0).reshape(16, 8, 128).sum(axis=1)
    select = (iota((128, 128), 0) // 8 == iota((128, 128), 1) % 16).astype(F32)
    spread = jnp.dot(folded, select, precision=lax.Precision.HIGHEST, preferred_element_type=F32)
    mine = iota((16, 128), 1) // 16 == iota((16, 128), 0) % 8
    tile = jnp.where(mine, spread, 0.0).reshape(2, 8, 128).sum(axis=1)
    gram_ref[...] = jnp.broadcast_to(tile[None], gram_ref.shape)
    for copy in copies:
        copy.wait()


def finish_kernel(scale, in_ref, late_ref, begun_hbm, out_ref, sketch_hbm, sem):
    copy = pltpu.make_async_copy(late_ref, sketch_hbm.at[:, 2:4], sem)
    copy.start()
    tile = jnp.sum(in_ref[...], axis=0) * scale
    row, col = iota((16, 128), 0), iota((16, 128), 1)
    work = jnp.concatenate([jnp.broadcast_to(tile[i : i + 1], (8, 128)) for i in range(2)], axis=0)
    work = jnp.where(col // 16 == row % 8, work, 0.0)
    for shift in (64, 32, 16):
        work = work + lane_roll(work, shift)
    work = jnp.where(col < 16, work, 0.0)
    columns = [jnp.broadcast_to(work[:, j : j + 1], (16, 128)) for j in range(16)]
    for k in range(16):
        pivot = columns[k][k : k + 1, :]
        if k < 15:
            scaled = jnp.where(row > k, columns[k] / pivot, 0.0)
            for j in range(k + 1, 16):
                columns[j] = columns[j] - scaled * columns[j][k : k + 1, :]
    factor = jnp.zeros((16, 128), F32)
    for k in range(16):
        factor = jnp.where(col == k, columns[k], factor)
    diagonal = jnp.sum(jnp.where(row == col, factor, 0.0), axis=1, keepdims=True)
    factor = jnp.where(col >= row, factor / jnp.sqrt(diagonal), 0.0)
    out_ref[...] = factor[:, :16]
    copy.wait()


def shape(*dims):
    return jax.ShapeDtypeStruct(dims, F32)


VMEM = pl.BlockSpec(memory_space=pltpu.VMEM)
ANY = pl.BlockSpec(memory_space=pl.ANY)


def call(kernel, name, inputs, outputs, scratch=(), in_specs=None, out_specs=None, flops=1_000_000, vmem=32, aliases=None):
    moved = 4 * sum(math.prod(a.shape) for a in (*inputs, *outputs))
    return pl.pallas_call(
        kernel,
        in_specs=in_specs or [VMEM] * len(inputs),
        out_specs=out_specs or [VMEM] * len(outputs),
        out_shape=list(outputs),
        scratch_shapes=list(scratch),
        compiler_params=pltpu.CompilerParams(vmem_limit_bytes=vmem << 20),
        cost_estimate=pl.CostEstimate(flops=flops, bytes_accessed=moved, transcendentals=0),
        input_output_aliases=aliases or {},
        name=name,
    )(*inputs)


def exchange(first, second, axes):
    count = lax.axis_size(axes)
    inner = [(i, i ^ 1) for i in range(count)]
    outer = [(i, (((i + 1) ^ 1) - 1) % count) for i in range(count)]
    return lax.ppermute(first, axes, inner), lax.ppermute(second, axes, outer)


def local(probes, coefficients):
    planes = probes.reshape(PLANES, ROWS, 128)
    weights = coefficients.reshape(COEFS, ROWS, 128)
    scratch = lambda *dims: pltpu.VMEM(dims, F32)
    x_first, x_second = call(
        pack_rows_kernel,
        "pack_rows",
        [pltpu.with_memory_space_constraint(array, pltpu.HBM) for array in (planes, weights)],
        [pltpu.VMEM((PAIRS, 8, 128), F32)] * 2,
        [scratch(PLANES, 8, 128)] * 2 + [scratch(COEFS, 8, 128)] * 2 + [pltpu.SemaphoreType.DMA((4,))],
        in_specs=[pl.BlockSpec(memory_space=pltpu.HBM)] * 2,
    )
    x_first, x_second = exchange(x_first, x_second, ACROSS)

    inner, own_left, own_right = call(
        inner_kernel,
        "inner",
        (planes, weights),
        [
            shape(PLANES, ROWS, 128),
            shape(15, 8, 128),
            shape(15, 8, 128),
        ],
        [scratch(PLANES, ROWS, 128)] * 2,
        flops=15_000_000,
    )
    y_first, y_second = call(
        halo_kernel, "halo", (x_first, x_second, own_left, own_right), [shape(15, 8, 128)] * 2
    )
    y_first, y_second = exchange(y_first, y_second, "z")

    main, partial, strip, cstrip = call(
        outer_kernel,
        "outer",
        (planes, weights, x_first, x_second, inner),
        [shape(PLANES, ROWS, 128), shape(128, 128), shape(16, 40, 128), shape(COEFS, 40, 128)],
        [scratch(PLANES, 32, 128)] * 2 + [scratch(COEFS, 32, 128), scratch(PLANES, 16, 128)],
        flops=10_000_000,
    )
    sketch, late, gram = call(
        edge_kernel,
        "edge",
        (main, partial, strip, cstrip, y_first, y_second),
        [shape(16, 4, ROWS, 128), pltpu.VMEM((16, 2, ROWS, 128), F32), shape(16, 2, 128)],
        [
            scratch(16, EXT, 128),
            scratch(16, EXT, 128),
            scratch(COEFS, EXT, 128),
            scratch(16, ROWS, 128),
            scratch(16, 2, ROWS, 128),
            pltpu.SemaphoreType.DMA((2,)),
        ],
        out_specs=[ANY, VMEM, VMEM],
    )

    gathered = lax.all_to_all(gram, ("core", "z"), 0, 0, tiled=True)
    gram = jnp.broadcast_to(gathered.sum(axis=0)[None], (16, 2, 128))
    gathered = lax.all_to_all(gram, ("x", "y"), 0, 0, tiled=True)
    total_rows = PLANES // 16 * ROWS * 128 * lax.axis_size(ACROSS + ("z",))
    factor, sketch = call(
        lambda *refs: finish_kernel(1.0 / total_rows, *refs),
        "finish",
        (gathered, late, sketch),
        [shape(16, 16), shape(16, 4, ROWS, 128)],
        [pltpu.SemaphoreType.DMA],
        in_specs=[VMEM, VMEM, ANY],
        out_specs=[VMEM, ANY],
        aliases={2: 1},
    )
    return sketch.reshape(probes.shape), factor


def solution(mesh):
    fine = Mesh(mesh.devices.reshape(4, 4, 2, 8), ("x", "y", "core", "z"))
    placed = (P(None, None, None, ACROSS, "z"), P(None, None, ACROSS, "z"))
    return jax.shard_map(
        local,
        mesh=fine,
        in_specs=placed,
        out_specs=(P(None, None, None, ACROSS, "z"), P()),
        check_vma=False,
    )
```

```python
import math

import jax
import jax.numpy as jnp
from jax import lax
from jax.experimental import pallas as pl
from jax.experimental.pallas import tpu as pltpu
from jax.sharding import Mesh, PartitionSpec as P

PLANES = 64
COEFS = 30
PAIRS = (PLANES + COEFS) // 2
ROWS = 32
EXT = 48
STRIP_STARTS = ((5, 13, 21, 29, 35), (6, 14, 22, 30, 34), (7, 15, 23, 31, 33), (8, 16, 24, 32))
INNER_STARTS = ((1, 9, 17, 23), (2, 10, 18, 22), (3, 11, 19, 21), (4, 12, 20))
OUTER_STARTS = ((5, 13, 19), (6, 18), (7, 17), (8, 16))
ACROSS = ("x", "y", "core")
F32 = jnp.float32


def iota(shape, dim):
    return lax.broadcasted_iota(jnp.int32, shape, dim)


def lane_roll(array, shift):
    shift = shift % 128
    return array if shift == 0 else pltpu.roll(array, shift, array.ndim - 1)


def half_roll(array):
    return pltpu.roll(array, 4, array.ndim - 2)


def is_even(axes):
    return lax.rem(lax.axis_index(axes), 2) == 0


def pack_rows_kernel(p_hbm, c_hbm, first_ref, second_ref, p_top, p_bottom, c_top, c_bottom, sems):
    sources = (p_hbm.at[:, 0:8], p_hbm.at[:, ROWS - 8 : ROWS], c_hbm.at[:, 0:8], c_hbm.at[:, ROWS - 8 : ROWS])
    targets = (p_top, p_bottom, c_top, c_bottom)
    copies = [pltpu.make_async_copy(src, dst, sems.at[i]) for i, (src, dst) in enumerate(zip(sources, targets))]
    for copy in copies:
        copy.start()
    even = is_even(ACROSS)
    for copy in copies:
        copy.wait()
    for first, last, offset, half in (
        (p_top, p_bottom, 0, PLANES // 2),
        (c_top, c_bottom, PLANES // 2, COEFS // 2),
    ):
        upper = iota((half, 8, 128), 1) < 4
        low = jnp.where(upper, first[:half], half_roll(first[half:]))
        high = jnp.where(upper, half_roll(last[:half]), last[half:])
        first_ref[offset : offset + half] = jnp.where(even, high, low)
        second_ref[offset : offset + half] = jnp.where(even, low, high)


def inside(axes):
    index = lax.axis_index(axes)
    last = lax.axis_size(axes) - 1
    return jnp.where(index > 0, 1.0, 0.0).astype(F32), jnp.where(index < last, 1.0, 0.0).astype(F32)


def pack_columns(values, lane):
    both = []
    for planes in (values[:16], values[16:]):
        packed = None
        for k, value in enumerate(planes):
            value = lane_roll(value, 8 * k + 4)
            packed = value if packed is None else jnp.where(lane // 8 == k, value, packed)
        both.append(packed)
    return split_columns(both, lane)


def halo_columns(left, right, lane):
    first = lane % 8 < 4
    return jnp.where(first, right, lane_roll(left, 4)), jnp.where(first, lane_roll(right, -4), left)


def gather_columns(load, count, lane):
    group = lane // 32
    gathered = []
    for index in range(count):
        total = lane_roll(load(index), 8)
        for q in range(1, 4):
            total = jnp.where(group == q, lane_roll(load(index + q * 16), q * 32 + 8), total)
        gathered.append(total)
    return gathered


def own_strips(gathered, lane):
    return [jnp.where(lane % 32 < 8, total, lane_roll(total, 8)) for total in gathered]


def split_columns(both, lane):
    first = lane % 8 < 4
    return jnp.where(first, lane_roll(both[0], -4), both[1]), jnp.where(first, both[0], lane_roll(both[1], 4))


def make_cstrips(values):
    source, target = iota((128, 128), 0), iota((128, 128), 1) % 32
    wanted = jnp.where(target < 8, target + 120, jnp.where((target >= 16) & (target < 24), target - 16, -1))
    select = (source == wanted).astype(jnp.bfloat16)
    total = None
    for _ in range(3):
        part = values.astype(jnp.bfloat16)
        values = values - part.astype(F32)
        moved = jnp.dot(part, select, preferred_element_type=F32)
        total = moved if total is None else total + moved
    return total


def inner_kernel(p_ref, c_ref, main_ref, left_ref, right_ref, first, second):
    lane = iota((8, 128), 1)
    for tile in range(4):
        rows = slice(8 * tile, 8 * tile + 8)
        for z in range(2):
            planes = [p_ref[p * 4 + c * 2 + z, rows, :] for c in range(2) for p in range(16)]
            left_ref[z * 5 + tile], right_ref[z * 5 + tile] = pack_columns(planes, lane)
        planes = [c_ref[index, rows, :] for index in range(COEFS)]
        left_ref[10 + tile], right_ref[10 + tile] = pack_columns(planes, lane)
    step(p_ref, first, c_ref, 16, INNER_STARTS[0], False)
    step(first, second, c_ref, 16, INNER_STARTS[1], False)
    step(second, first, c_ref, 16, INNER_STARTS[2], True)
    step(first, main_ref, c_ref, 16, INNER_STARTS[3], True)


def halo_kernel(x_first_ref, x_second_ref, own_left_ref, own_right_ref, first_ref, second_ref):
    lane = iota((8, 128), 1)
    upper = iota((8, 128), 0) < 4
    has_low, has_high = inside(ACROSS)
    even, even_z = is_even(ACROSS), is_even("z")

    def put(index, left, right):
        first_ref[index] = jnp.where(even_z, right, left)
        second_ref[index] = jnp.where(even_z, left, right)

    halos = {}
    for offset, half in ((0, PLANES // 2), (PLANES // 2, COEFS // 2)):
        for k in range(half):
            x_first, x_second = x_first_ref[offset + k], x_second_ref[offset + k]
            low = jnp.where(even, x_second, x_first) * has_low
            high = jnp.where(even, x_first, x_second) * has_high
            halos[offset * 2 + k] = jnp.where(upper, low, half_roll(high))
            halos[offset * 2 + k + half] = jnp.where(upper, half_roll(low), high)
    for part in range(3):
        rows = slice(part * 5, part * 5 + 4)
        put(rows, own_left_ref[rows], own_right_ref[rows])
    for z in range(2):
        planes = [halos[p * 4 + c * 2 + z] for c in range(2) for p in range(16)]
        put(z * 5 + 4, *pack_columns(planes, lane))
    put(14, *pack_columns([halos[PLANES + i] for i in range(COEFS)], lane))


def step(source, target, coef, groups, starts, adjoint, shift=0, unroll=16):
    for s in starts:

        def weight(slot, z, move=0):
            return coef[slot * 2 + z, s + move : s + move + 8, :]

        up, down = (-1, 1) if adjoint else (0, 0)
        weights = {}
        for z in range(2):
            weights[14, z] = weight(14, z)
            for c in range(2):
                weights[c, z] = weight(c, z)
                slot = 2 + 6 * c
                weights[slot, z] = weight(slot, z, up)
                weights[slot + 1, z] = weight(slot + 1, z, down)
                weights[slot + 2, z] = weight(slot + 2, z)
                weights[slot + 3, z] = weight(slot + 3, z)
                vertical = slot + (4 if z == 0 else 5)
                weights[vertical, z] = weight(vertical, z)

        def body(group, carry):
            base = group * 4

            def field(c, z, move=0):
                return source[base + (c * 2 + z), s + move : s + move + 8, :]

            centre = {(c, z): field(c, z) for c in range(2) for z in range(2)}
            for c in range(2):
                for z in range(2):
                    value = centre[c, z]
                    slot = 2 + 6 * c
                    total = weights[c, z] * value
                    before, after = field(c, z, -1), field(c, z, 1)
                    if adjoint:
                        total = total + weights[slot, z] * before + weights[slot + 1, z] * after
                        total = total + lane_roll(weights[slot + 2, z] * value, 1)
                        total = total + lane_roll(weights[slot + 3, z] * value, -1)
                        vertical = slot + (5 if z == 0 else 4)
                        total = total + weights[vertical, 1 - z] * centre[c, 1 - z]
                        if c == 0:
                            total = total + weights[14, z] * centre[1, z]
                    else:
                        total = total + weights[slot, z] * after + weights[slot + 1, z] * before
                        total = total + weights[slot + 2, z] * lane_roll(value, -1)
                        total = total + weights[slot + 3, z] * lane_roll(value, 1)
                        vertical = slot + (4 if z == 0 else 5)
                        total = total + weights[vertical, z] * centre[c, 1 - z]
                        if c == 1:
                            total = total + weights[14, z] * centre[0, z]
                    target[base + (c * 2 + z), s + shift : s + shift + 8, :] = total
            return carry

        lax.fori_loop(0, groups, body, 0, unroll=min(unroll, groups))


def fill(outer, own, x_first, x_second, half, offset, has_low, has_high, even):
    outer[:, 8:16, :] = own[:, 0:8, :]
    outer[:, 16:24, :] = own[:, ROWS - 8 : ROWS, :]
    for here, there, row, has in ((x_second, x_first, 4, has_low), (x_first, x_second, 24, has_high)):
        side = jnp.where(even, here[offset : offset + half], there[offset : offset + half]) * has
        outer[:half, row : row + 4, :] = side[:, 0:4, :]
        outer[half:, row : row + 4, :] = side[:, 4:8, :]


def put_tile(ref, index, tile, value):
    if tile < 4:
        ref[index, 8 + 8 * tile : 16 + 8 * tile, :] = value
    else:
        ref[index, 4:8, :] = value[0:4]
        ref[index, 40:44, :] = value[4:8]


def gram_of(block, contract):
    return lax.dot_general(
        block,
        block,
        (((contract,), (contract,)), ((), ())),
        precision=lax.Precision.HIGHEST,
        preferred_element_type=F32,
    )


def outer_kernel(
    p_ref, c_ref, x_first_ref, x_second_ref, inner_ref, main_ref, gram_ref, strip_ref, cstrip_ref, first, second, coef, result
):
    has_low, has_high = inside(ACROSS)
    even = is_even(ACROSS)
    fill(first, p_ref, x_first_ref, x_second_ref, PLANES // 2, 0, has_low, has_high, even)
    fill(coef, c_ref, x_first_ref, x_second_ref, COEFS // 2, PLANES // 2, has_low, has_high, even)
    lane = iota((8, 128), 1)
    upper = iota((8, 128), 0) < 4

    def halo(ref, index):
        return jnp.where(upper, ref[index, 4:12, :], ref[index, 20:28, :])

    for tile in range(5):
        rows = slice(8 * tile, 8 * tile + 8)
        load = (lambda i: p_ref[i, rows, :]) if tile < 4 else (lambda i: halo(first, i))
        for index, strip in enumerate(own_strips(gather_columns(load, 16, lane), lane)):
            strip_ref[index, rows, :] = strip
    halos = jnp.concatenate([halo(coef, index) for index in range(COEFS)], axis=0)
    cstrip_ref[:, 32:40, :] = make_cstrips(halos).reshape(COEFS, 8, 128)
    cstrip_ref[:, 0:32, :] = make_cstrips(c_ref[...].reshape(COEFS * ROWS, 128)).reshape(COEFS, ROWS, 128)
    step(first, second, coef, 16, OUTER_STARTS[0], False)
    step(second, first, coef, 16, OUTER_STARTS[1], False)
    step(first, second, coef, 16, OUTER_STARTS[2], True)
    step(second, result, coef, 16, OUTER_STARTS[3], True, -8)
    known = (lane >= 4) & (lane < 124)
    blocks = []
    for part in range(4):
        for row in range(0, ROWS, 8):
            block = []
            for p in range(16):
                plane = p * 4 + part
                value = inner_ref[plane, row : row + 8, :]
                if row == 0:
                    value = jnp.where(upper, result[plane, 0:8, :], value)
                elif row == ROWS - 8:
                    value = jnp.where(upper, value, result[plane, 8:16, :])
                main_ref[plane, row : row + 8, :] = value
                block.append(jnp.where(known, value, 0.0))
            blocks.append(jnp.concatenate(block, axis=0))
    high = [block.astype(jnp.bfloat16) for block in blocks]
    low = [(block - part.astype(F32)).astype(jnp.bfloat16) for block, part in zip(blocks, high)]
    high, low = jnp.concatenate(high, axis=1), jnp.concatenate(low, axis=1)
    product = lambda a, b: lax.dot_general(a, b, (((1,), (1,)), ((), ())), preferred_element_type=F32)
    mixed = product(high, low)
    gram_ref[...] = product(high, high) + product(low, low) + (mixed + mixed.T)


def edge_kernel(
    main_ref,
    partial_ref,
    strip_ref,
    cstrip_ref,
    y_first_ref,
    y_second_ref,
    out_ref,
    gram_ref,
    first,
    second,
    coef,
    result,
):
    lane = iota((8, 128), 1)
    group, offset = lane // 32, lane % 32
    is_halo = (offset >= 8) & (offset < 16)
    has_left, has_right = inside("z")
    even = is_even("z")

    def own(ref, index, tile):
        return ref[index, 8 * tile : 8 * tile + 8, :]

    def columns(part, tile):
        index = part * 5 + tile
        y_first, y_second = y_first_ref[index], y_second_ref[index]
        left, right = jnp.where(even, y_second, y_first), jnp.where(even, y_first, y_second)
        return halo_columns(left * has_left, right * has_right, lane)

    for z in range(2):
        for tile in range(5):
            halos = columns(z, tile)
            for t in range(4):
                for c in range(2):
                    index = t * 4 + c * 2 + z
                    value = own(strip_ref, index, tile)
                    put_tile(first, index, tile, jnp.where(is_halo, lane_roll(halos[c], 8 - 8 * t), value))
    for tile in range(5):
        halos = columns(2, tile)
        for half in range(2):
            rolled = [lane_roll(halos[half], 8 * k) for k in range(16)]
            for k in range(16 if half == 0 else COEFS - 16):
                index = half * 16 + k
                spread = rolled[(1 - k) % 16]
                for q in range(1, 4):
                    spread = jnp.where(group == q, rolled[(4 * q + 1 - k) % 16], spread)
                value = own(cstrip_ref, index, tile)
                put_tile(coef, index, tile, jnp.where(is_halo, spread, value))
    step(first, second, coef, 4, STRIP_STARTS[0], False)
    step(second, first, coef, 4, STRIP_STARTS[1], False)
    step(first, second, coef, 4, STRIP_STARTS[2], True)
    step(second, result, coef, 4, STRIP_STARTS[3], True, -8)

    blocks = []
    for part in range(4):
        for row in range(0, ROWS, 8):
            packed = None
            for t in range(4):
                value = result[t * 4 + part, row : row + 8, :]
                value = jnp.where(lane % 8 < 4, lane_roll(value, 8 * t - 4), lane_roll(value, 8 * t - 12))
                packed = value if packed is None else jnp.where(offset // 8 == t, value, packed)
            blocks.append(packed)
    is_edge = (lane < 4) | (lane >= 124)
    for i, packed in enumerate(blocks):
        part, row = i // 4, i % 4 * 8
        for p in range(16):
            plane = p * 4 + part
            value = main_ref[plane, row : row + 8, :]
            out_ref[plane, row : row + 8, :] = jnp.where(is_edge, lane_roll(packed, 124 - 8 * p), value)

    gram = partial_ref[...] + gram_of(jnp.concatenate(blocks, axis=0), 0)
    same = iota((128, 128), 0) % 8 == iota((128, 128), 1) % 8
    folded = jnp.where(same, gram, 0.0).reshape(16, 8, 128).sum(axis=1)
    select = (iota((128, 128), 0) // 8 == iota((128, 128), 1) % 16).astype(F32)
    spread = jnp.dot(folded, select, precision=lax.Precision.HIGHEST, preferred_element_type=F32)
    mine = iota((16, 128), 1) // 16 == iota((16, 128), 0) % 8
    tile = jnp.where(mine, spread, 0.0).reshape(2, 8, 128).sum(axis=1)
    gram_ref[...] = jnp.broadcast_to(tile[None], gram_ref.shape)


def finish_kernel(scale, in_ref, sketch_ref, factor_hbm, sketch_hbm, out_ref, sems):
    copy = pltpu.make_async_copy(sketch_ref, sketch_hbm, sems.at[0])
    copy.start()
    tile = jnp.sum(in_ref[...], axis=0) * scale
    row, col = iota((16, 128), 0), iota((16, 128), 1)
    work = jnp.concatenate([jnp.broadcast_to(tile[i : i + 1], (8, 128)) for i in range(2)], axis=0)
    work = jnp.where(col // 16 == row % 8, work, 0.0)
    for shift in (64, 32, 16):
        work = work + lane_roll(work, shift)
    work = jnp.where(col < 16, work, 0.0)
    columns = [jnp.broadcast_to(work[:, j : j + 1], (16, 128)) for j in range(16)]
    for k in range(16):
        pivot = columns[k][k : k + 1, :]
        if k < 15:
            scaled = jnp.where(row > k, columns[k] / pivot, 0.0)
            for j in range(k + 1, 16):
                columns[j] = columns[j] - scaled * columns[j][k : k + 1, :]
    factor = jnp.zeros((16, 128), F32)
    for k in range(16):
        factor = jnp.where(col == k, columns[k], factor)
    diagonal = jnp.sum(jnp.where(row == col, factor, 0.0), axis=1, keepdims=True)
    factor = jnp.where(col >= row, factor / jnp.sqrt(diagonal), 0.0)
    out_ref[...] = factor[:, :16]
    last = pltpu.make_async_copy(out_ref, factor_hbm, sems.at[1])
    last.start()
    copy.wait()
    last.wait()


def shape(*dims):
    return jax.ShapeDtypeStruct(dims, F32)


VMEM = pl.BlockSpec(memory_space=pltpu.VMEM)
ANY = pl.BlockSpec(memory_space=pl.ANY)


def call(kernel, name, inputs, outputs, scratch=(), in_specs=None, out_specs=None, flops=1_000_000, vmem=32):
    moved = 4 * sum(math.prod(a.shape) for a in (*inputs, *outputs))
    return pl.pallas_call(
        kernel,
        in_specs=in_specs or [VMEM] * len(inputs),
        out_specs=out_specs or [VMEM] * len(outputs),
        out_shape=list(outputs),
        scratch_shapes=list(scratch),
        compiler_params=pltpu.CompilerParams(vmem_limit_bytes=vmem << 20),
        cost_estimate=pl.CostEstimate(flops=flops, bytes_accessed=moved, transcendentals=0),
        name=name,
    )(*inputs)


def exchange(first, second, axes):
    count = lax.axis_size(axes)
    inner = [(i, i ^ 1) for i in range(count)]
    outer = [(i, (((i + 1) ^ 1) - 1) % count) for i in range(count)]
    return lax.ppermute(first, axes, inner), lax.ppermute(second, axes, outer)


def local(probes, coefficients):
    planes = probes.reshape(PLANES, ROWS, 128)
    weights = coefficients.reshape(COEFS, ROWS, 128)
    scratch = lambda *dims: pltpu.VMEM(dims, F32)
    x_first, x_second = call(
        pack_rows_kernel,
        "pack_rows",
        [pltpu.with_memory_space_constraint(array, pltpu.HBM) for array in (planes, weights)],
        [pltpu.VMEM((PAIRS, 8, 128), F32)] * 2,
        [scratch(PLANES, 8, 128)] * 2 + [scratch(COEFS, 8, 128)] * 2 + [pltpu.SemaphoreType.DMA((4,))],
        in_specs=[pl.BlockSpec(memory_space=pltpu.HBM)] * 2,
    )
    x_first, x_second = exchange(x_first, x_second, ACROSS)

    inner, own_left, own_right = call(
        inner_kernel,
        "inner",
        (planes, weights),
        [
            shape(PLANES, ROWS, 128),
            shape(15, 8, 128),
            shape(15, 8, 128),
        ],
        [scratch(PLANES, ROWS, 128)] * 2,
        flops=15_000_000,
    )
    y_first, y_second = call(
        halo_kernel, "halo", (x_first, x_second, own_left, own_right), [shape(15, 8, 128)] * 2
    )
    y_first, y_second = exchange(y_first, y_second, "z")

    main, partial, strip, cstrip = call(
        outer_kernel,
        "outer",
        (planes, weights, x_first, x_second, inner),
        [shape(PLANES, ROWS, 128), shape(128, 128), shape(16, 40, 128), shape(COEFS, 40, 128)],
        [scratch(PLANES, 32, 128)] * 2 + [scratch(COEFS, 32, 128), scratch(PLANES, 16, 128)],
        flops=10_000_000,
    )
    sketch, gram = call(
        edge_kernel,
        "edge",
        (main, partial, strip, cstrip, y_first, y_second),
        [pltpu.VMEM((PLANES, ROWS, 128), F32), shape(16, 2, 128)],
        [
            scratch(16, EXT, 128),
            scratch(16, EXT, 128),
            scratch(COEFS, EXT, 128),
            scratch(16, ROWS, 128),
        ],
    )

    gathered = lax.all_to_all(gram, ("core", "z"), 0, 0, tiled=True)
    gram = jnp.broadcast_to(gathered.sum(axis=0)[None], (16, 2, 128))
    gathered = lax.all_to_all(gram, ("x", "y"), 0, 0, tiled=True)
    total_rows = PLANES // 16 * ROWS * 128 * lax.axis_size(ACROSS + ("z",))
    factor, sketch = call(
        lambda *refs: finish_kernel(1.0 / total_rows, *refs),
        "finish",
        (gathered, sketch),
        [shape(16, 16), shape(PLANES, ROWS, 128)],
        [scratch(16, 16), pltpu.SemaphoreType.DMA((2,))],
        out_specs=[ANY, ANY],
    )
    return sketch.reshape(probes.shape), factor


def solution(mesh):
    fine = Mesh(mesh.devices.reshape(4, 4, 2, 8), ("x", "y", "core", "z"))
    placed = (P(None, None, None, ACROSS, "z"), P(None, None, ACROSS, "z"))
    return jax.shard_map(
        local,
        mesh=fine,
        in_specs=placed,
        out_specs=(P(None, None, None, ACROSS, "z"), P()),
        check_vma=False,
    )
```

```python
import math

import jax
import jax.numpy as jnp
from jax import lax
from jax.experimental import pallas as pl
from jax.experimental.pallas import tpu as pltpu
from jax.sharding import Mesh, PartitionSpec as P

PLANES = 64
COEFS = 30
PAIRS = (PLANES + COEFS) // 2
ROWS = 32
EXT = 48
STRIP_STARTS = ((5, 13, 21, 29, 35), (6, 14, 22, 30, 34), (7, 15, 23, 31, 33), (8, 16, 24, 32))
INNER_STARTS = ((1, 9, 17, 23), (2, 10, 18, 22), (3, 11, 19, 21), (4, 12, 20))
OUTER_STARTS = ((5, 13, 19), (6, 18), (7, 17), (8, 16))
ACROSS = ("x", "y", "core")
F32 = jnp.float32


def iota(shape, dim):
    return lax.broadcasted_iota(jnp.int32, shape, dim)


def lane_roll(array, shift):
    shift = shift % 128
    return array if shift == 0 else pltpu.roll(array, shift, array.ndim - 1)


def half_roll(array):
    return pltpu.roll(array, 4, array.ndim - 2)


def is_even(axes):
    return lax.rem(lax.axis_index(axes), 2) == 0


def pack_rows_kernel(p_hbm, c_hbm, first_ref, second_ref, p_top, p_bottom, c_top, c_bottom, sems):
    sources = (p_hbm.at[:, 0:8], p_hbm.at[:, ROWS - 8 : ROWS], c_hbm.at[:, 0:8], c_hbm.at[:, ROWS - 8 : ROWS])
    targets = (p_top, p_bottom, c_top, c_bottom)
    copies = [pltpu.make_async_copy(src, dst, sems.at[i]) for i, (src, dst) in enumerate(zip(sources, targets))]
    for copy in copies:
        copy.start()
    even = is_even(ACROSS)
    for copy in copies:
        copy.wait()
    for first, last, offset, half in (
        (p_top, p_bottom, 0, PLANES // 2),
        (c_top, c_bottom, PLANES // 2, COEFS // 2),
    ):
        upper = iota((half, 8, 128), 1) < 4
        low = jnp.where(upper, first[:half], half_roll(first[half:]))
        high = jnp.where(upper, half_roll(last[:half]), last[half:])
        first_ref[offset : offset + half] = jnp.where(even, high, low)
        second_ref[offset : offset + half] = jnp.where(even, low, high)


def inside(axes):
    index = lax.axis_index(axes)
    last = lax.axis_size(axes) - 1
    return jnp.where(index > 0, 1.0, 0.0).astype(F32), jnp.where(index < last, 1.0, 0.0).astype(F32)


def pack_columns(values, lane):
    both = []
    for planes in (values[:16], values[16:]):
        packed = None
        for k, value in enumerate(planes):
            value = lane_roll(value, 8 * k + 4)
            packed = value if packed is None else jnp.where(lane // 8 == k, value, packed)
        both.append(packed)
    return split_columns(both, lane)


def halo_columns(left, right, lane):
    first = lane % 8 < 4
    return jnp.where(first, right, lane_roll(left, 4)), jnp.where(first, lane_roll(right, -4), left)


def gather_columns(load, count, lane):
    group = lane // 32
    gathered = []
    for index in range(count):
        total = lane_roll(load(index), 8)
        for q in range(1, 4):
            total = jnp.where(group == q, lane_roll(load(index + q * 16), q * 32 + 8), total)
        gathered.append(total)
    return gathered


def own_strips(gathered, lane):
    return [jnp.where(lane % 32 < 8, total, lane_roll(total, 8)) for total in gathered]


def split_columns(both, lane):
    first = lane % 8 < 4
    return jnp.where(first, lane_roll(both[0], -4), both[1]), jnp.where(first, both[0], lane_roll(both[1], 4))


def make_cstrips(values):
    source, target = iota((128, 128), 0), iota((128, 128), 1) % 32
    wanted = jnp.where(target < 8, target + 120, jnp.where((target >= 16) & (target < 24), target - 16, -1))
    select = (source == wanted).astype(jnp.bfloat16)
    total = None
    for _ in range(3):
        part = values.astype(jnp.bfloat16)
        values = values - part.astype(F32)
        moved = jnp.dot(part, select, preferred_element_type=F32)
        total = moved if total is None else total + moved
    return total


def inner_kernel(p_ref, c_ref, main_ref, left_ref, right_ref, first, second):
    lane = iota((8, 128), 1)
    for tile in range(4):
        rows = slice(8 * tile, 8 * tile + 8)
        for z in range(2):
            planes = [p_ref[p * 4 + c * 2 + z, rows, :] for c in range(2) for p in range(16)]
            left_ref[z * 5 + tile], right_ref[z * 5 + tile] = pack_columns(planes, lane)
        planes = [c_ref[index, rows, :] for index in range(COEFS)]
        left_ref[10 + tile], right_ref[10 + tile] = pack_columns(planes, lane)
    step(p_ref, first, c_ref, 16, INNER_STARTS[0], False)
    step(first, second, c_ref, 16, INNER_STARTS[1], False)
    step(second, first, c_ref, 16, INNER_STARTS[2], True)
    step(first, main_ref, c_ref, 16, INNER_STARTS[3], True)


def halo_kernel(x_first_ref, x_second_ref, own_left_ref, own_right_ref, first_ref, second_ref):
    lane = iota((8, 128), 1)
    upper = iota((8, 128), 0) < 4
    has_low, has_high = inside(ACROSS)
    even, even_z = is_even(ACROSS), is_even("z")

    def put(index, left, right):
        first_ref[index] = jnp.where(even_z, right, left)
        second_ref[index] = jnp.where(even_z, left, right)

    halos = {}
    for offset, half in ((0, PLANES // 2), (PLANES // 2, COEFS // 2)):
        for k in range(half):
            x_first, x_second = x_first_ref[offset + k], x_second_ref[offset + k]
            low = jnp.where(even, x_second, x_first) * has_low
            high = jnp.where(even, x_first, x_second) * has_high
            halos[offset * 2 + k] = jnp.where(upper, low, half_roll(high))
            halos[offset * 2 + k + half] = jnp.where(upper, half_roll(low), high)
    for part in range(3):
        rows = slice(part * 5, part * 5 + 4)
        put(rows, own_left_ref[rows], own_right_ref[rows])
    for z in range(2):
        planes = [halos[p * 4 + c * 2 + z] for c in range(2) for p in range(16)]
        put(z * 5 + 4, *pack_columns(planes, lane))
    put(14, *pack_columns([halos[PLANES + i] for i in range(COEFS)], lane))


def step(source, target, coef, groups, starts, adjoint, shift=0, unroll=16):
    for s in starts:

        def weight(slot, z, move=0):
            return coef[slot * 2 + z, s + move : s + move + 8, :]

        up, down = (-1, 1) if adjoint else (0, 0)
        weights = {}
        for z in range(2):
            weights[14, z] = weight(14, z)
            for c in range(2):
                weights[c, z] = weight(c, z)
                slot = 2 + 6 * c
                weights[slot, z] = weight(slot, z, up)
                weights[slot + 1, z] = weight(slot + 1, z, down)
                weights[slot + 2, z] = weight(slot + 2, z)
                weights[slot + 3, z] = weight(slot + 3, z)
                vertical = slot + (4 if z == 0 else 5)
                weights[vertical, z] = weight(vertical, z)

        def body(group, carry):
            base = group * 4

            def field(c, z, move=0):
                return source[base + (c * 2 + z), s + move : s + move + 8, :]

            centre = {(c, z): field(c, z) for c in range(2) for z in range(2)}
            for c in range(2):
                for z in range(2):
                    value = centre[c, z]
                    slot = 2 + 6 * c
                    total = weights[c, z] * value
                    before, after = field(c, z, -1), field(c, z, 1)
                    if adjoint:
                        total = total + weights[slot, z] * before + weights[slot + 1, z] * after
                        total = total + lane_roll(weights[slot + 2, z] * value, 1)
                        total = total + lane_roll(weights[slot + 3, z] * value, -1)
                        vertical = slot + (5 if z == 0 else 4)
                        total = total + weights[vertical, 1 - z] * centre[c, 1 - z]
                        if c == 0:
                            total = total + weights[14, z] * centre[1, z]
                    else:
                        total = total + weights[slot, z] * after + weights[slot + 1, z] * before
                        total = total + weights[slot + 2, z] * lane_roll(value, -1)
                        total = total + weights[slot + 3, z] * lane_roll(value, 1)
                        vertical = slot + (4 if z == 0 else 5)
                        total = total + weights[vertical, z] * centre[c, 1 - z]
                        if c == 1:
                            total = total + weights[14, z] * centre[0, z]
                    target[base + (c * 2 + z), s + shift : s + shift + 8, :] = total
            return carry

        lax.fori_loop(0, groups, body, 0, unroll=min(unroll, groups))


def fill(outer, own, x_first, x_second, half, offset, has_low, has_high, even):
    outer[:, 8:16, :] = own[:, 0:8, :]
    outer[:, 16:24, :] = own[:, ROWS - 8 : ROWS, :]
    for here, there, row, has in ((x_second, x_first, 4, has_low), (x_first, x_second, 24, has_high)):
        side = jnp.where(even, here[offset : offset + half], there[offset : offset + half]) * has
        outer[:half, row : row + 4, :] = side[:, 0:4, :]
        outer[half:, row : row + 4, :] = side[:, 4:8, :]


def put_tile(ref, index, tile, value):
    if tile < 4:
        ref[index, 8 + 8 * tile : 16 + 8 * tile, :] = value
    else:
        ref[index, 4:8, :] = value[0:4]
        ref[index, 40:44, :] = value[4:8]


def gram_of(block, contract):
    return lax.dot_general(
        block,
        block,
        (((contract,), (contract,)), ((), ())),
        precision=lax.Precision.HIGHEST,
        preferred_element_type=F32,
    )


def outer_kernel(
    p_ref, c_ref, x_first_ref, x_second_ref, inner_ref, main_ref, gram_ref, strip_ref, cstrip_ref, first, second, coef, result
):
    has_low, has_high = inside(ACROSS)
    even = is_even(ACROSS)
    fill(first, p_ref, x_first_ref, x_second_ref, PLANES // 2, 0, has_low, has_high, even)
    fill(coef, c_ref, x_first_ref, x_second_ref, COEFS // 2, PLANES // 2, has_low, has_high, even)
    lane = iota((8, 128), 1)
    upper = iota((8, 128), 0) < 4

    def halo(ref, index):
        return jnp.where(upper, ref[index, 4:12, :], ref[index, 20:28, :])

    for tile in range(5):
        rows = slice(8 * tile, 8 * tile + 8)
        load = (lambda i: p_ref[i, rows, :]) if tile < 4 else (lambda i: halo(first, i))
        for index, strip in enumerate(own_strips(gather_columns(load, 16, lane), lane)):
            strip_ref[index, rows, :] = strip
    halos = jnp.concatenate([halo(coef, index) for index in range(COEFS)], axis=0)
    cstrip_ref[:, 32:40, :] = make_cstrips(halos).reshape(COEFS, 8, 128)
    cstrip_ref[:, 0:32, :] = make_cstrips(c_ref[...].reshape(COEFS * ROWS, 128)).reshape(COEFS, ROWS, 128)
    step(first, second, coef, 16, OUTER_STARTS[0], False)
    step(second, first, coef, 16, OUTER_STARTS[1], False)
    step(first, second, coef, 16, OUTER_STARTS[2], True)
    step(second, result, coef, 16, OUTER_STARTS[3], True, -8)
    known = (lane >= 4) & (lane < 124)
    blocks = []
    for part in range(4):
        for row in range(0, ROWS, 8):
            block = []
            for p in range(16):
                plane = p * 4 + part
                value = inner_ref[plane, row : row + 8, :]
                if row == 0:
                    value = jnp.where(upper, result[plane, 0:8, :], value)
                elif row == ROWS - 8:
                    value = jnp.where(upper, value, result[plane, 8:16, :])
                main_ref[plane, row : row + 8, :] = value
                block.append(jnp.where(known, value, 0.0))
            blocks.append(jnp.concatenate(block, axis=0))
    high = [block.astype(jnp.bfloat16) for block in blocks]
    low = [(block - part.astype(F32)).astype(jnp.bfloat16) for block, part in zip(blocks, high)]
    high, low = jnp.concatenate(high, axis=1), jnp.concatenate(low, axis=1)
    product = lambda a, b: lax.dot_general(a, b, (((1,), (1,)), ((), ())), preferred_element_type=F32)
    mixed = product(high, low)
    gram_ref[...] = product(high, high) + product(low, low) + (mixed + mixed.T)


def edge_kernel(
    main_ref,
    partial_ref,
    strip_ref,
    cstrip_ref,
    y_first_ref,
    y_second_ref,
    out_ref,
    gram_ref,
    first,
    second,
    coef,
    result,
):
    lane = iota((8, 128), 1)
    group, offset = lane // 32, lane % 32
    is_halo = (offset >= 8) & (offset < 16)
    has_left, has_right = inside("z")
    even = is_even("z")

    def own(ref, index, tile):
        return ref[index, 8 * tile : 8 * tile + 8, :]

    def columns(part, tile):
        index = part * 5 + tile
        y_first, y_second = y_first_ref[index], y_second_ref[index]
        left, right = jnp.where(even, y_second, y_first), jnp.where(even, y_first, y_second)
        return halo_columns(left * has_left, right * has_right, lane)

    for z in range(2):
        for tile in range(5):
            halos = columns(z, tile)
            for t in range(4):
                for c in range(2):
                    index = t * 4 + c * 2 + z
                    value = own(strip_ref, index, tile)
                    put_tile(first, index, tile, jnp.where(is_halo, lane_roll(halos[c], 8 - 8 * t), value))
    for tile in range(5):
        halos = columns(2, tile)
        for half in range(2):
            rolled = [lane_roll(halos[half], 8 * k) for k in range(16)]
            for k in range(16 if half == 0 else COEFS - 16):
                index = half * 16 + k
                spread = rolled[(1 - k) % 16]
                for q in range(1, 4):
                    spread = jnp.where(group == q, rolled[(4 * q + 1 - k) % 16], spread)
                value = own(cstrip_ref, index, tile)
                put_tile(coef, index, tile, jnp.where(is_halo, spread, value))
    step(first, second, coef, 4, STRIP_STARTS[0], False)
    step(second, first, coef, 4, STRIP_STARTS[1], False)
    step(first, second, coef, 4, STRIP_STARTS[2], True)
    step(second, result, coef, 4, STRIP_STARTS[3], True, -8)

    blocks = []
    for part in range(4):
        for row in range(0, ROWS, 8):
            packed = None
            for t in range(4):
                value = result[t * 4 + part, row : row + 8, :]
                value = jnp.where(lane % 8 < 4, lane_roll(value, 8 * t - 4), lane_roll(value, 8 * t - 12))
                packed = value if packed is None else jnp.where(offset // 8 == t, value, packed)
            blocks.append(packed)
    is_edge = (lane < 4) | (lane >= 124)
    for i, packed in enumerate(blocks):
        part, row = i // 4, i % 4 * 8
        for p in range(16):
            plane = p * 4 + part
            value = main_ref[plane, row : row + 8, :]
            out_ref[plane, row : row + 8, :] = jnp.where(is_edge, lane_roll(packed, 124 - 8 * p), value)

    gram = partial_ref[...] + gram_of(jnp.concatenate(blocks, axis=0), 0)
    same = iota((128, 128), 0) % 8 == iota((128, 128), 1) % 8
    folded = jnp.where(same, gram, 0.0).reshape(16, 8, 128).sum(axis=1)
    select = (iota((128, 128), 0) // 8 == iota((128, 128), 1) % 16).astype(jnp.bfloat16)
    spread, rest = None, folded
    for _ in range(3):
        part = rest.astype(jnp.bfloat16)
        rest = rest - part.astype(F32)
        moved = jnp.dot(part, select, preferred_element_type=F32)
        spread = moved if spread is None else spread + moved
    mine = iota((16, 128), 1) // 16 == iota((16, 128), 0) % 8
    tile = jnp.where(mine, spread, 0.0).reshape(2, 8, 128).sum(axis=1)
    gram_ref[...] = jnp.broadcast_to(tile[None], gram_ref.shape)


def finish_kernel(scale, in_ref, sketch_ref, factor_hbm, sketch_hbm, out_ref, sems):
    copy = pltpu.make_async_copy(sketch_ref, sketch_hbm, sems.at[0])
    copy.start()
    tile = jnp.sum(in_ref[...], axis=0) * scale
    row, col = iota((16, 128), 0), iota((16, 128), 1)
    work = jnp.concatenate([jnp.broadcast_to(tile[i : i + 1], (8, 128)) for i in range(2)], axis=0)
    work = jnp.where(col // 16 == row % 8, work, 0.0)
    for shift in (64, 32, 16):
        work = work + lane_roll(work, shift)
    work = jnp.where(col < 16, work, 0.0)
    columns = [jnp.broadcast_to(work[:, j : j + 1], (16, 128)) for j in range(16)]
    for k in range(16):
        pivot = columns[k][k : k + 1, :]
        if k < 15:
            scaled = jnp.where(row > k, columns[k] / pivot, 0.0)
            for j in range(k + 1, 16):
                columns[j] = columns[j] - scaled * columns[j][k : k + 1, :]
    factor = jnp.zeros((16, 128), F32)
    for k in range(16):
        factor = jnp.where(col == k, columns[k], factor)
    diagonal = jnp.sum(jnp.where(row == col, factor, 0.0), axis=1, keepdims=True)
    factor = jnp.where(col >= row, factor / jnp.sqrt(diagonal), 0.0)
    out_ref[...] = factor[:, :16]
    last = pltpu.make_async_copy(out_ref, factor_hbm, sems.at[1])
    last.start()
    copy.wait()
    last.wait()


def shape(*dims):
    return jax.ShapeDtypeStruct(dims, F32)


VMEM = pl.BlockSpec(memory_space=pltpu.VMEM)
ANY = pl.BlockSpec(memory_space=pl.ANY)


def call(kernel, name, inputs, outputs, scratch=(), in_specs=None, out_specs=None, flops=1_000_000, vmem=32):
    moved = 4 * sum(math.prod(a.shape) for a in (*inputs, *outputs))
    return pl.pallas_call(
        kernel,
        in_specs=in_specs or [VMEM] * len(inputs),
        out_specs=out_specs or [VMEM] * len(outputs),
        out_shape=list(outputs),
        scratch_shapes=list(scratch),
        compiler_params=pltpu.CompilerParams(vmem_limit_bytes=vmem << 20),
        cost_estimate=pl.CostEstimate(flops=flops, bytes_accessed=moved, transcendentals=0),
        name=name,
    )(*inputs)


def exchange(first, second, axes):
    count = lax.axis_size(axes)
    inner = [(i, i ^ 1) for i in range(count)]
    outer = [(i, (((i + 1) ^ 1) - 1) % count) for i in range(count)]
    return lax.ppermute(first, axes, inner), lax.ppermute(second, axes, outer)


def local(probes, coefficients):
    planes = probes.reshape(PLANES, ROWS, 128)
    weights = coefficients.reshape(COEFS, ROWS, 128)
    scratch = lambda *dims: pltpu.VMEM(dims, F32)
    x_first, x_second = call(
        pack_rows_kernel,
        "pack_rows",
        [pltpu.with_memory_space_constraint(array, pltpu.HBM) for array in (planes, weights)],
        [pltpu.VMEM((PAIRS, 8, 128), F32)] * 2,
        [scratch(PLANES, 8, 128)] * 2 + [scratch(COEFS, 8, 128)] * 2 + [pltpu.SemaphoreType.DMA((4,))],
        in_specs=[pl.BlockSpec(memory_space=pltpu.HBM)] * 2,
    )
    x_first, x_second = exchange(x_first, x_second, ACROSS)

    inner, own_left, own_right = call(
        inner_kernel,
        "inner",
        (planes, weights),
        [
            shape(PLANES, ROWS, 128),
            shape(15, 8, 128),
            shape(15, 8, 128),
        ],
        [scratch(PLANES, ROWS, 128)] * 2,
        flops=15_000_000,
    )
    y_first, y_second = call(
        halo_kernel, "halo", (x_first, x_second, own_left, own_right), [shape(15, 8, 128)] * 2
    )
    y_first, y_second = exchange(y_first, y_second, "z")

    main, partial, strip, cstrip = call(
        outer_kernel,
        "outer",
        (planes, weights, x_first, x_second, inner),
        [shape(PLANES, ROWS, 128), shape(128, 128), shape(16, 40, 128), shape(COEFS, 40, 128)],
        [scratch(PLANES, 32, 128)] * 2 + [scratch(COEFS, 32, 128), scratch(PLANES, 16, 128)],
        flops=10_000_000,
    )
    sketch, gram = call(
        edge_kernel,
        "edge",
        (main, partial, strip, cstrip, y_first, y_second),
        [pltpu.VMEM((PLANES, ROWS, 128), F32), shape(16, 2, 128)],
        [
            scratch(16, EXT, 128),
            scratch(16, EXT, 128),
            scratch(COEFS, EXT, 128),
            scratch(16, ROWS, 128),
        ],
    )

    gathered = lax.all_to_all(gram, ("core", "z"), 0, 0, tiled=True)
    gram = jnp.broadcast_to(gathered.sum(axis=0)[None], (16, 2, 128))
    gathered = lax.all_to_all(gram, ("x", "y"), 0, 0, tiled=True)
    total_rows = PLANES // 16 * ROWS * 128 * lax.axis_size(ACROSS + ("z",))
    factor, sketch = call(
        lambda *refs: finish_kernel(1.0 / total_rows, *refs),
        "finish",
        (gathered, sketch),
        [shape(16, 16), shape(PLANES, ROWS, 128)],
        [scratch(16, 16), pltpu.SemaphoreType.DMA((2,))],
        out_specs=[ANY, ANY],
    )
    return sketch.reshape(probes.shape), factor


def solution(mesh):
    fine = Mesh(mesh.devices.reshape(4, 4, 2, 8), ("x", "y", "core", "z"))
    placed = (P(None, None, None, ACROSS, "z"), P(None, None, ACROSS, "z"))
    return jax.shard_map(
        local,
        mesh=fine,
        in_specs=placed,
        out_specs=(P(None, None, None, ACROSS, "z"), P()),
        check_vma=False,
    )
```

```python
import math

import jax
import jax.numpy as jnp
from jax import lax
from jax.experimental import pallas as pl
from jax.experimental.pallas import tpu as pltpu
from jax.sharding import Mesh, PartitionSpec as P

PLANES = 64
COEFS = 30
PAIRS = (PLANES + COEFS) // 2
ROWS = 32
EXT = 48
STRIP_STARTS = ((5, 13, 21, 29, 35), (6, 14, 22, 30, 34), (7, 15, 23, 31, 33), (8, 16, 24, 32))
INNER_STARTS = ((1, 9, 17, 23), (2, 10, 18, 22), (3, 11, 19, 21), (4, 12, 20))
OUTER_STARTS = ((5, 13, 19), (6, 18), (7, 17), (8, 16))
ACROSS = ("x", "y", "core")
F32 = jnp.float32


def iota(shape, dim):
    return lax.broadcasted_iota(jnp.int32, shape, dim)


def lane_roll(array, shift):
    shift = shift % 128
    return array if shift == 0 else pltpu.roll(array, shift, array.ndim - 1)


def half_roll(array):
    return pltpu.roll(array, 4, array.ndim - 2)


def is_even(axes):
    return lax.rem(lax.axis_index(axes), 2) == 0


def pack_rows_kernel(p_hbm, c_hbm, first_ref, second_ref, p_top, p_bottom, c_top, c_bottom, sems):
    sources = (p_hbm.at[:, 0:8], p_hbm.at[:, ROWS - 8 : ROWS], c_hbm.at[:, 0:8], c_hbm.at[:, ROWS - 8 : ROWS])
    targets = (p_top, p_bottom, c_top, c_bottom)
    copies = [pltpu.make_async_copy(src, dst, sems.at[i]) for i, (src, dst) in enumerate(zip(sources, targets))]
    for copy in copies:
        copy.start()
    even = is_even(ACROSS)
    for copy in copies:
        copy.wait()
    for first, last, offset, half in (
        (p_top, p_bottom, 0, PLANES // 2),
        (c_top, c_bottom, PLANES // 2, COEFS // 2),
    ):
        upper = iota((half, 8, 128), 1) < 4
        low = jnp.where(upper, first[:half], half_roll(first[half:]))
        high = jnp.where(upper, half_roll(last[:half]), last[half:])
        first_ref[offset : offset + half] = jnp.where(even, high, low)
        second_ref[offset : offset + half] = jnp.where(even, low, high)


def inside(axes):
    index = lax.axis_index(axes)
    last = lax.axis_size(axes) - 1
    return jnp.where(index > 0, 1.0, 0.0).astype(F32), jnp.where(index < last, 1.0, 0.0).astype(F32)


def pack_columns(values, lane):
    both = []
    for planes in (values[:16], values[16:]):
        packed = None
        for k, value in enumerate(planes):
            value = lane_roll(value, 8 * k + 4)
            packed = value if packed is None else jnp.where(lane // 8 == k, value, packed)
        both.append(packed)
    return split_columns(both, lane)


def halo_columns(left, right, lane):
    first = lane % 8 < 4
    return jnp.where(first, right, lane_roll(left, 4)), jnp.where(first, lane_roll(right, -4), left)


def gather_columns(load, count, lane):
    group = lane // 32
    gathered = []
    for index in range(count):
        total = lane_roll(load(index), 8)
        for q in range(1, 4):
            total = jnp.where(group == q, lane_roll(load(index + q * 16), q * 32 + 8), total)
        gathered.append(total)
    return gathered


def own_strips(gathered, lane):
    return [jnp.where(lane % 32 < 8, total, lane_roll(total, 8)) for total in gathered]


def split_columns(both, lane):
    first = lane % 8 < 4
    return jnp.where(first, lane_roll(both[0], -4), both[1]), jnp.where(first, both[0], lane_roll(both[1], 4))


def make_cstrips(values):
    source, target = iota((128, 128), 0), iota((128, 128), 1) % 32
    wanted = jnp.where(target < 8, target + 120, jnp.where((target >= 16) & (target < 24), target - 16, -1))
    select = (source == wanted).astype(jnp.bfloat16)
    total = None
    for _ in range(3):
        part = values.astype(jnp.bfloat16)
        values = values - part.astype(F32)
        moved = jnp.dot(part, select, preferred_element_type=F32)
        total = moved if total is None else total + moved
    return total


def inner_kernel(p_ref, c_ref, main_ref, left_ref, right_ref, first, second):
    lane = iota((8, 128), 1)
    for tile in range(4):
        rows = slice(8 * tile, 8 * tile + 8)
        for z in range(2):
            planes = [p_ref[p * 4 + c * 2 + z, rows, :] for c in range(2) for p in range(16)]
            left_ref[z * 5 + tile], right_ref[z * 5 + tile] = pack_columns(planes, lane)
        planes = [c_ref[index, rows, :] for index in range(COEFS)]
        left_ref[10 + tile], right_ref[10 + tile] = pack_columns(planes, lane)
    step(p_ref, first, c_ref, 16, INNER_STARTS[0], False)
    step(first, second, c_ref, 16, INNER_STARTS[1], False)
    step(second, first, c_ref, 16, INNER_STARTS[2], True)
    step(first, main_ref, c_ref, 16, INNER_STARTS[3], True)


def halo_kernel(x_first_ref, x_second_ref, own_left_ref, own_right_ref, first_ref, second_ref):
    lane = iota((8, 128), 1)
    upper = iota((8, 128), 0) < 4
    has_low, has_high = inside(ACROSS)
    even, even_z = is_even(ACROSS), is_even("z")

    def put(index, left, right):
        first_ref[index] = jnp.where(even_z, right, left)
        second_ref[index] = jnp.where(even_z, left, right)

    halos = {}
    for offset, half in ((0, PLANES // 2), (PLANES // 2, COEFS // 2)):
        for k in range(half):
            x_first, x_second = x_first_ref[offset + k], x_second_ref[offset + k]
            low = jnp.where(even, x_second, x_first) * has_low
            high = jnp.where(even, x_first, x_second) * has_high
            halos[offset * 2 + k] = jnp.where(upper, low, half_roll(high))
            halos[offset * 2 + k + half] = jnp.where(upper, half_roll(low), high)
    for part in range(3):
        rows = slice(part * 5, part * 5 + 4)
        put(rows, own_left_ref[rows], own_right_ref[rows])
    for z in range(2):
        planes = [halos[p * 4 + c * 2 + z] for c in range(2) for p in range(16)]
        put(z * 5 + 4, *pack_columns(planes, lane))
    put(14, *pack_columns([halos[PLANES + i] for i in range(COEFS)], lane))


def step(source, target, coef, groups, starts, adjoint, shift=0, unroll=16):
    for s in starts:

        def weight(slot, z, move=0):
            return coef[slot * 2 + z, s + move : s + move + 8, :]

        up, down = (-1, 1) if adjoint else (0, 0)
        weights = {}
        for z in range(2):
            weights[14, z] = weight(14, z)
            for c in range(2):
                weights[c, z] = weight(c, z)
                slot = 2 + 6 * c
                weights[slot, z] = weight(slot, z, up)
                weights[slot + 1, z] = weight(slot + 1, z, down)
                weights[slot + 2, z] = weight(slot + 2, z)
                weights[slot + 3, z] = weight(slot + 3, z)
                vertical = slot + (4 if z == 0 else 5)
                weights[vertical, z] = weight(vertical, z)

        def body(group, carry):
            base = group * 4

            def field(c, z, move=0):
                return source[base + (c * 2 + z), s + move : s + move + 8, :]

            centre = {(c, z): field(c, z) for c in range(2) for z in range(2)}
            for c in range(2):
                for z in range(2):
                    value = centre[c, z]
                    slot = 2 + 6 * c
                    total = weights[c, z] * value
                    before, after = field(c, z, -1), field(c, z, 1)
                    if adjoint:
                        total = total + weights[slot, z] * before + weights[slot + 1, z] * after
                        total = total + lane_roll(weights[slot + 2, z] * value, 1)
                        total = total + lane_roll(weights[slot + 3, z] * value, -1)
                        vertical = slot + (5 if z == 0 else 4)
                        total = total + weights[vertical, 1 - z] * centre[c, 1 - z]
                        if c == 0:
                            total = total + weights[14, z] * centre[1, z]
                    else:
                        total = total + weights[slot, z] * after + weights[slot + 1, z] * before
                        total = total + weights[slot + 2, z] * lane_roll(value, -1)
                        total = total + weights[slot + 3, z] * lane_roll(value, 1)
                        vertical = slot + (4 if z == 0 else 5)
                        total = total + weights[vertical, z] * centre[c, 1 - z]
                        if c == 1:
                            total = total + weights[14, z] * centre[0, z]
                    target[base + (c * 2 + z), s + shift : s + shift + 8, :] = total
            return carry

        lax.fori_loop(0, groups, body, 0, unroll=min(unroll, groups))


def fill(outer, own, x_first, x_second, half, offset, has_low, has_high, even):
    outer[:, 8:16, :] = own[:, 0:8, :]
    outer[:, 16:24, :] = own[:, ROWS - 8 : ROWS, :]
    for here, there, row, has in ((x_second, x_first, 4, has_low), (x_first, x_second, 24, has_high)):
        side = jnp.where(even, here[offset : offset + half], there[offset : offset + half]) * has
        outer[:half, row : row + 4, :] = side[:, 0:4, :]
        outer[half:, row : row + 4, :] = side[:, 4:8, :]


def put_tile(ref, index, tile, value):
    if tile < 4:
        ref[index, 8 + 8 * tile : 16 + 8 * tile, :] = value
    else:
        ref[index, 4:8, :] = value[0:4]
        ref[index, 40:44, :] = value[4:8]


def gram_of(blocks, joined, contract):
    high = [block.astype(jnp.bfloat16) for block in blocks]
    low = [(block - part.astype(F32)).astype(jnp.bfloat16) for block, part in zip(blocks, high)]
    high, low = jnp.concatenate(high, axis=joined), jnp.concatenate(low, axis=joined)
    dims = (((contract,), (contract,)), ((), ()))
    product = lambda a, b: lax.dot_general(a, b, dims, preferred_element_type=F32)
    mixed = product(high, low)
    return product(high, high) + product(low, low) + (mixed + mixed.T)


def outer_kernel(
    p_ref, c_ref, x_first_ref, x_second_ref, inner_ref, main_ref, gram_ref, strip_ref, cstrip_ref, first, second, coef, result
):
    has_low, has_high = inside(ACROSS)
    even = is_even(ACROSS)
    fill(first, p_ref, x_first_ref, x_second_ref, PLANES // 2, 0, has_low, has_high, even)
    fill(coef, c_ref, x_first_ref, x_second_ref, COEFS // 2, PLANES // 2, has_low, has_high, even)
    lane = iota((8, 128), 1)
    upper = iota((8, 128), 0) < 4

    def halo(ref, index):
        return jnp.where(upper, ref[index, 4:12, :], ref[index, 20:28, :])

    for tile in range(5):
        rows = slice(8 * tile, 8 * tile + 8)
        load = (lambda i: p_ref[i, rows, :]) if tile < 4 else (lambda i: halo(first, i))
        for index, strip in enumerate(own_strips(gather_columns(load, 16, lane), lane)):
            strip_ref[index, rows, :] = strip
    halos = jnp.concatenate([halo(coef, index) for index in range(COEFS)], axis=0)
    cstrip_ref[:, 32:40, :] = make_cstrips(halos).reshape(COEFS, 8, 128)
    cstrip_ref[:, 0:32, :] = make_cstrips(c_ref[...].reshape(COEFS * ROWS, 128)).reshape(COEFS, ROWS, 128)
    step(first, second, coef, 16, OUTER_STARTS[0], False)
    step(second, first, coef, 16, OUTER_STARTS[1], False)
    step(first, second, coef, 16, OUTER_STARTS[2], True)
    step(second, result, coef, 16, OUTER_STARTS[3], True, -8)
    known = (lane >= 4) & (lane < 124)
    blocks = []
    for part in range(4):
        for row in range(0, ROWS, 8):
            block = []
            for p in range(16):
                plane = p * 4 + part
                value = inner_ref[plane, row : row + 8, :]
                if row == 0:
                    value = jnp.where(upper, result[plane, 0:8, :], value)
                elif row == ROWS - 8:
                    value = jnp.where(upper, value, result[plane, 8:16, :])
                main_ref[plane, row : row + 8, :] = value
                block.append(jnp.where(known, value, 0.0))
            blocks.append(jnp.concatenate(block, axis=0))
    gram_ref[...] = gram_of(blocks, 1, 1)


def edge_kernel(
    main_ref,
    partial_ref,
    strip_ref,
    cstrip_ref,
    y_first_ref,
    y_second_ref,
    out_ref,
    gram_ref,
    first,
    second,
    coef,
    result,
):
    lane = iota((8, 128), 1)
    group, offset = lane // 32, lane % 32
    is_halo = (offset >= 8) & (offset < 16)
    has_left, has_right = inside("z")
    even = is_even("z")

    def own(ref, index, tile):
        return ref[index, 8 * tile : 8 * tile + 8, :]

    def columns(part, tile):
        index = part * 5 + tile
        y_first, y_second = y_first_ref[index], y_second_ref[index]
        left, right = jnp.where(even, y_second, y_first), jnp.where(even, y_first, y_second)
        return halo_columns(left * has_left, right * has_right, lane)

    for z in range(2):
        for tile in range(5):
            halos = columns(z, tile)
            for t in range(4):
                for c in range(2):
                    index = t * 4 + c * 2 + z
                    value = own(strip_ref, index, tile)
                    put_tile(first, index, tile, jnp.where(is_halo, lane_roll(halos[c], 8 - 8 * t), value))
    for tile in range(5):
        halos = columns(2, tile)
        for half in range(2):
            rolled = [lane_roll(halos[half], 8 * k) for k in range(16)]
            for k in range(16 if half == 0 else COEFS - 16):
                index = half * 16 + k
                spread = rolled[(1 - k) % 16]
                for q in range(1, 4):
                    spread = jnp.where(group == q, rolled[(4 * q + 1 - k) % 16], spread)
                value = own(cstrip_ref, index, tile)
                put_tile(coef, index, tile, jnp.where(is_halo, spread, value))
    step(first, second, coef, 4, STRIP_STARTS[0], False)
    step(second, first, coef, 4, STRIP_STARTS[1], False)
    step(first, second, coef, 4, STRIP_STARTS[2], True)
    step(second, result, coef, 4, STRIP_STARTS[3], True, -8)

    blocks = []
    for part in range(4):
        for row in range(0, ROWS, 8):
            packed = None
            for t in range(4):
                value = result[t * 4 + part, row : row + 8, :]
                value = jnp.where(lane % 8 < 4, lane_roll(value, 8 * t - 4), lane_roll(value, 8 * t - 12))
                packed = value if packed is None else jnp.where(offset // 8 == t, value, packed)
            blocks.append(packed)
    is_edge = (lane < 4) | (lane >= 124)
    for i, packed in enumerate(blocks):
        part, row = i // 4, i % 4 * 8
        for p in range(16):
            plane = p * 4 + part
            value = main_ref[plane, row : row + 8, :]
            out_ref[plane, row : row + 8, :] = jnp.where(is_edge, lane_roll(packed, 124 - 8 * p), value)

    gram = partial_ref[...] + gram_of([jnp.concatenate(blocks, axis=0)], 0, 0)
    same = iota((128, 128), 0) % 8 == iota((128, 128), 1) % 8
    folded = jnp.where(same, gram, 0.0).reshape(16, 8, 128).sum(axis=1)
    select = (iota((128, 128), 0) // 8 == iota((128, 128), 1) % 16).astype(jnp.bfloat16)
    spread, rest = None, folded
    for _ in range(3):
        part = rest.astype(jnp.bfloat16)
        rest = rest - part.astype(F32)
        moved = jnp.dot(part, select, preferred_element_type=F32)
        spread = moved if spread is None else spread + moved
    mine = iota((16, 128), 1) // 16 == iota((16, 128), 0) % 8
    tile = jnp.where(mine, spread, 0.0).reshape(2, 8, 128).sum(axis=1)
    gram_ref[...] = jnp.broadcast_to(tile[None], gram_ref.shape)


def finish_kernel(scale, in_ref, sketch_ref, factor_hbm, sketch_hbm, out_ref, sems):
    copy = pltpu.make_async_copy(sketch_ref, sketch_hbm, sems.at[0])
    copy.start()
    tile = jnp.sum(in_ref[...], axis=0) * scale
    row, col = iota((16, 128), 0), iota((16, 128), 1)
    work = jnp.concatenate([jnp.broadcast_to(tile[i : i + 1], (8, 128)) for i in range(2)], axis=0)
    work = jnp.where(col // 16 == row % 8, work, 0.0)
    for shift in (64, 32, 16):
        work = work + lane_roll(work, shift)
    work = jnp.where(col < 16, work, 0.0)
    columns = [jnp.broadcast_to(work[:, j : j + 1], (16, 128)) for j in range(16)]
    for k in range(16):
        pivot = columns[k][k : k + 1, :]
        if k < 15:
            scaled = jnp.where(row > k, columns[k] / pivot, 0.0)
            for j in range(k + 1, 16):
                columns[j] = columns[j] - scaled * columns[j][k : k + 1, :]
    factor = jnp.zeros((16, 128), F32)
    for k in range(16):
        factor = jnp.where(col == k, columns[k], factor)
    diagonal = jnp.sum(jnp.where(row == col, factor, 0.0), axis=1, keepdims=True)
    factor = jnp.where(col >= row, factor / jnp.sqrt(diagonal), 0.0)
    out_ref[...] = factor[:, :16]
    last = pltpu.make_async_copy(out_ref, factor_hbm, sems.at[1])
    last.start()
    copy.wait()
    last.wait()


def shape(*dims):
    return jax.ShapeDtypeStruct(dims, F32)


VMEM = pl.BlockSpec(memory_space=pltpu.VMEM)
ANY = pl.BlockSpec(memory_space=pl.ANY)


def call(kernel, name, inputs, outputs, scratch=(), in_specs=None, out_specs=None, flops=1_000_000, vmem=32):
    moved = 4 * sum(math.prod(a.shape) for a in (*inputs, *outputs))
    return pl.pallas_call(
        kernel,
        in_specs=in_specs or [VMEM] * len(inputs),
        out_specs=out_specs or [VMEM] * len(outputs),
        out_shape=list(outputs),
        scratch_shapes=list(scratch),
        compiler_params=pltpu.CompilerParams(vmem_limit_bytes=vmem << 20),
        cost_estimate=pl.CostEstimate(flops=flops, bytes_accessed=moved, transcendentals=0),
        name=name,
    )(*inputs)


def exchange(first, second, axes):
    count = lax.axis_size(axes)
    inner = [(i, i ^ 1) for i in range(count)]
    outer = [(i, (((i + 1) ^ 1) - 1) % count) for i in range(count)]
    return lax.ppermute(first, axes, inner), lax.ppermute(second, axes, outer)


def local(probes, coefficients):
    planes = probes.reshape(PLANES, ROWS, 128)
    weights = coefficients.reshape(COEFS, ROWS, 128)
    scratch = lambda *dims: pltpu.VMEM(dims, F32)
    x_first, x_second = call(
        pack_rows_kernel,
        "pack_rows",
        [pltpu.with_memory_space_constraint(array, pltpu.HBM) for array in (planes, weights)],
        [pltpu.VMEM((PAIRS, 8, 128), F32)] * 2,
        [scratch(PLANES, 8, 128)] * 2 + [scratch(COEFS, 8, 128)] * 2 + [pltpu.SemaphoreType.DMA((4,))],
        in_specs=[pl.BlockSpec(memory_space=pltpu.HBM)] * 2,
    )
    x_first, x_second = exchange(x_first, x_second, ACROSS)

    inner, own_left, own_right = call(
        inner_kernel,
        "inner",
        (planes, weights),
        [
            shape(PLANES, ROWS, 128),
            shape(15, 8, 128),
            shape(15, 8, 128),
        ],
        [scratch(PLANES, ROWS, 128)] * 2,
        flops=15_000_000,
    )
    y_first, y_second = call(
        halo_kernel, "halo", (x_first, x_second, own_left, own_right), [shape(15, 8, 128)] * 2
    )
    y_first, y_second = exchange(y_first, y_second, "z")

    main, partial, strip, cstrip = call(
        outer_kernel,
        "outer",
        (planes, weights, x_first, x_second, inner),
        [shape(PLANES, ROWS, 128), shape(128, 128), shape(16, 40, 128), shape(COEFS, 40, 128)],
        [scratch(PLANES, 32, 128)] * 2 + [scratch(COEFS, 32, 128), scratch(PLANES, 16, 128)],
        flops=10_000_000,
    )
    sketch, gram = call(
        edge_kernel,
        "edge",
        (main, partial, strip, cstrip, y_first, y_second),
        [pltpu.VMEM((PLANES, ROWS, 128), F32), shape(16, 2, 128)],
        [
            scratch(16, EXT, 128),
            scratch(16, EXT, 128),
            scratch(COEFS, EXT, 128),
            scratch(16, ROWS, 128),
        ],
    )

    gathered = lax.all_to_all(gram, ("core", "z"), 0, 0, tiled=True)
    gram = jnp.broadcast_to(gathered.sum(axis=0)[None], (16, 2, 128))
    gathered = lax.all_to_all(gram, ("x", "y"), 0, 0, tiled=True)
    total_rows = PLANES // 16 * ROWS * 128 * lax.axis_size(ACROSS + ("z",))
    factor, sketch = call(
        lambda *refs: finish_kernel(1.0 / total_rows, *refs),
        "finish",
        (gathered, sketch),
        [shape(16, 16), shape(PLANES, ROWS, 128)],
        [scratch(16, 16), pltpu.SemaphoreType.DMA((2,))],
        out_specs=[ANY, ANY],
    )
    return sketch.reshape(probes.shape), factor


def solution(mesh):
    fine = Mesh(mesh.devices.reshape(4, 4, 2, 8), ("x", "y", "core", "z"))
    placed = (P(None, None, None, ACROSS, "z"), P(None, None, ACROSS, "z"))
    return jax.shard_map(
        local,
        mesh=fine,
        in_specs=placed,
        out_specs=(P(None, None, None, ACROSS, "z"), P()),
        check_vma=False,
    )
```
